32 devices in a mesh: dp: 8 (over z, x), lat: 4 (over y, core).
Axes of the slice: x: 2, y: 2, z: 4, core: 2. Of those that a mesh axis runs over, the one named last changes fastest.
Arguments:
- tokens: bfloat16 [24576, 512], P(('dp', 'lat')), may hold values from -6 to 6
- latents: bfloat16 [1536, 1024], P(('dp', 'lat')), may hold values from -6 to 6
- gain_self: float32 [512], replicated, may hold values from 0.1 to 1.9
- w_qkv_tok: bfloat16 [512, 1536], replicated, may hold values from -1 to 1
- w_o_tok: bfloat16 [512, 512], replicated, may hold values from -0.25 to 0.25
- gain_read: float32 [512], replicated, may hold values from 0.1 to 1.9
- w_kv_read: bfloat16 [512, 2048], replicated, may hold values from -1 to 1
- gain_lat: float32 [1024], replicated, may hold values from 0.1 to 1.9
- w_q_read: bfloat16 [1024, 1024], replicated, may hold values from -1 to 1
- gain_glob: float32 [1024], replicated, may hold values from 0.1 to 1.9
- w_qkv_glob: bfloat16 [3, 1024, 1024], P(None, None, 'lat'), may hold values from -1 to 1
- w_o_glob: bfloat16 [1024, 1024], P('lat'), may hold values from -0.375 to 0.375
- gain_write: float32 [512], replicated, may hold values from 0.1 to 1.9
- w_q_write: bfloat16 [512, 512], replicated, may hold values from -1 to 1
- gain_wlat: float32 [1024], replicated, may hold values from 0.1 to 1.9
- w_kv_write: bfloat16 [1024, 1024], replicated, may hold values from -1 to 1
Outputs:
- tokens_out: bfloat16 [24576, 512], P(('dp', 'lat'))
- latents_out: bfloat16 [1536, 1024], P(('dp', 'lat'))
The draws below stay inside these ranges and needn't reach their ends.
All inputs are finite; a program needn't handle non-finite values.
Results may differ from the reference program's by a relative error of at most 0.015.
Values may be sent and summed in bfloat16 or wider, within the bound.
A program may use at most 128 MiB of HBM per device.

```python
import jax
import jax.numpy as jnp
from jax import lax

D = 512
DL = 1024
HEAD = 64
G = 256
NLAT = 16
TOKENS = 24576
LATENTS = 1536


image_count = 64


def spread_weight(key, salt, shape, fan_in):
    return jax.random.truncated_normal(jax.random.fold_in(key, salt), -6.0, 6.0, shape, jnp.float32) * fan_in ** (-0.5)


def activations(key, salt, rows, width):
    noise = jax.random.truncated_normal(jax.random.fold_in(key, salt), -6.0, 6.0, (rows, width), jnp.float32)
    return noise


def image_part(key, salt, rows, width):
    index = jnp.arange(rows, dtype=jnp.int32) * image_count // rows
    directions = jax.random.truncated_normal(jax.random.fold_in(key, salt), -4.0, 4.0, (image_count, width), jnp.float32)
    amplitude = jax.random.uniform(jax.random.fold_in(key, salt + 1), (image_count,), jnp.float32, 0.5, 1.0)
    return directions[index] * amplitude[index][:, None]


def draw_tokens(key, part):
    values = activations(key, 21, TOKENS, D)
    return values.astype(jnp.bfloat16)


def draw_latents(key, part):
    values = activations(key, 22, LATENTS, DL)
    values = values + image_part(key, 23, LATENTS, DL)
    values = jnp.clip(values, -6.0, 6.0)
    return values.astype(jnp.bfloat16)


def draw_w_qkv_tok(key, part):
    full = spread_weight(key, 31, (D, 3 * D), D)
    return full.astype(jnp.bfloat16)


def draw_w_q_read(key, part):
    full = spread_weight(key, 32, (DL, DL), DL)
    return full.astype(jnp.bfloat16)


def draw_w_kv_read(key, part):
    full = spread_weight(key, 33, (D, 2 * DL), D)
    return full.astype(jnp.bfloat16)


def draw_w_qkv_glob(key, part):
    factors = jnp.array([1.5, 1.5, 1.0], jnp.float32)
    full = spread_weight(key, 35, (3, DL, DL), DL) * factors[:, None, None]
    return full.astype(jnp.bfloat16)


def draw_w_q_write(key, part):
    full = spread_weight(key, 36, (D, D), D)
    return full.astype(jnp.bfloat16)


def draw_w_kv_write(key, part):
    full = spread_weight(key, 37, (DL, 2 * D), DL)
    return full.astype(jnp.bfloat16)


def steps_of(stream_key, shape, cuts, least, largest):
    factor_of = 1.0
    for position, parts in cuts:
        steps = jax.random.uniform(jax.random.fold_in(jax.random.fold_in(stream_key, 6), position), (parts,), jnp.float32, least / len(cuts), largest / len(cuts))
        factor_of = factor_of * jnp.repeat(jnp.exp(steps), shape[position] // parts).reshape((-1,) + (1,) * (len(shape) - 1 - position))
    return factor_of


def centred(key, extent, spread, reach, pieces=(), kind=jnp.bfloat16):
    entries = spread * jax.random.normal(key, extent, jnp.float32)
    if pieces:
        entries = entries * steps_of(key, extent, pieces, -0.22, 0.18)
    return jnp.clip(entries, -reach, reach).astype(kind)


def setup_inputs(seed: int = 0) -> dict:
    seeds = jax.random.split(jax.random.key(seed), 17)
    tokens = draw_tokens(jax.random.fold_in(seeds[16], 71), 0)
    latents = draw_latents(jax.random.fold_in(seeds[16], 71), 0)
    gain_self = jnp.clip(1.0 + 0.18 * jax.random.normal(seeds[2], (D,), jnp.float32), 0.1, 1.9)
    w_qkv_tok = draw_w_qkv_tok(jax.random.fold_in(seeds[16], 71), 0)
    w_o_tok = centred(seeds[4], (D, D), D ** -0.5, 0.25)
    gain_read = jnp.clip(1.0 + 0.18 * jax.random.normal(seeds[5], (D,), jnp.float32), 0.1, 1.9)
    w_kv_read = draw_w_kv_read(jax.random.fold_in(seeds[16], 71), 0)
    gain_lat = jnp.clip(1.0 + 0.18 * jax.random.normal(seeds[7], (DL,), jnp.float32), 0.1, 1.9)
    w_q_read = draw_w_q_read(jax.random.fold_in(seeds[16], 71), 0)
    gain_glob = jnp.clip(1.0 + 0.18 * jax.random.normal(seeds[9], (DL,), jnp.float32), 0.1, 1.9)
    w_qkv_glob = draw_w_qkv_glob(jax.random.fold_in(seeds[16], 71), 0)
    w_o_glob = centred(seeds[11], (DL, DL), (DL // 4) ** -0.5, 0.375, ((0, 4),))
    gain_write = jnp.clip(1.0 + 0.18 * jax.random.normal(seeds[12], (D,), jnp.float32), 0.1, 1.9)
    w_q_write = draw_w_q_write(jax.random.fold_in(seeds[16], 71), 0)
    gain_wlat = jnp.clip(1.0 + 0.18 * jax.random.normal(seeds[14], (DL,), jnp.float32), 0.1, 1.9)
    w_kv_write = draw_w_kv_write(jax.random.fold_in(seeds[16], 71), 0)
    return dict(tokens=tokens, latents=latents, gain_self=gain_self, w_qkv_tok=w_qkv_tok, w_o_tok=w_o_tok, gain_read=gain_read, w_kv_read=w_kv_read, gain_lat=gain_lat, w_q_read=w_q_read, gain_glob=gain_glob, w_qkv_glob=w_qkv_glob, w_o_glob=w_o_glob, gain_write=gain_write, w_q_write=w_q_write, gain_wlat=gain_wlat, w_kv_write=w_kv_write)


def rms_norm(values, gain):
    floats = values.astype(jnp.float32)
    factor = lax.rsqrt(lax.optimization_barrier(jnp.mean(floats * floats, axis=-1, keepdims=True)) + 1e-06)
    return (floats * factor * gain).astype(jnp.bfloat16)

def attend(query, keys, values):
    scores = jnp.einsum('qhe,khe->hqk', query.astype(jnp.float32), keys.astype(jnp.float32)) * HEAD ** (-0.5)
    peak = lax.optimization_barrier(jnp.max(scores, axis=-1, keepdims=True))
    weights = jnp.exp(scores - peak)
    total = lax.optimization_barrier(jnp.sum(weights, axis=-1))
    rounded = lax.optimization_barrier(weights.astype(jnp.bfloat16)).astype(jnp.float32)
    mixed = jnp.einsum('hqk,khe->hqe', rounded, values.astype(jnp.float32))
    return jnp.transpose(mixed / total[:, :, None], (1, 0, 2))

def front(inputs, gain_self, w_qkv_tok, w_o_tok, gain_read, w_kv_read, gain_lat, w_q_read):
    group, lat_rows = inputs
    rows = group.shape[0]
    packed = jnp.dot(rms_norm(group, gain_self), w_qkv_tok, preferred_element_type=jnp.float32)
    packed = packed.astype(jnp.bfloat16).reshape(rows, 3, -1, HEAD)
    mixed = attend(packed[:, 0], packed[:, 1], packed[:, 2]).reshape(rows, -1).astype(jnp.bfloat16)
    tokens_mid = (group.astype(jnp.float32) + jnp.dot(mixed, w_o_tok, preferred_element_type=jnp.float32)).astype(jnp.bfloat16)
    key_vals = jnp.dot(rms_norm(tokens_mid, gain_read), w_kv_read, preferred_element_type=jnp.float32)
    key_vals = key_vals.astype(jnp.bfloat16).reshape(rows, 2, -1, HEAD)
    query = jnp.dot(rms_norm(lat_rows, gain_lat), w_q_read, preferred_element_type=jnp.float32)
    query = query.astype(jnp.bfloat16).reshape(lat_rows.shape[0], -1, HEAD)
    read = attend(query, key_vals[:, 0], key_vals[:, 1]).reshape(lat_rows.shape[0], -1)
    return (tokens_mid, (lat_rows.astype(jnp.float32) + read).astype(jnp.bfloat16))

def back(inputs, gain_write, w_q_write, gain_wlat, w_kv_write):
    tokens_mid, lat_rows = inputs
    rows = tokens_mid.shape[0]
    query = jnp.dot(rms_norm(tokens_mid, gain_write), w_q_write, preferred_element_type=jnp.float32)
    query = query.astype(jnp.bfloat16).reshape(rows, -1, HEAD)
    key_vals = jnp.dot(rms_norm(lat_rows, gain_wlat), w_kv_write, preferred_element_type=jnp.float32)
    key_vals = key_vals.astype(jnp.bfloat16).reshape(lat_rows.shape[0], 2, -1, HEAD)
    written = attend(query, key_vals[:, 0], key_vals[:, 1]).reshape(rows, -1)
    return (tokens_mid.astype(jnp.float32) + written).astype(jnp.bfloat16)

def one_head(inputs):
    query, keys, values = inputs
    scores = jnp.dot(query, keys.T, preferred_element_type=jnp.float32) * HEAD ** (-0.5)
    peak = lax.optimization_barrier(jnp.max(scores, axis=-1, keepdims=True))
    weights = jnp.exp(scores - peak)
    total = lax.optimization_barrier(jnp.sum(weights, axis=-1, keepdims=True))
    mixed = jnp.dot(weights.astype(jnp.bfloat16), values, preferred_element_type=jnp.float32)
    return (mixed / total).astype(jnp.bfloat16)

def reference(tokens, latents, gain_self, w_qkv_tok, w_o_tok, gain_read, w_kv_read, gain_lat, w_q_read, gain_glob, w_qkv_glob, w_o_glob, gain_write, w_q_write, gain_wlat, w_kv_write):
    groups = tokens.reshape(-1, G, D)
    lat_groups = latents.reshape(-1, NLAT, DL)
    tokens_mid, latents_mid = lax.map(lambda pair: front(pair, gain_self, w_qkv_tok, w_o_tok, gain_read, w_kv_read, gain_lat, w_q_read), (groups, lat_groups))
    latents_mid = latents_mid.reshape(-1, DL)
    count = latents_mid.shape[0]
    normed = rms_norm(latents_mid, gain_glob)
    heads = []
    for which in range(3):
        projected = jnp.dot(normed, w_qkv_glob[which], preferred_element_type=jnp.float32).astype(jnp.bfloat16)
        heads.append(jnp.transpose(projected.reshape(count, -1, HEAD), (1, 0, 2)))
    mixed = lax.map(one_head, (heads[0], heads[1], heads[2]))
    mixed = jnp.transpose(mixed, (1, 0, 2)).reshape(count, -1)
    latents_out = (latents_mid.astype(jnp.float32) + jnp.dot(mixed, w_o_glob, preferred_element_type=jnp.float32)).astype(jnp.bfloat16)
    tokens_out = lax.map(lambda pair: back(pair, gain_write, w_q_write, gain_wlat, w_kv_write), (tokens_mid, latents_out.reshape(-1, NLAT, DL)))
    return (tokens_out.reshape(-1, D), latents_out)
```

```python
import functools

import jax
import jax.numpy as jnp
from jax import lax
from jax.experimental import pallas as pl
from jax.experimental.pallas import tpu as pltpu
from jax.sharding import PartitionSpec as P

HEAD = 64
G = 256
NLAT = 16
SCALE = HEAD ** (-0.5)
MESH = pl.DeviceIdType.MESH
PARTS = 4
F32 = jnp.float32
BF16 = jnp.bfloat16


def rms_norm(values, gain):
    floats = values.astype(F32)
    factor = lax.rsqrt(jnp.mean(floats * floats, axis=-1, keepdims=True) + 1e-06)
    return (floats * factor * gain).astype(BF16)


def dot(a, b):
    return jnp.dot(a, b, preferred_element_type=F32)


def dot_nt(a, b):
    return lax.dot_general(a, b, (((1,), (1,)), ((), ())), preferred_element_type=F32)


def dot_tn(a, b):
    return lax.dot_general(a, b, (((0,), (0,)), ((), ())), preferred_element_type=F32)


def spread_heads(query, count):
    lane_head = lax.broadcasted_iota(jnp.int32, query.shape, 1) // HEAD
    zero = jnp.zeros_like(query)
    return jnp.concatenate([jnp.where(lane_head == h, query, zero) for h in range(count)], axis=0)


def fold_heads(stacked, count):
    rows = stacked.shape[0] // count
    lane_head = lax.broadcasted_iota(jnp.int32, (rows, stacked.shape[1]), 1) // HEAD
    out = stacked[:rows]
    for h in range(1, count):
        out = jnp.where(lane_head == h, stacked[h * rows : (h + 1) * rows], out)
    return out


def softmax_mix(stacked, keys, values):
    scores = dot_nt(stacked, keys)
    peak = jnp.max(scores, axis=-1, keepdims=True)
    weights = jnp.exp(scores - peak)
    total = jnp.sum(weights, axis=-1, keepdims=True)
    return dot(weights.astype(BF16), values) * (1.0 / total)


def kernel(
    dp_count,
    lat_count,
    tok,
    lat_in,
    g_self,
    w_qkv_h,
    w_o_h,
    g_read,
    w_kvr_h,
    g_lat,
    w_qr_h,
    g_glob,
    w_glob_h,
    w_og_h,
    g_write,
    w_qw_h,
    g_wlat,
    w_kvw_h,
    tok_out,
    lat_out,
    mid,
    lfin,
    w_qkv,
    w_o,
    w_kvr,
    w_qr,
    w_glob,
    w_og,
    w_qw,
    w_kvw,
    lmid,
    rq,
    packed,
    mixed,
    kvr,
    gath,
    kv,
    qq,
    msend,
    mrecv,
    top,
    norm,
    acc,
    load_sem,
    z_send,
    z_recv,
    f_send,
    f_recv,
    s_send,
    s_recv,
    c_send,
    c_recv,
    wo_send,
    wo_recv,
    m_send,
    m_recv,
):
    width = tok.shape[1]
    lat_width = lat_in.shape[1]
    groups = tok.shape[0] // G
    lat_rows = lat_in.shape[0]
    nz = dp_count // 2
    dp = lax.axis_index("dp")
    lat = lax.axis_index("lat")
    z, x = dp // 2, dp % 2
    y, core = lat // 2, lat % 2
    dp_x = dp + 1 - 2 * x
    lat_y = (lat + 2) % 4
    partner = lat + 1 - 2 * core
    diag = (partner + 2) % 4
    a = (1 - core) * y + core * x
    b = (1 - core) * x + core * y
    first = ((1 - core) * dp + core * dp_x, (1 - core) * lat_y + core * lat)
    second = ((1 - core) * dp_x + core * dp, (1 - core) * lat + core * lat_y)
    base = (b * 2 + a) * nz
    other = (b * 2 + 1 - a) * nz
    me = base + z
    far = (1 - 2 * b) * 2 * nz
    run = nz // PARTS

    loads = []
    for i, (src, dst) in enumerate(
        ((w_qkv_h, w_qkv), (w_o_h, w_o), (w_qr_h, w_qr), (w_kvr_h, w_kvr), (w_glob_h, w_glob),
         (w_qw_h, w_qw), (w_kvw_h, w_kvw), (w_og_h, w_og.at[lat]))
    ):
        loads.append(pltpu.make_async_copy(src, dst, load_sem.at[i]))
        loads[-1].start()

    barrier = pltpu.get_barrier_semaphore()

    def greet(offset, carry):
        pl.semaphore_signal(
            barrier, inc=1, device_id=((z + offset) % nz * 2 + x, lat), device_id_type=MESH
        )
        return carry

    lax.fori_loop(1, nz, greet, 0)
    for peer in ((dp_x, lat), (dp, lat_y), (dp, partner), (dp, diag)):
        pl.semaphore_signal(barrier, inc=1, device_id=peer, device_id_type=MESH)

    def remote(src, dst, send_sem, recv_sem, peer):
        return pltpu.make_async_remote_copy(
            src_ref=src, dst_ref=dst, send_sem=send_sem, recv_sem=recv_sem, device_id=peer,
            device_id_type=MESH,
        )

    wo_share = remote(w_og_h, w_og.at[lat], wo_send.at[0], wo_recv.at[0], (dp, partner))
    wo_cross, wo_relay = [], []
    wo_rows = w_og_h.shape[0] // 2
    for i in range(2):
        part_rows = pl.ds(i * wo_rows, wo_rows)
        there = w_og.at[lat_y, part_rows]
        wo_cross.append(
            remote(w_og_h.at[part_rows], w_og.at[lat, part_rows], wo_send.at[1 + i], wo_recv.at[1 + i], (dp, lat_y))
        )
        wo_relay.append(remote(there, there, wo_send.at[3 + i], wo_recv.at[3 + i], (dp, partner)))

    def piece(g, start, count):
        return gath.at[g, core, pl.ds(start, count)]

    def along(ref, send_sem, recv_sem, peer):
        return remote(ref, ref, send_sem, recv_sem, peer)

    def on_first(g, p):
        return along(
            piece(g, base + p * run, run), f_send.at[g, p], f_recv.at[g, p], first
        )

    def on_second(g, half, p):
        start = base + (other - base) * half + p * run
        k = half * PARTS + p
        return along(piece(g, start, run), s_send.at[g, k], s_recv.at[g, k], second)

    def share(g, line, p):
        start = (base, other, base + far, other + far)[line] + p * run
        k = line * PARTS + p
        return along(
            piece(g, start, run), c_send.at[g, k], c_recv.at[g, k], (dp, partner)
        )

    late_half = z * 2 // nz

    def near(o):
        q = z // run
        return q + o - 2 * ((q % 2) * (o % 2) + 2 * (q // 2) * (o // 2))

    def z_copy(g, step):
        offset = late_half * step + (1 - late_half) * (nz - step)
        return remote(
            gath.at[g, core, me], gath.at[g, core, me], z_send.at[g, (z + offset) % nz],
            z_recv.at[g, z], ((z + offset) % nz * 2 + x, lat),
        )

    def each(low, high, body):
        def one(i, carry):
            body(i)
            return carry

        lax.fori_loop(low, high, one, 0)

    def z_start(g):
        each(1, nz, lambda offset: z_copy(g, offset).start())

    def z_arrived(g, block):
        ref = piece(g, base + block, 1)

        @pl.when(block != z)
        def _():
            pltpu.make_async_copy(ref, ref, z_recv.at[g, block]).wait()

    def stage_one(g, low, high):
        def body(o):
            p = near(o)
            each(0, run, lambda i: z_arrived(g, p * run + i))
            on_first(g, p).start()
            on_second(g, 0, p).start()
            share(g, 0, p).start()

        each(low, high, body)

    def stage_two(g, low=0, high=PARTS):
        def body(o):
            p = near(o)
            on_first(g, p).wait_recv()
            on_second(g, 1, p).start()
            share(g, 1, p).start()

        each(low, high, body)

    def second_arrived(g, half, o):
        p = near(o)
        on_second(g, half, p).wait_recv()
        share(g, 2 + half, p).start()

    def stage_three(g):
        for half in range(2):
            each(0, PARTS, lambda o: second_arrived(g, half, o))

    def gathered(g):
        for line in range(4):
            each(0, PARTS, lambda p: share(g, line, p).wait_recv())

    def self_part(g):
        rows = pl.ds(g * G, G)
        group = tok[rows, :]
        normed = rms_norm(group, g_self[...])
        if g == 0:
            loads[0].wait()
        packed[...] = dot(normed, w_qkv[...]).astype(BF16)
        for pair in range(width // (2 * HEAD)):
            at = pair * 2 * HEAD
            query = packed[:, at : at + 2 * HEAD] * jnp.asarray(SCALE, BF16)
            keys = packed[:, width + at : width + at + 2 * HEAD]
            values = packed[:, 2 * width + at : 2 * width + at + 2 * HEAD]
            out = softmax_mix(spread_heads(query, 2), keys, values)
            mixed[:, at : at + 2 * HEAD] = fold_heads(out, 2).astype(BF16)
        if g == 0:
            loads[1].wait()
        mid[rows, :] = (group.astype(F32) + dot(mixed[...], w_o[...])).astype(BF16)

    def read_part(g):
        if g == 0:
            loads[2].wait()
            query = dot(rms_norm(lat_in[...], g_lat[...]), w_qr[...]).astype(BF16)
            rq[...] = query * jnp.asarray(SCALE, BF16)
            loads[3].wait()
        rows = pl.ds(g * G, G)
        lrows = pl.ds(g * NLAT, NLAT)
        kvr[...] = dot(rms_norm(mid[rows, :], g_read[...]), w_kvr[...]).astype(BF16)
        quad = 4 * HEAD
        for at in range(0, lat_width, quad):
            out = softmax_mix(
                spread_heads(rq[lrows, at : at + quad], 4),
                kvr[:, at : at + quad],
                kvr[:, lat_width + at : lat_width + at + quad],
            )
            lmid[lrows, at : at + quad] = (
                lat_in[lrows, at : at + quad].astype(F32) + fold_heads(out, 4)
            ).astype(BF16)
        gath[g, core, me] = rms_norm(lmid[lrows, :], g_glob[...])
        z_start(g)
        stage_one(g, 0, 1)

    def scope(name):
        return jax.named_scope(name)

    last = groups - 1
    for g in range(groups):
        with scope(f"self{g}"):
            self_part(g)
        if g == 0:
            with scope("bar"):
                pl.semaphore_wait(barrier, nz + 3)
            wo_share.start()
            wo_cross[0].start()
        if g >= 2:
            with scope("fwdA"):
                stage_one(g - 2, 2, PARTS)
                if g == 2:
                    wo_cross[0].wait_recv()
                    wo_relay[0].start()
        with scope(f"read{g}"):
            read_part(g)
        if g >= 1 and g < last:
            with scope("fwdB"):
                stage_one(g - 1, 1, 2)

    block_rows = 4 * nz * NLAT
    tile = min(block_rows, G)
    blocks = tile // NLAT

    def project(g, c):
        def one(i, carry):
            rows = gath[g, c, pl.ds(i * blocks, blocks)].reshape(tile, lat_width)
            at = pl.multiple_of((g * 2 + c) * block_rows + i * tile, tile)
            kv[0, pl.ds(at, tile), :] = dot(rows, w_glob[1]).astype(BF16)
            kv[1, pl.ds(at, tile), :] = dot(rows, w_glob[2]).astype(BF16)
            return carry

        lax.fori_loop(0, block_rows // tile, one, 0)

    with scope("fwdC"):
        for g in range(last - 1):
            stage_two(g)
        stage_one(last - 1, 1, PARTS)
    loads[5].wait()
    with scope("wq"):
        for g in range(groups):
            rows = pl.ds(g * G, G)
            query = dot(rms_norm(mid[rows, :], g_write[...]), w_qw[...]).astype(BF16)
            tok_out[rows, :] = query * jnp.asarray(SCALE, BF16)
    loads[4].wait()
    with scope("fwdD"):
        for g in range(last - 1):
            stage_three(g)
        stage_two(last - 1)
    for g in range(last - 1):
        with scope("gath0"):
            gathered(g)
        with scope("proj0"):
            project(g, 0)
            project(g, 1)
    with scope("fwdE"):
        stage_one(last, 1, PARTS)
        stage_three(last - 1)
    with scope("fwdF"):
        stage_two(last)
        wo_cross[1].start()
    with scope("gath1"):
        gathered(last - 1)
    with scope("proj1"):
        project(last - 1, 0)
        project(last - 1, 1)
    own_p = z // run

    with scope('ownw'):
        @pl.when(core == 1)
        def _():
            on_second(last, 0, own_p).wait_recv()
            share(last, 2, own_p).start()
            for line in range(2):
                share(last, line, own_p).wait_recv()

        @pl.when(core == 0)
        def _():
            for line in (0, 2):
                share(last, line, own_p).wait_recv()

    own = []
    for l in range(lat_count):
        ly, lc = l // 2, l % 2
        index = ((x * 2 + ly) if lc == 0 else (ly * 2 + x)) * nz + z
        for g in range(groups):
            own.append(gath[g, lc, index])
    query = dot(jnp.concatenate(own, axis=0), w_glob[0]).astype(BF16) * jnp.asarray(SCALE, BF16)
    heads = query.shape[1] // HEAD
    qq[...] = spread_heads(query, heads)
    early = last * 2 * block_rows
    full = lat_rows * lat_count
    part = full if early * full <= 2**20 else lat_rows

    def attend_early(i, carry):
        rows = pl.ds(pl.multiple_of(i * part, part), part)
        scores = dot_nt(qq[rows, :], kv[0, :early, :])
        peak = jnp.max(scores, axis=-1, keepdims=True)
        weights = jnp.exp(scores - peak)
        top[rows, :] = peak
        norm[rows, :] = jnp.sum(weights, axis=-1, keepdims=True)
        acc[rows, :] = dot(weights.astype(BF16), kv[1, :early, :])
        return carry

    def attend_late(i, carry):
        rows = pl.ds(pl.multiple_of(i * part, part), part)
        scores = dot_nt(qq[rows, :], kv[0, early:, :])
        peak = jnp.maximum(top[rows, :], jnp.max(scores, axis=-1, keepdims=True))
        weights = jnp.exp(scores - peak)
        keep = jnp.exp(top[rows, :] - peak)
        total = norm[rows, :] * keep + jnp.sum(weights, axis=-1, keepdims=True)
        both = acc[rows, :] * keep + dot(weights.astype(BF16), kv[1, early:, :])
        qq[rows, :] = (both * (1.0 / total)).astype(BF16)
        return carry

    with scope("attE"):
        lax.fori_loop(0, qq.shape[0] // part, attend_early, 0)

    with scope('lastw'):
        @pl.when(core == 1)
        def _():
            each(1, PARTS, lambda o: second_arrived(last, 0, o))
            each(0, PARTS, lambda o: second_arrived(last, 1, o))
            for line in range(2):
                each(1, PARTS, lambda o: share(last, line, near(o)).wait_recv())
            for line in range(2, 4):
                each(0, PARTS, lambda p: share(last, line, p).wait_recv())

        @pl.when(core == 0)
        def _():
            stage_three(last)
            for line in (0, 2):
                each(1, PARTS, lambda o: share(last, line, near(o)).wait_recv())
            for line in (1, 3):
                each(0, PARTS, lambda p: share(last, line, p).wait_recv())

    with scope("proj2"):
        project(last, 0)
        project(last, 1)
    with scope("woB"):
        wo_cross[1].wait_recv()
        wo_relay[1].start()
    with scope("attL"):
        lax.fori_loop(0, qq.shape[0] // part, attend_late, 0)
    result = fold_heads(qq[...], heads)
    for l in range(lat_count):
        msend[l] = result[l * lat_rows : (l + 1) * lat_rows]
    mix_copies = []
    for i, peer in enumerate((partner, lat_y, diag)):
        mix_copies.append(remote(msend.at[peer], mrecv.at[lat], m_send.at[i], m_recv.at[i], (dp, peer)))
        mix_copies[-1].start()
    mrecv[lat] = msend[lat]
    loads[7].wait()
    loads[6].wait()
    with scope("mixw"):
        wo_share.wait_recv()
        for copy in wo_relay:
            copy.wait_recv()
        for copy in mix_copies:
            copy.wait_recv()
    total = dot(mrecv[0], w_og[0])
    for l in range(1, lat_count):
        total = total + dot(mrecv[l], w_og[l])
    final = (lmid[...].astype(F32) + total).astype(BF16)
    lat_out[...] = final
    lfin[...] = dot(rms_norm(final, g_wlat[...]), w_kvw[...]).astype(BF16)

    for copy in [wo_share] + wo_cross + wo_relay + mix_copies:
        copy.wait_send()
    for g in range(groups):
        each(1, nz, lambda offset: z_copy(g, offset).wait_send())

        def sent(p):
            on_first(g, p).wait_send()
            for half in range(2):
                on_second(g, half, p).wait_send()
            for line in range(4):
                share(g, line, p).wait_send()

        each(0, PARTS, sent)


def back(query, final, mid, key_vals, tok_out, lat_out):
    width = query.shape[1]
    heads = width // HEAD
    keys = spread_heads(key_vals[:, :width], heads)
    values = spread_heads(key_vals[:, width:], heads)
    scores = dot_nt(keys, query[...]).reshape(heads, NLAT, G)
    peak = jnp.max(scores, axis=1, keepdims=True)
    weights = jnp.exp(scores - peak)
    weights = weights * (1.0 / jnp.sum(weights, axis=1, keepdims=True))
    written = dot_tn(weights.reshape(heads * NLAT, G).astype(BF16), values)
    tok_out[...] = (mid[...].astype(F32) + written).astype(BF16)
    lat_out[...] = final[...]


def local(
    tokens, latents, gain_self, w_qkv_tok, w_o_tok, gain_read, w_kv_read, gain_lat, w_q_read,
    gain_glob, w_qkv_glob, w_o_glob, gain_write, w_q_write, gain_wlat, w_kv_write,
):
    dp_count = lax.axis_size("dp")
    lat_count = lax.axis_size("lat")
    rows, width = tokens.shape
    lat_rows, lat_width = latents.shape
    groups = rows // G
    here = w_qkv_glob.shape[2]
    nz = dp_count // 2
    all_rows = lat_rows * dp_count * lat_count
    vmem = pl.BlockSpec(memory_space=pltpu.VMEM)
    hbm = pl.BlockSpec(memory_space=pl.ANY)
    dma = pltpu.SemaphoreType.DMA
    query, final, mid, key_vals = pl.pallas_call(
        functools.partial(kernel, dp_count, lat_count),
        out_shape=(
            jax.ShapeDtypeStruct(tokens.shape, BF16),
            jax.ShapeDtypeStruct(latents.shape, BF16),
            jax.ShapeDtypeStruct(tokens.shape, BF16),
            jax.ShapeDtypeStruct((lat_rows, w_kv_write.shape[1]), BF16),
        ),
        in_specs=[vmem, vmem, vmem, hbm, hbm, vmem, hbm, vmem, hbm, vmem, hbm, hbm, vmem, hbm, vmem, hbm],
        out_specs=(vmem,) * 4,
        scratch_shapes=[
            pltpu.VMEM(w_qkv_tok.shape, BF16),
            pltpu.VMEM(w_o_tok.shape, BF16),
            pltpu.VMEM(w_kv_read.shape, BF16),
            pltpu.VMEM(w_q_read.shape, BF16),
            pltpu.VMEM(w_qkv_glob.shape, BF16),
            pltpu.VMEM((lat_count,) + w_o_glob.shape, BF16),
            pltpu.VMEM(w_q_write.shape, BF16),
            pltpu.VMEM(w_kv_write.shape, BF16),
            pltpu.VMEM(latents.shape, BF16),
            pltpu.VMEM(latents.shape, BF16),
            pltpu.VMEM((G, w_qkv_tok.shape[1]), BF16),
            pltpu.VMEM((G, width), BF16),
            pltpu.VMEM((G, w_kv_read.shape[1]), BF16),
            pltpu.VMEM((groups, 2, 4 * nz, NLAT, lat_width), BF16),
            pltpu.VMEM((2, all_rows, here), BF16),
            pltpu.VMEM((lat_rows * lat_count * (here // HEAD), here), BF16),
            pltpu.VMEM((lat_count, lat_rows, here), BF16),
            pltpu.VMEM((lat_count, lat_rows, here), BF16),
            pltpu.VMEM((lat_rows * lat_count * (here // HEAD), 1), F32),
            pltpu.VMEM((lat_rows * lat_count * (here // HEAD), 1), F32),
            pltpu.VMEM((lat_rows * lat_count * (here // HEAD), here), F32),
            dma((8,)),
            dma((groups, nz)),
            dma((groups, nz)),
            dma((groups, PARTS)),
            dma((groups, PARTS)),
            dma((groups, 2 * PARTS)),
            dma((groups, 2 * PARTS)),
            dma((groups, 4 * PARTS)),
            dma((groups, 4 * PARTS)),
            dma((5,)),
            dma((5,)),
            dma((3,)),
            dma((3,)),
        ],
        compiler_params=pltpu.CompilerParams(
            collective_id=0, has_side_effects=True, vmem_limit_bytes=67043328
        ),
    )(
        tokens, latents, gain_self[None], w_qkv_tok, w_o_tok, gain_read[None], w_kv_read,
        gain_lat[None], w_q_read, gain_glob[None], w_qkv_glob, w_o_glob, gain_write[None],
        w_q_write, gain_wlat[None], w_kv_write,
    )
    per_group = pl.BlockSpec((G, width), lambda g: (g, 0))
    per_lat = pl.BlockSpec((NLAT, lat_width), lambda g: (g, 0))
    return pl.pallas_call(
        back,
        grid=(groups,),
        out_shape=(
            jax.ShapeDtypeStruct(tokens.shape, BF16),
            jax.ShapeDtypeStruct(latents.shape, BF16),
        ),
        in_specs=[
            per_group,
            per_lat,
            per_group,
            pl.BlockSpec((NLAT, key_vals.shape[1]), lambda g: (g, 0)),
        ],
        out_specs=(per_group, per_lat),
    )(query, final, mid, key_vals)


def solution(mesh):
    rows = P(("dp", "lat"), None)
    whole = P()
    placed = (
        rows, rows, whole, whole, whole, whole, whole, whole, whole, whole,
        P(None, None, "lat"), P("lat", None), whole, whole, whole, whole,
    )
    return jax.shard_map(
        local, mesh=mesh, in_specs=placed, out_specs=(rows, rows), check_vma=False
    )
```

```python
import functools

import jax
import jax.numpy as jnp
from jax import lax
from jax.experimental import pallas as pl
from jax.experimental.pallas import tpu as pltpu
from jax.sharding import PartitionSpec as P

HEAD = 64
G = 256
NLAT = 16
SCALE = HEAD ** (-0.5)
LOG2E = 1.4426950408889634
MESH = pl.DeviceIdType.MESH
PARTS = 4
F32 = jnp.float32
BF16 = jnp.bfloat16


def rms_norm(values, gain):
    floats = values.astype(F32)
    factor = lax.rsqrt(jnp.mean(floats * floats, axis=-1, keepdims=True) + 1e-06)
    return (floats * factor * gain).astype(BF16)


def dot(a, b):
    return jnp.dot(a, b, preferred_element_type=F32)


def dot_nt(a, b):
    return lax.dot_general(a, b, (((1,), (1,)), ((), ())), preferred_element_type=F32)


def dot_tn(a, b):
    return lax.dot_general(a, b, (((0,), (0,)), ((), ())), preferred_element_type=F32)


def spread_heads(query, count):
    lane_head = lax.broadcasted_iota(jnp.int32, query.shape, 1) // HEAD
    zero = jnp.zeros_like(query)
    return jnp.concatenate([jnp.where(lane_head == h, query, zero) for h in range(count)], axis=0)


def fold_heads(stacked, count):
    rows = stacked.shape[0] // count
    lane_head = lax.broadcasted_iota(jnp.int32, (rows, stacked.shape[1]), 1) // HEAD
    out = stacked[:rows]
    for h in range(1, count):
        out = jnp.where(lane_head == h, stacked[h * rows : (h + 1) * rows], out)
    return out


def softmax_mix(stacked, keys, values):
    scores = dot_nt(stacked, keys)
    peak = jnp.max(scores, axis=-1, keepdims=True)
    weights = jnp.exp2(scores - peak)
    total = jnp.sum(weights, axis=-1, keepdims=True)
    return dot(weights.astype(BF16), values) * (1.0 / total)


def kernel(
    dp_count,
    lat_count,
    tok_h,
    lat_h,
    g_self_h,
    w_qkv_h,
    w_o_h,
    g_read_h,
    w_kvr_h,
    g_lat_h,
    w_qr_h,
    g_glob_h,
    w_glob_h,
    w_og_h,
    g_write_h,
    w_qw_h,
    g_wlat_h,
    w_kvw_h,
    tok_out,
    lat_out,
    mid,
    lfin,
    tok,
    lat_in,
    g_self,
    g_read,
    g_lat,
    g_glob,
    g_write,
    g_wlat,
    w_qkv,
    w_o,
    w_kvr,
    w_qr,
    w_glob,
    w_og,
    w_qw,
    w_kvw,
    lmid,
    packed,
    mixed,
    read_q,
    gath,
    kv,
    qq,
    msend,
    mrecv,
    top,
    norm,
    acc,
    load_sem,
    z_send,
    z_recv,
    f_send,
    f_recv,
    s_send,
    s_recv,
    c_send,
    c_recv,
    wo_send,
    wo_recv,
    m_send,
    m_recv,
):
    width = tok_h.shape[1]
    lat_width = lat_h.shape[1]
    groups = tok_h.shape[0] // G
    lat_rows = lat_h.shape[0]
    nz = dp_count // 2
    dp = lax.axis_index("dp")
    lat = lax.axis_index("lat")
    z, x = dp // 2, dp % 2
    y, core = lat // 2, lat % 2
    dp_x = dp + 1 - 2 * x
    lat_y = (lat + 2) % 4
    partner = lat + 1 - 2 * core
    diag = (partner + 2) % 4
    a = (1 - core) * y + core * x
    b = (1 - core) * x + core * y
    first = ((1 - core) * dp + core * dp_x, (1 - core) * lat_y + core * lat)
    second = ((1 - core) * dp_x + core * dp, (1 - core) * lat + core * lat_y)
    base = (b * 2 + a) * nz
    other = (b * 2 + 1 - a) * nz
    me = base + z
    far = (1 - 2 * b) * 2 * nz
    run = nz // PARTS

    loads = []

    def load(src, dst):
        loads.append(pltpu.make_async_copy(src, dst, load_sem.at[len(loads)]))
        loads[-1].start()
        return loads[-1]

    def group_load(g):
        rows = pl.ds(g * G, G)
        return load(tok_h.at[rows], tok.at[rows])

    tok_load = [group_load(0)]
    gain_load = [load(g_self_h, g_self)]
    qkv_load = load(w_qkv_h, w_qkv)

    barrier = pltpu.get_barrier_semaphore()

    def greet(offset, carry):
        pl.semaphore_signal(
            barrier, inc=1, device_id=((z + offset) % nz * 2 + x, lat), device_id_type=MESH
        )
        return carry

    lax.fori_loop(1, nz, greet, 0)
    for peer in ((dp_x, lat), (dp, lat_y), (dp, partner), (dp, diag)):
        pl.semaphore_signal(barrier, inc=1, device_id=peer, device_id_type=MESH)

    o_load = load(w_o_h, w_o)
    for src, dst in ((lat_h, lat_in), (g_lat_h, g_lat), (g_read_h, g_read), (g_glob_h, g_glob), (g_write_h, g_write), (g_wlat_h, g_wlat)):
        gain_load.append(load(src, dst))
    qr_load = load(w_qr_h, w_qr)
    kvr_load = load(w_kvr_h, w_kvr)
    for g in range(1, groups):
        tok_load.append(group_load(g))

    def remote(src, dst, send_sem, recv_sem, peer):
        return pltpu.make_async_remote_copy(
            src_ref=src, dst_ref=dst, send_sem=send_sem, recv_sem=recv_sem, device_id=peer,
            device_id_type=MESH,
        )

    wo_share = remote(w_og_h, w_og.at[lat], wo_send.at[0], wo_recv.at[0], (dp, partner))
    wo_cross, wo_relay = [], []
    wo_rows = w_og_h.shape[0] // 2
    for i in range(2):
        part_rows = pl.ds(i * wo_rows, wo_rows)
        there = w_og.at[lat_y, part_rows]
        wo_cross.append(
            remote(w_og_h.at[part_rows], w_og.at[lat, part_rows], wo_send.at[1 + i], wo_recv.at[1 + i], (dp, lat_y))
        )
        wo_relay.append(remote(there, there, wo_send.at[3 + i], wo_recv.at[3 + i], (dp, partner)))

    def piece(g, start, count):
        return gath.at[g, core, pl.ds(start, count)]

    def along(ref, send_sem, recv_sem, peer):
        return remote(ref, ref, send_sem, recv_sem, peer)

    def on_first(g, p):
        return along(
            piece(g, base + p * run, run), f_send.at[g, p], f_recv.at[g, p], first
        )

    def on_second(g, half, p):
        start = base + (other - base) * half + p * run
        k = half * PARTS + p
        return along(piece(g, start, run), s_send.at[g, k], s_recv.at[g, k], second)

    def share(g, line, p):
        start = (base, other, base + far, other + far)[line] + p * run
        k = line * PARTS + p
        return along(
            piece(g, start, run), c_send.at[g, k], c_recv.at[g, k], (dp, partner)
        )

    late_half = z * 2 // nz

    def near(o):
        q = z // run
        return q + o - 2 * ((q % 2) * (o % 2) + 2 * (q // 2) * (o // 2))

    def z_copy(g, step):
        offset = late_half * step + (1 - late_half) * (nz - step)
        return remote(
            gath.at[g, core, me], gath.at[g, core, me], z_send.at[g, (z + offset) % nz],
            z_recv.at[g, z], ((z + offset) % nz * 2 + x, lat),
        )

    def each(low, high, body):
        def one(i, carry):
            body(i)
            return carry

        lax.fori_loop(low, high, one, 0)

    def z_start(g):
        each(1, nz, lambda offset: z_copy(g, offset).start())

    def z_arrived(g, block):
        ref = piece(g, base + block, 1)

        @pl.when(block != z)
        def _():
            pltpu.make_async_copy(ref, ref, z_recv.at[g, block]).wait()

    def stage_one(g, low, high):
        def body(o):
            p = near(o)
            each(0, run, lambda i: z_arrived(g, p * run + i))
            on_first(g, p).start()
            on_second(g, 0, p).start()
            share(g, 0, p).start()

        each(low, high, body)

    def stage_two(g, low=0, high=PARTS):
        def body(o):
            p = near(o)
            on_first(g, p).wait_recv()
            on_second(g, 1, p).start()
            share(g, 1, p).start()

        each(low, high, body)

    def second_arrived(g, half, o):
        p = near(o)
        on_second(g, half, p).wait_recv()
        share(g, 2 + half, p).start()

    def stage_three(g):
        for half in range(2):
            each(0, PARTS, lambda o: second_arrived(g, half, o))

    def gathered(g):
        for line in range(4):
            each(0, PARTS, lambda p: share(g, line, p).wait_recv())

    later = []

    def self_part(g):
        rows = pl.ds(g * G, G)
        tok_load[g].wait()
        if g == 0:
            gain_load[0].wait()
        group = tok[rows, :]
        normed = rms_norm(group, g_self[...])
        if g == 0:
            qkv_load.wait()
            for src, dst in ((w_glob_h, w_glob), (w_qw_h, w_qw), (w_kvw_h, w_kvw), (w_og_h, w_og.at[lat])):
                later.append(load(src, dst))
        packed[:, :width] = (dot(normed, w_qkv[:, :width]) * (SCALE * LOG2E)).astype(BF16)
        packed[:, width:] = dot(normed, w_qkv[:, width:]).astype(BF16)
        for pair in range(width // (2 * HEAD)):
            at = pair * 2 * HEAD
            query = packed[:, at : at + 2 * HEAD]
            keys = packed[:, width + at : width + at + 2 * HEAD]
            values = packed[:, 2 * width + at : 2 * width + at + 2 * HEAD]
            out = softmax_mix(spread_heads(query, 2), keys, values)
            mixed[:, at : at + 2 * HEAD] = fold_heads(out, 2).astype(BF16)
        if g == 0:
            o_load.wait()
        mid[rows, :] = (group.astype(F32) + dot(mixed[...], w_o[...])).astype(BF16)

    quad = 4 * HEAD

    def read_queries():
        for copy in gain_load[1:]:
            copy.wait()
        qr_load.wait()
        query = dot(rms_norm(lat_in[...], g_lat[...]), w_qr[...])
        query = (query * (SCALE * LOG2E)).astype(BF16)
        kvr_load.wait()
        for at in range(0, lat_width, quad):
            keyed = dot_nt(spread_heads(query[:, at : at + quad], 4), w_kvr[:, at : at + quad]).astype(BF16)
            for h in range(4):
                for g in range(groups):
                    start = h * lat_rows + g * NLAT
                    head = at // HEAD + h
                    read_q[g, head * NLAT : (head + 1) * NLAT, :] = keyed[start : start + NLAT, :]

    def read_part(g):
        if g == 0:
            read_queries()
        rows = pl.ds(g * G, G)
        lrows = pl.ds(g * NLAT, NLAT)
        normed = rms_norm(mid[rows, :], g_read[...])
        scores = dot_nt(read_q[g], normed)
        peak = jnp.max(scores, axis=-1, keepdims=True)
        weights = jnp.exp2(scores - peak)
        inverse = 1.0 / jnp.sum(weights, axis=-1, keepdims=True)
        seen = (dot(weights.astype(BF16), normed) * inverse).astype(BF16)
        for at in range(0, lat_width, quad):
            start = at // HEAD * NLAT
            out = dot(seen[start : start + 4 * NLAT], w_kvr[:, lat_width + at : lat_width + at + quad])
            lmid[lrows, at : at + quad] = (
                lat_in[lrows, at : at + quad].astype(F32) + fold_heads(out, 4)
            ).astype(BF16)
        gath[g, core, me] = rms_norm(lmid[lrows, :], g_glob[...])
        z_start(g)
        stage_one(g, 0, 1)

    def scope(name):
        return jax.named_scope(name)

    last = groups - 1
    for g in range(groups):
        with scope(f"self{g}"):
            self_part(g)
        if g == 0:
            with scope("bar"):
                pl.semaphore_wait(barrier, nz + 3)
            wo_share.start()
            wo_cross[0].start()
        if g >= 2:
            with scope("fwdA"):
                stage_one(g - 2, 2, PARTS)
                if g == 2:
                    wo_cross[0].wait_recv()
                    wo_relay[0].start()
        with scope(f"read{g}"):
            read_part(g)
        if g >= 1 and g < last:
            with scope("fwdB"):
                stage_one(g - 1, 1, 2)

    block_rows = 4 * nz * NLAT
    tile = min(block_rows, G)
    blocks = tile // NLAT

    def project(g, c):
        def one(i, carry):
            rows = gath[g, c, pl.ds(i * blocks, blocks)].reshape(tile, lat_width)
            at = pl.multiple_of((g * 2 + c) * block_rows + i * tile, tile)
            kv[0, pl.ds(at, tile), :] = dot(rows, w_glob[1]).astype(BF16)
            kv[1, pl.ds(at, tile), :] = dot(rows, w_glob[2]).astype(BF16)
            return carry

        lax.fori_loop(0, block_rows // tile, one, 0)

    with scope("fwdC"):
        for g in range(last - 1):
            stage_two(g)
        stage_one(last - 1, 1, PARTS)
    later[1].wait()
    with scope("wq"):
        for g in range(groups):
            rows = pl.ds(g * G, G)
            query = dot(rms_norm(mid[rows, :], g_write[...]), w_qw[...]).astype(BF16)
            tok_out[rows, :] = query * jnp.asarray(SCALE, BF16)
    later[0].wait()
    with scope("fwdD"):
        for g in range(last - 1):
            stage_three(g)
        stage_two(last - 1)
    for g in range(last - 1):
        with scope("gath0"):
            gathered(g)
        with scope("proj0"):
            project(g, 0)
            project(g, 1)
    with scope("fwdE"):
        stage_one(last, 1, PARTS)
        stage_three(last - 1)
    with scope("fwdF"):
        stage_two(last)
        wo_cross[1].start()
    with scope("gath1"):
        gathered(last - 1)
    with scope("proj1"):
        project(last - 1, 0)
        project(last - 1, 1)
    own_p = z // run

    with scope('ownw'):
        @pl.when(core == 1)
        def _():
            on_second(last, 0, own_p).wait_recv()
            share(last, 2, own_p).start()
            for line in range(2):
                share(last, line, own_p).wait_recv()

        @pl.when(core == 0)
        def _():
            for line in (0, 2):
                share(last, line, own_p).wait_recv()

    own = []
    for l in range(lat_count):
        ly, lc = l // 2, l % 2
        index = ((x * 2 + ly) if lc == 0 else (ly * 2 + x)) * nz + z
        for g in range(groups):
            own.append(gath[g, lc, index])
    query = dot(jnp.concatenate(own, axis=0), w_glob[0])
    query = (query * (SCALE * LOG2E)).astype(BF16)
    heads = query.shape[1] // HEAD
    part = lat_rows * heads
    for l in range(lat_count):
        qq[l * part : (l + 1) * part, :] = spread_heads(query[l * lat_rows : (l + 1) * lat_rows], heads)
    early = last * 2 * block_rows
    wide = early * part <= 2**20
    step = part if wide else part // heads

    def attend_early(at):
        rows = pl.ds(pl.multiple_of(at, 16), step)
        scores = dot_nt(qq[rows, :], kv[0, :early, :])
        peak = jnp.max(scores, axis=-1, keepdims=True)
        weights = jnp.exp2(scores - peak)
        top[rows, :] = peak
        norm[rows, :] = jnp.sum(weights, axis=-1, keepdims=True)
        acc[rows, :] = dot(weights.astype(BF16), kv[1, :early, :])

    def attend_late(at):
        rows = pl.ds(pl.multiple_of(at, 16), step)
        scores = dot_nt(qq[rows, :], kv[0, early:, :])
        peak = jnp.maximum(top[rows, :], jnp.max(scores, axis=-1, keepdims=True))
        weights = jnp.exp2(scores - peak)
        keep = jnp.exp2(top[rows, :] - peak)
        total = norm[rows, :] * keep + jnp.sum(weights, axis=-1, keepdims=True)
        both = acc[rows, :] * keep + dot(weights.astype(BF16), kv[1, early:, :])
        return both * (1.0 / total)

    with scope("attE"):
        if wide:
            for l in range(lat_count):
                attend_early(l * part)
        else:
            each(0, qq.shape[0] // step, lambda i: attend_early(i * step))

    with scope('lastw'):
        @pl.when(core == 1)
        def _():
            each(1, PARTS, lambda o: second_arrived(last, 0, o))
            each(0, PARTS, lambda o: second_arrived(last, 1, o))
            for line in range(2):
                each(1, PARTS, lambda o: share(last, line, near(o)).wait_recv())
            for line in range(2, 4):
                each(0, PARTS, lambda p: share(last, line, p).wait_recv())

        @pl.when(core == 0)
        def _():
            stage_three(last)
            for line in (0, 2):
                each(1, PARTS, lambda o: share(last, line, near(o)).wait_recv())
            for line in (1, 3):
                each(0, PARTS, lambda p: share(last, line, p).wait_recv())

    with scope("proj2"):
        project(last, 0)
        project(last, 1)
    with scope("woB"):
        wo_cross[1].wait_recv()
        wo_relay[1].start()
    mix_copies = []
    with scope("attL"):
        for i, peer in enumerate((diag, lat_y, partner, lat)):
            if wide:
                result = fold_heads(attend_late(peer * part), heads)
            else:
                def late_step(k, carry):
                    at = peer * part + k * step
                    qq[pl.ds(pl.multiple_of(at, 16), step), :] = attend_late(at).astype(BF16)
                    return carry

                lax.fori_loop(0, heads, late_step, 0)
                result = fold_heads(qq[pl.ds(pl.multiple_of(peer * part, 16), part), :], heads)
            if i < 3:
                msend[peer] = result.astype(BF16)
                mix_copies.append(
                    remote(msend.at[peer], mrecv.at[lat], m_send.at[i], m_recv.at[i], (dp, peer))
                )
                mix_copies[-1].start()
            else:
                mrecv[lat] = result.astype(BF16)
    later[3].wait()
    later[2].wait()
    with scope("mixw"):
        wo_share.wait_recv()
        for copy in wo_relay:
            copy.wait_recv()
        for copy in mix_copies:
            copy.wait_recv()
    total = dot(mrecv[0], w_og[0])
    for l in range(1, lat_count):
        total = total + dot(mrecv[l], w_og[l])
    final = (lmid[...].astype(F32) + total).astype(BF16)
    lat_out[...] = final
    lfin[...] = dot(rms_norm(final, g_wlat[...]), w_kvw[...]).astype(BF16)

    for copy in [wo_share] + wo_cross + wo_relay + mix_copies:
        copy.wait_send()
    for g in range(groups):
        each(1, nz, lambda offset: z_copy(g, offset).wait_send())

        def sent(p):
            on_first(g, p).wait_send()
            for half in range(2):
                on_second(g, half, p).wait_send()
            for line in range(4):
                share(g, line, p).wait_send()

        each(0, PARTS, sent)


def back(query, final, mid, key_vals, tok_out, lat_out):
    width = query.shape[1]
    heads = width // HEAD
    keys = spread_heads(key_vals[:, :width], heads)
    values = spread_heads(key_vals[:, width:], heads)
    scores = dot_nt(keys, query[...]).reshape(heads, NLAT, G)
    peak = jnp.max(scores, axis=1, keepdims=True)
    weights = jnp.exp(scores - peak)
    weights = weights * (1.0 / jnp.sum(weights, axis=1, keepdims=True))
    written = dot_tn(weights.reshape(heads * NLAT, G).astype(BF16), values)
    tok_out[...] = (mid[...].astype(F32) + written).astype(BF16)
    lat_out[...] = final[...]


def local(
    tokens, latents, gain_self, w_qkv_tok, w_o_tok, gain_read, w_kv_read, gain_lat, w_q_read,
    gain_glob, w_qkv_glob, w_o_glob, gain_write, w_q_write, gain_wlat, w_kv_write,
):
    dp_count = lax.axis_size("dp")
    lat_count = lax.axis_size("lat")
    rows, width = tokens.shape
    lat_rows, lat_width = latents.shape
    groups = rows // G
    here = w_qkv_glob.shape[2]
    nz = dp_count // 2
    all_rows = lat_rows * dp_count * lat_count
    vmem = pl.BlockSpec(memory_space=pltpu.VMEM)
    hbm = pl.BlockSpec(memory_space=pl.ANY)
    dma = pltpu.SemaphoreType.DMA
    query, final, mid, key_vals = pl.pallas_call(
        functools.partial(kernel, dp_count, lat_count),
        out_shape=(
            jax.ShapeDtypeStruct(tokens.shape, BF16),
            jax.ShapeDtypeStruct(latents.shape, BF16),
            jax.ShapeDtypeStruct(tokens.shape, BF16),
            jax.ShapeDtypeStruct((lat_rows, w_kv_write.shape[1]), BF16),
        ),
        in_specs=[hbm] * 16,
        out_specs=(vmem,) * 4,
        scratch_shapes=[
            pltpu.VMEM(tokens.shape, BF16),
            pltpu.VMEM(latents.shape, BF16),
            pltpu.VMEM((1, width), F32),
            pltpu.VMEM((1, width), F32),
            pltpu.VMEM((1, lat_width), F32),
            pltpu.VMEM((1, lat_width), F32),
            pltpu.VMEM((1, width), F32),
            pltpu.VMEM((1, lat_width), F32),
            pltpu.VMEM(w_qkv_tok.shape, BF16),
            pltpu.VMEM(w_o_tok.shape, BF16),
            pltpu.VMEM(w_kv_read.shape, BF16),
            pltpu.VMEM(w_q_read.shape, BF16),
            pltpu.VMEM(w_qkv_glob.shape, BF16),
            pltpu.VMEM((lat_count,) + w_o_glob.shape, BF16),
            pltpu.VMEM(w_q_write.shape, BF16),
            pltpu.VMEM(w_kv_write.shape, BF16),
            pltpu.VMEM(latents.shape, BF16),
            pltpu.VMEM((G, w_qkv_tok.shape[1]), BF16),
            pltpu.VMEM((G, width), BF16),
            pltpu.VMEM((groups, lat_width // HEAD * NLAT, width), BF16),
            pltpu.VMEM((groups, 2, 4 * nz, NLAT, lat_width), BF16),
            pltpu.VMEM((2, all_rows, here), BF16),
            pltpu.VMEM((lat_rows * lat_count * (here // HEAD), here), BF16),
            pltpu.VMEM((lat_count, lat_rows, here), BF16),
            pltpu.VMEM((lat_count, lat_rows, here), BF16),
            pltpu.VMEM((lat_rows * lat_count * (here // HEAD), 1), F32),
            pltpu.VMEM((lat_rows * lat_count * (here // HEAD), 1), F32),
            pltpu.VMEM((lat_rows * lat_count * (here // HEAD), here), F32),
            dma((15 + groups,)),
            dma((groups, nz)),
            dma((groups, nz)),
            dma((groups, PARTS)),
            dma((groups, PARTS)),
            dma((groups, 2 * PARTS)),
            dma((groups, 2 * PARTS)),
            dma((groups, 4 * PARTS)),
            dma((groups, 4 * PARTS)),
            dma((5,)),
            dma((5,)),
            dma((3,)),
            dma((3,)),
        ],
        compiler_params=pltpu.CompilerParams(
            collective_id=0, has_side_effects=True, vmem_limit_bytes=67043328
        ),
    )(
        tokens, latents, gain_self[None], w_qkv_tok, w_o_tok, gain_read[None], w_kv_read,
        gain_lat[None], w_q_read, gain_glob[None], w_qkv_glob, w_o_glob, gain_write[None],
        w_q_write, gain_wlat[None], w_kv_write,
    )
    per_group = pl.BlockSpec((G, width), lambda g: (g, 0))
    per_lat = pl.BlockSpec((NLAT, lat_width), lambda g: (g, 0))
    return pl.pallas_call(
        back,
        grid=(groups,),
        out_shape=(
            jax.ShapeDtypeStruct(tokens.shape, BF16),
            jax.ShapeDtypeStruct(latents.shape, BF16),
        ),
        in_specs=[
            per_group,
            per_lat,
            per_group,
            pl.BlockSpec((NLAT, key_vals.shape[1]), lambda g: (g, 0)),
        ],
        out_specs=(per_group, per_lat),
    )(query, final, mid, key_vals)


def solution(mesh):
    rows = P(("dp", "lat"), None)
    whole = P()
    placed = (
        rows, rows, whole, whole, whole, whole, whole, whole, whole, whole,
        P(None, None, "lat"), P("lat", None), whole, whole, whole, whole,
    )
    return jax.shard_map(
        local, mesh=mesh, in_specs=placed, out_specs=(rows, rows), check_vma=False
    )
```

```python
import functools

import jax
import jax.numpy as jnp
from jax import lax
from jax.experimental import pallas as pl
from jax.experimental.pallas import tpu as pltpu
from jax.sharding import PartitionSpec as P

HEAD = 64
G = 256
NLAT = 16
SCALE = HEAD ** (-0.5)
LOG2E = 1.4426950408889634
MESH = pl.DeviceIdType.MESH
F32 = jnp.float32
BF16 = jnp.bfloat16


def rms_norm(values, gain):
    floats = values.astype(F32)
    factor = lax.rsqrt(jnp.mean(floats * floats, axis=-1, keepdims=True) + 1e-06)
    return (floats * factor * gain).astype(BF16)


def dot(a, b):
    return jnp.dot(a, b, preferred_element_type=F32)


def dot_nt(a, b):
    return lax.dot_general(a, b, (((1,), (1,)), ((), ())), preferred_element_type=F32)


def dot_tn(a, b):
    return lax.dot_general(a, b, (((0,), (0,)), ((), ())), preferred_element_type=F32)


def spread_heads(query, count):
    lane_head = lax.broadcasted_iota(jnp.int32, query.shape, 1) // HEAD
    zero = jnp.zeros_like(query)
    return jnp.concatenate([jnp.where(lane_head == h, query, zero) for h in range(count)], axis=0)


def fold_heads(stacked, count):
    rows = stacked.shape[0] // count
    lane_head = lax.broadcasted_iota(jnp.int32, (rows, stacked.shape[1]), 1) // HEAD
    out = stacked[:rows]
    for h in range(1, count):
        out = jnp.where(lane_head == h, stacked[h * rows : (h + 1) * rows], out)
    return out


def softmax_mix(stacked, keys, values):
    scores = dot_nt(stacked, keys)
    peak = jnp.max(scores, axis=-1, keepdims=True)
    weights = jnp.exp2(scores - peak)
    total = jnp.sum(weights, axis=-1, keepdims=True)
    return dot(weights.astype(BF16), values) * (1.0 / total)


def kernel(
    dp_count, lat_count,
    tok_h, lat_h, g_self_h, w_qkv_h, w_o_h, g_read_h, w_kvr_h, g_lat_h, w_qr_h, g_glob_h,
    w_glob_h, w_og_h, g_write_h, w_qw_h, g_wlat_h, w_kvw_h,
    tok_out, lat_out, mid, lfin,
    tok, lat_in, g_self, g_read, g_lat, g_glob, g_write, g_wlat,
    w_qkv, w_o, w_kvr, w_qr, w_glob, w_og, w_qw, w_kvw,
    lmid, packed, mixed, read_q, normed_lat, outgoing, arrived, results, returned, mix,
    load_sem, l_send, l_recv, s_send, s_recv, t_send, t_recv, wo_send, wo_recv,
):
    width = tok_h.shape[1]
    lat_width = lat_h.shape[1]
    groups = tok_h.shape[0] // G
    lat_rows = lat_h.shape[0]
    last = groups - 1
    here = w_glob_h.shape[2] // HEAD
    slots = dp_count // here
    line = lat_count * NLAT
    lanes = 2 * HEAD
    dp = lax.axis_index("dp")
    lat = lax.axis_index("lat")
    head, slot = dp // slots, dp % slots
    core = lat % 2
    lat_y = (lat + 2) % 4
    partner = lat + 1 - 2 * core
    diag = (partner + 2) % 4
    upper = head * 2 // here

    def scope(name):
        return jax.named_scope(name)

    def each(low, high, body):
        def one(i, carry):
            body(i)
            return carry

        lax.fori_loop(low, high, one, 0)

    loads = []

    def load(src, dst):
        loads.append(pltpu.make_async_copy(src, dst, load_sem.at[len(loads)]))
        loads[-1].start()
        return loads[-1]

    def group_load(g):
        rows = pl.ds(g * G, G)
        return load(tok_h.at[rows], tok.at[rows])

    tok_load = [group_load(0)]
    gain_load = [load(g_self_h, g_self)]
    qkv_load = []
    for i in range(3):
        columns = pl.ds(i * width, width)
        qkv_load.append(load(w_qkv_h.at[:, columns], w_qkv.at[:, columns]))

    barrier = pltpu.get_barrier_semaphore()

    def greet(peer):
        pl.semaphore_signal(barrier, inc=1, device_id=peer, device_id_type=MESH)

    each(1, dp_count, lambda o: greet(((dp + o) % dp_count, lat)))
    for o in range(1, lat_count):
        each(0, here, lambda h: greet((h * slots + slot, (lat + o) % lat_count)))

    o_load = load(w_o_h, w_o)
    for src, dst in (
        (lat_h, lat_in), (g_lat_h, g_lat), (g_read_h, g_read), (g_glob_h, g_glob), (g_write_h, g_write),
        (g_wlat_h, g_wlat),
    ):
        gain_load.append(load(src, dst))
    qr_load = load(w_qr_h, w_qr)
    kvr_load = load(w_kvr_h, w_kvr)
    for g in range(1, groups):
        tok_load.append(group_load(g))
    later = []

    def remote(src, dst, send_sem, recv_sem, peer):
        return pltpu.make_async_remote_copy(
            src_ref=src, dst_ref=dst, send_sem=send_sem, recv_sem=recv_sem, device_id=peer,
            device_id_type=MESH,
        )

    def landed(ref, sem):
        pltpu.make_async_copy(ref, ref, sem).wait()

    wo_share = remote(w_og_h, w_og.at[lat], wo_send.at[0], wo_recv.at[0], (dp, partner))
    wo_cross, wo_relay = [], []
    wo_rows = w_og_h.shape[0] // 2
    for i in range(2):
        part_rows = pl.ds(i * wo_rows, wo_rows)
        there = w_og.at[lat_y, part_rows]
        wo_cross.append(
            remote(w_og_h.at[part_rows], w_og.at[lat, part_rows], wo_send.at[1 + i], wo_recv.at[1 + i], (dp, lat_y))
        )
        wo_relay.append(remote(there, there, wo_send.at[3 + i], wo_recv.at[3 + i], (dp, partner)))

    def lat_copy(g, i):
        own = normed_lat.at[g, lat]
        peer = (diag, lat_y, partner)[i]
        return remote(own, own, l_send.at[g, i], l_recv.at[g, lat], (dp, peer))

    def far(i):
        return upper * i + (1 - upper) * (here - 1 - i)

    def to_head(g, h, j):
        rows = pl.ds(0, line)
        src, dst = outgoing.at[g, h], arrived.at[g, dp]
        if j is not None:
            src, dst = src.at[rows], dst.at[rows]
        spot = 0 if j is None else j
        peer = (h * slots + (slot + spot) % slots, lat)
        return remote(src, dst, s_send.at[g, h * slots + spot], s_recv.at[g, dp], peer)

    def spread(g):
        def one(i):
            h = far(i)

            @pl.when(h != head)
            def _():
                to_head(g, h, None).start()

            each(1, slots, lambda j: to_head(g, h, j).start())

        each(0, here, one)
        arrived[g, dp] = outgoing[g, head]

    def gathered(g):
        def one(h):
            @pl.when(h != head)
            def _():
                source = h * slots + slot
                landed(arrived.at[g, source], s_recv.at[g, source])

            def other(j):
                source = h * slots + (slot + j) % slots
                landed(arrived.at[g, source, pl.ds(0, line)], s_recv.at[g, source])

            each(1, slots, other)

        each(0, here, one)

    def low_lanes(rows):
        return lax.broadcasted_iota(jnp.int32, (rows, lanes), 1) < HEAD

    def swap(values):
        return pltpu.roll(values, HEAD, 1)

    def project(g):
        for i in range(1, lat_count):
            source = (lat + i) % lat_count
            landed(normed_lat.at[g, source], l_recv.at[g, source])
        rows = normed_lat[g].reshape(line, lat_width)
        queries = dot(rows, w_glob[0]) * (SCALE * LOG2E)
        keys = dot(rows, w_glob[1])
        values = dot(rows, w_glob[2])
        low, half = low_lanes(line), line // 2
        for h in range(0, here, 2):
            at = slice(h * HEAD, h * HEAD + lanes)
            k, v, q = keys[:, at], values[:, at], queries[:, at]
            outgoing[g, h, :line] = jnp.where(low, k, swap(v)).astype(BF16)
            outgoing[g, h + 1, :line] = jnp.where(low, swap(k), v).astype(BF16)
            q_swap = swap(q)
            outgoing[g, h, line:] = jnp.where(low[:half], q[:half], q_swap[half:]).astype(BF16)
            outgoing[g, h + 1, line:] = jnp.where(low[:half], q_swap[:half], q[half:]).astype(BF16)
        spread(g)

    def self_part(g):
        rows = pl.ds(g * G, G)
        tok_load[g].wait()
        if g == 0:
            gain_load[0].wait()
        group = tok[rows, :]
        normed = rms_norm(group, g_self[...])
        if g == 0:
            qkv_load[0].wait()
        packed[:, :width] = (dot(normed, w_qkv[:, :width]) * (SCALE * LOG2E)).astype(BF16)
        if g == 0:
            qkv_load[1].wait()
            qkv_load[2].wait()
            for src, dst in (
                (w_glob_h, w_glob), (w_qw_h, w_qw), (w_kvw_h, w_kvw), (w_og_h, w_og.at[lat]),
            ):
                later.append(load(src, dst))
        packed[:, width:] = dot(normed, w_qkv[:, width:]).astype(BF16)
        for pair in range(width // lanes):
            at = pair * lanes
            query = packed[:, at : at + lanes]
            keys = packed[:, width + at : width + at + lanes]
            values = packed[:, 2 * width + at : 2 * width + at + lanes]
            out = softmax_mix(spread_heads(query, 2), keys, values)
            mixed[:, at : at + lanes] = fold_heads(out, 2).astype(BF16)
        if g == 0:
            o_load.wait()
        mid[rows, :] = (group.astype(F32) + dot(mixed[...], w_o[...])).astype(BF16)

    quad = 4 * HEAD

    def read_queries():
        for copy in gain_load[1:]:
            copy.wait()
        qr_load.wait()
        query = dot(rms_norm(lat_in[...], g_lat[...]), w_qr[...])
        query = (query * (SCALE * LOG2E)).astype(BF16)
        kvr_load.wait()
        for at in range(0, lat_width, quad):
            keyed = dot_nt(spread_heads(query[:, at : at + quad], 4), w_kvr[:, at : at + quad]).astype(BF16)
            for h in range(4):
                for g in range(groups):
                    start = h * lat_rows + g * NLAT
                    at_head = at // HEAD + h
                    read_q[g, at_head * NLAT : (at_head + 1) * NLAT, :] = keyed[start : start + NLAT, :]

    def read_part(g):
        if g == 0:
            read_queries()
        rows = pl.ds(g * G, G)
        lrows = pl.ds(g * NLAT, NLAT)
        normed = rms_norm(mid[rows, :], g_read[...])
        scores = dot_nt(read_q[g], normed)
        peak = jnp.max(scores, axis=-1, keepdims=True)
        weights = jnp.exp2(scores - peak)
        inverse = 1.0 / jnp.sum(weights, axis=-1, keepdims=True)
        seen = (dot(weights.astype(BF16), normed) * inverse).astype(BF16)
        for at in range(0, lat_width, quad):
            start = at // HEAD * NLAT
            out = dot(seen[start : start + 4 * NLAT], w_kvr[:, lat_width + at : lat_width + at + quad])
            lmid[lrows, at : at + quad] = (
                lat_in[lrows, at : at + quad].astype(F32) + fold_heads(out, 4)
            ).astype(BF16)
        normed_lat[g, lat] = rms_norm(lmid[lrows, :], g_glob[...])
        for i in range(3):
            lat_copy(g, i).start()

    for g in range(groups):
        with scope(f"self{g}"):
            self_part(g)
        if g == 0:
            with scope("bar"):
                pl.semaphore_wait(barrier, dp_count - 1 + here * (lat_count - 1))
            wo_share.start()
        with scope(f"read{g}"):
            read_part(g)
        if g == 1:
            later[0].wait()
        if 1 <= g < last:
            with scope(f"proj{g - 1}"):
                project(g - 1)
    for copy in wo_cross:
        copy.start()
    with scope("projM"):
        project(last - 1)
    later[1].wait()
    with scope("wq"):
        for g in range(groups):
            rows = pl.ds(g * G, G)
            query = dot(rms_norm(mid[rows, :], g_write[...]), w_qw[...]).astype(BF16)
            tok_out[rows, :] = query * jnp.asarray(SCALE, BF16)
    with scope("projL"):
        project(last)
    later[2].wait()
    later[3].wait()
    for g in range(last):
        with scope(f"gath{g}"):
            gathered(g)
    with scope("wo0"):
        wo_cross[0].wait_recv()
        wo_relay[0].start()
    with scope("gathL"):
        gathered(last)

    def queries_of(c):
        parts = []
        for g in range(groups):
            pack = arrived[g, c * slots + slot, line:].astype(F32)
            low = low_lanes(line // 2)
            parts.append(jnp.where(low, pack, 0.0))
            parts.append(jnp.where(low, swap(pack), 0.0))
        return jnp.concatenate(parts, axis=0).astype(BF16)

    def attend(c):
        query = queries_of(c)
        if dp_count * line * groups <= 2048:
            key_vals = jnp.concatenate(
                [arrived[g, d, :line] for g in range(groups) for d in range(dp_count)], axis=0
            )
            return softmax_mix(query, key_vals, key_vals)

        def fold(i, carry):
            peak, total, acc = carry
            for g in range(groups):
                key_vals = arrived[g, i, :line]
                scores = dot_nt(query, key_vals)
                new = jnp.maximum(peak, jnp.max(scores, axis=-1, keepdims=True))
                weights = jnp.exp2(scores - new)
                keep = jnp.exp2(peak - new)
                total = total * keep + jnp.sum(weights, axis=-1, keepdims=True)
                acc = acc * keep + dot(weights.astype(BF16), key_vals)
                peak = new
            return peak, total, acc

        rows = query.shape[0]
        first = (
            jnp.full((rows, 1), -jnp.inf, F32), jnp.zeros((rows, 1), F32), jnp.zeros((rows, lanes), F32)
        )
        _, total, acc = lax.fori_loop(0, dp_count, fold, first)
        return acc * (1.0 / total)

    mine = lat * here + head

    def result_copy(c, i):
        to = (lat + i) % lat_count
        return remote(
            results.at[c, to], returned.at[mine], t_send.at[c, to], t_recv.at[mine], (c * slots + slot, to)
        )

    with scope("att"):
        for i in range(here):
            c = (head + 1 + i) % here
            out = attend(c)
            low = low_lanes(line)
            for k in range(0, groups, 2):
                even = out[k * line : (k + 1) * line]
                odd = out[(k + 1) * line : (k + 2) * line] if k + 1 < groups else even
                pair = jnp.where(low, swap(even), odd).astype(BF16)
                for l in range(lat_count):
                    results[c, l, k // 2 * NLAT : (k // 2 + 1) * NLAT] = pair[l * NLAT : (l + 1) * NLAT]
            for l in range(1, lat_count):
                result_copy(c, l).start()
            if i < here - 1:
                result_copy(c, 0).start()
            else:
                returned[mine] = results[c, lat]
    with scope("wo1"):
        wo_cross[1].wait_recv()
        wo_relay[1].start()
    with scope("retw"):
        def back_from(h):
            @pl.when(h != mine)
            def _():
                landed(returned.at[h], t_recv.at[h])

        each(0, lat_count * here, back_from)
        wo_share.wait_recv()
        for copy in wo_relay:
            copy.wait_recv()
    with scope("final"):
        low = low_lanes(NLAT)
        for p in range(lat_count * here // 2):
            a, b = returned[2 * p].astype(F32), returned[2 * p + 1].astype(F32)
            a_swap, b_swap = swap(a), swap(b)
            for g in range(groups):
                at = slice(g // 2 * NLAT, (g // 2 + 1) * NLAT)
                both = jnp.where(low, a[at], b_swap[at]) if g % 2 == 0 else jnp.where(low, a_swap[at], b[at])
                mix[g * NLAT : (g + 1) * NLAT, p * lanes : (p + 1) * lanes] = both.astype(BF16)
        total = dot(mix[...], w_og[...].reshape(lat_width, lat_width))
        final = (lmid[...].astype(F32) + total).astype(BF16)
        lat_out[...] = final
        lfin[...] = dot(rms_norm(final, g_wlat[...]), w_kvw[...]).astype(BF16)

    with scope("drain"):
        for copy in [wo_share] + wo_cross + wo_relay:
            copy.wait_send()
        for g in range(groups):
            for i in range(3):
                lat_copy(g, i).wait_send()

            def sent(h):
                @pl.when(h != head)
                def _():
                    to_head(g, h, None).wait_send()

                each(1, slots, lambda j: to_head(g, h, j).wait_send())

            each(0, here, sent)

        def answered(c):
            for l in range(1, lat_count):
                result_copy(c, l).wait_send()

            @pl.when(c != head)
            def _():
                result_copy(c, 0).wait_send()

        each(0, here, answered)


def back(query, final, mid, key_vals, tok_out, lat_out):
    width = query.shape[1]
    heads = width // HEAD
    keys = spread_heads(key_vals[:, :width], heads)
    values = spread_heads(key_vals[:, width:], heads)
    scores = dot_nt(keys, query[...]).reshape(heads, NLAT, G)
    peak = jnp.max(scores, axis=1, keepdims=True)
    weights = jnp.exp(scores - peak)
    weights = weights * (1.0 / jnp.sum(weights, axis=1, keepdims=True))
    written = dot_tn(weights.reshape(heads * NLAT, G).astype(BF16), values)
    tok_out[...] = (mid[...].astype(F32) + written).astype(BF16)
    lat_out[...] = final[...]


def local(
    tokens, latents, gain_self, w_qkv_tok, w_o_tok, gain_read, w_kv_read, gain_lat, w_q_read,
    gain_glob, w_qkv_glob, w_o_glob, gain_write, w_q_write, gain_wlat, w_kv_write,
):
    dp_count = lax.axis_size("dp")
    lat_count = lax.axis_size("lat")
    rows, width = tokens.shape
    lat_rows, lat_width = latents.shape
    groups = rows // G
    here = w_qkv_glob.shape[2] // HEAD
    line = lat_count * NLAT
    packs = (groups + 1) // 2
    vmem = pl.BlockSpec(memory_space=pltpu.VMEM)
    hbm = pl.BlockSpec(memory_space=pl.ANY)
    dma = pltpu.SemaphoreType.DMA
    query, final, mid, key_vals = pl.pallas_call(
        functools.partial(kernel, dp_count, lat_count),
        out_shape=(
            jax.ShapeDtypeStruct(tokens.shape, BF16),
            jax.ShapeDtypeStruct(latents.shape, BF16),
            jax.ShapeDtypeStruct(tokens.shape, BF16),
            jax.ShapeDtypeStruct((lat_rows, w_kv_write.shape[1]), BF16),
        ),
        in_specs=[hbm] * 16,
        out_specs=(vmem,) * 4,
        scratch_shapes=[
            pltpu.VMEM(tokens.shape, BF16),
            pltpu.VMEM(latents.shape, BF16),
            pltpu.VMEM((1, width), F32),
            pltpu.VMEM((1, width), F32),
            pltpu.VMEM((1, lat_width), F32),
            pltpu.VMEM((1, lat_width), F32),
            pltpu.VMEM((1, width), F32),
            pltpu.VMEM((1, lat_width), F32),
            pltpu.VMEM(w_qkv_tok.shape, BF16),
            pltpu.VMEM(w_o_tok.shape, BF16),
            pltpu.VMEM(w_kv_read.shape, BF16),
            pltpu.VMEM(w_q_read.shape, BF16),
            pltpu.VMEM(w_qkv_glob.shape, BF16),
            pltpu.VMEM((lat_count,) + w_o_glob.shape, BF16),
            pltpu.VMEM(w_q_write.shape, BF16),
            pltpu.VMEM(w_kv_write.shape, BF16),
            pltpu.VMEM(latents.shape, BF16),
            pltpu.VMEM((G, w_qkv_tok.shape[1]), BF16),
            pltpu.VMEM((G, width), BF16),
            pltpu.VMEM((groups, lat_width // HEAD * NLAT, width), BF16),
            pltpu.VMEM((groups, lat_count, NLAT, lat_width), BF16),
            pltpu.VMEM((groups, here, line * 3 // 2, 2 * HEAD), BF16),
            pltpu.VMEM((groups, dp_count, line * 3 // 2, 2 * HEAD), BF16),
            pltpu.VMEM((here, lat_count, packs * NLAT, 2 * HEAD), BF16),
            pltpu.VMEM((lat_count * here, packs * NLAT, 2 * HEAD), BF16),
            pltpu.VMEM(latents.shape, BF16),
            dma((17 + groups,)),
            dma((groups, 3)),
            dma((groups, lat_count)),
            dma((groups, dp_count)),
            dma((groups, dp_count)),
            dma((here, lat_count)),
            dma((lat_count * here,)),
            dma((5,)),
            dma((5,)),
        ],
        compiler_params=pltpu.CompilerParams(
            collective_id=0, has_side_effects=True, vmem_limit_bytes=67043328
        ),
    )(
        tokens, latents, gain_self[None], w_qkv_tok, w_o_tok, gain_read[None], w_kv_read,
        gain_lat[None], w_q_read, gain_glob[None], w_qkv_glob, w_o_glob, gain_write[None],
        w_q_write, gain_wlat[None], w_kv_write,
    )
    per_group = pl.BlockSpec((G, width), lambda g: (g, 0))
    per_lat = pl.BlockSpec((NLAT, lat_width), lambda g: (g, 0))
    return pl.pallas_call(
        back,
        grid=(groups,),
        out_shape=(
            jax.ShapeDtypeStruct(tokens.shape, BF16),
            jax.ShapeDtypeStruct(latents.shape, BF16),
        ),
        in_specs=[
            per_group,
            per_lat,
            per_group,
            pl.BlockSpec((NLAT, key_vals.shape[1]), lambda g: (g, 0)),
        ],
        out_specs=(per_group, per_lat),
    )(query, final, mid, key_vals)


def solution(mesh):
    rows = P(("dp", "lat"), None)
    whole = P()
    placed = (
        rows, rows, whole, whole, whole, whole, whole, whole, whole, whole,
        P(None, None, "lat"), P("lat", None), whole, whole, whole, whole,
    )
    return jax.shard_map(
        local, mesh=mesh, in_specs=placed, out_specs=(rows, rows), check_vma=False
    )
```

```python
import functools

import jax
import jax.numpy as jnp
from jax import lax
from jax.experimental import pallas as pl
from jax.experimental.pallas import tpu as pltpu
from jax.sharding import PartitionSpec as P

HEAD = 64
G = 256
NLAT = 16
WO_EIGHTHS = (1, 1, 2, 4)
FRONT_BYTES = 40 * 2**20
BACK_BYTES = 8 * 2**20
SCALE = HEAD ** (-0.5)
LOG2E = 1.4426950408889634
MESH = pl.DeviceIdType.MESH
F32 = jnp.float32
BF16 = jnp.bfloat16


def rms_norm(values, gain):
    floats = values.astype(F32)
    factor = lax.rsqrt(jnp.mean(floats * floats, axis=-1, keepdims=True) + 1e-06)
    return (floats * factor * gain).astype(BF16)


def dot(a, b):
    return jnp.dot(a, b, preferred_element_type=F32)


def dot_nt(a, b):
    return lax.dot_general(a, b, (((1,), (1,)), ((), ())), preferred_element_type=F32)


def dot_tn(a, b):
    return lax.dot_general(a, b, (((0,), (0,)), ((), ())), preferred_element_type=F32)


def spread_heads(query, count):
    lane_head = lax.broadcasted_iota(jnp.int32, query.shape, 1) // HEAD
    zero = jnp.zeros_like(query)
    return jnp.concatenate([jnp.where(lane_head == h, query, zero) for h in range(count)], axis=0)


def fold_heads(stacked, count):
    rows = stacked.shape[0] // count
    lane_head = lax.broadcasted_iota(jnp.int32, (rows, stacked.shape[1]), 1) // HEAD
    out = stacked[:rows]
    for h in range(1, count):
        out = jnp.where(lane_head == h, stacked[h * rows : (h + 1) * rows], out)
    return out


def softmax_mix(stacked, keys, values):
    scores = dot_nt(stacked, keys)
    peak = jnp.max(scores, axis=-1, keepdims=True)
    weights = jnp.exp2(scores - peak)
    total = jnp.sum(weights, axis=-1, keepdims=True)
    return dot(weights.astype(BF16), values) * (1.0 / total)


def kernel(
    dp_count, lat_count,
    tok_h, lat_h, g_self_h, w_qkv_h, w_o_h, g_read_h, w_kvr_h, g_lat_h, w_qr_h, g_glob_h,
    w_glob_h, w_og_h, g_write_h, w_qw_h, g_wlat_h, w_kvw_h,
    tok_out, lat_out, mid, lfin,
    tok, lat_in, g_self, g_read, g_lat, g_glob, g_write, g_wlat,
    w_qkv, w_o, w_kvr, w_qr, w_glob, w_og, w_qw, w_kvw,
    lmid, packed, mixed, read_q, normed_lat, outgoing, arrived, results, returned, mix,
    load_sem, l_send, l_recv, s_send, s_recv, t_send, t_recv, wo_send, wo_recv,
):
    width = tok_h.shape[1]
    lat_width = lat_h.shape[1]
    groups = tok_h.shape[0] // G
    lat_rows = lat_h.shape[0]
    last = groups - 1
    here = w_glob_h.shape[2] // HEAD
    slots = dp_count // here
    line = lat_count * NLAT
    lanes = 2 * HEAD
    dp = lax.axis_index("dp")
    lat = lax.axis_index("lat")
    head, slot = dp // slots, dp % slots
    core = lat % 2
    lat_y = (lat + 2) % 4
    partner = lat + 1 - 2 * core
    diag = (partner + 2) % 4
    upper = head * 2 // here

    def scope(name):
        return jax.named_scope(name)

    def each(low, high, body):
        def one(i, carry):
            body(i)
            return carry

        lax.fori_loop(low, high, one, 0)

    loads = []

    def load(src, dst):
        loads.append(pltpu.make_async_copy(src, dst, load_sem.at[len(loads)]))
        loads[-1].start()
        return loads[-1]

    def group_load(g):
        rows = pl.ds(g * G, G)
        return load(tok_h.at[rows], tok.at[rows])

    tok_load = [group_load(0)]
    gain_load = [load(g_self_h, g_self)]
    qkv_load = []
    for i in range(3):
        columns = pl.ds(i * width, width)
        qkv_load.append(load(w_qkv_h.at[:, columns], w_qkv.at[:, columns]))

    barrier = pltpu.get_barrier_semaphore()

    def greet(peer):
        pl.semaphore_signal(barrier, inc=1, device_id=peer, device_id_type=MESH)

    each(1, dp_count, lambda o: greet(((dp + o) % dp_count, lat)))
    for o in range(1, lat_count):
        each(0, here, lambda h: greet((h * slots + slot, (lat + o) % lat_count)))

    o_load = load(w_o_h, w_o)
    for src, dst in (
        (lat_h, lat_in), (g_lat_h, g_lat), (g_read_h, g_read), (g_glob_h, g_glob), (g_write_h, g_write),
        (g_wlat_h, g_wlat),
    ):
        gain_load.append(load(src, dst))
    qr_load = load(w_qr_h, w_qr)
    kvr_load = load(w_kvr_h, w_kvr)
    for g in range(1, groups):
        tok_load.append(group_load(g))
    later = []

    def remote(src, dst, send_sem, recv_sem, peer):
        return pltpu.make_async_remote_copy(
            src_ref=src, dst_ref=dst, send_sem=send_sem, recv_sem=recv_sem, device_id=peer,
            device_id_type=MESH,
        )

    def landed(ref, sem):
        pltpu.make_async_copy(ref, ref, sem).wait()

    wo_share = remote(w_og_h, w_og.at[lat], wo_send.at[0], wo_recv.at[0], (dp, partner))
    wo_cross, wo_relay = [], []
    wo_rows = w_og_h.shape[0] // 8
    wo_parts = len(WO_EIGHTHS)
    for i, count in enumerate(WO_EIGHTHS):
        part_rows = pl.ds(sum(WO_EIGHTHS[:i]) * wo_rows, count * wo_rows)
        there = w_og.at[lat_y, part_rows]
        wo_cross.append(
            remote(w_og_h.at[part_rows], w_og.at[lat, part_rows], wo_send.at[1 + i], wo_recv.at[1 + i], (dp, lat_y))
        )
        k = 1 + wo_parts + i
        wo_relay.append(remote(there, there, wo_send.at[k], wo_recv.at[k], (dp, partner)))

    def relay(i):
        wo_cross[i].wait_recv()
        wo_relay[i].start()


    def lat_copy(g, i):
        own = normed_lat.at[g, lat]
        peer = (diag, lat_y, partner)[i]
        return remote(own, own, l_send.at[g, i], l_recv.at[g, lat], (dp, peer))

    def far(i):
        return upper * i + (1 - upper) * (here - 1 - i)

    def to_head(g, h, j):
        rows = pl.ds(0, line)
        src, dst = outgoing.at[g, h], arrived.at[g, dp]
        if j is not None:
            src, dst = src.at[rows], dst.at[rows]
        spot = 0 if j is None else j
        peer = (h * slots + (slot + spot) % slots, lat)
        return remote(src, dst, s_send.at[g, h * slots + spot], s_recv.at[g, dp], peer)

    def spread(g):
        def one(i):
            h = far(i)

            @pl.when(h != head)
            def _():
                to_head(g, h, None).start()

            each(1, slots, lambda j: to_head(g, h, j).start())

        each(0, here, one)
        arrived[g, dp] = outgoing[g, head]

    def gathered(g):
        def one(h):
            @pl.when(h != head)
            def _():
                source = h * slots + slot
                landed(arrived.at[g, source], s_recv.at[g, source])

            def other(j):
                source = h * slots + (slot + j) % slots
                landed(arrived.at[g, source, pl.ds(0, line)], s_recv.at[g, source])

            each(1, slots, other)

        each(0, here, one)

    def low_lanes(rows):
        return lax.broadcasted_iota(jnp.int32, (rows, lanes), 1) < HEAD

    def swap(values):
        return pltpu.roll(values, HEAD, 1)

    def project(g):
        for i in range(1, lat_count):
            source = (lat + i) % lat_count
            landed(normed_lat.at[g, source], l_recv.at[g, source])
        rows = normed_lat[g].reshape(line, lat_width)
        queries = dot(rows, w_glob[0]) * (SCALE * LOG2E)
        keys = dot(rows, w_glob[1])
        values = dot(rows, w_glob[2])
        low, half = low_lanes(line), line // 2
        for h in range(0, here, 2):
            at = slice(h * HEAD, h * HEAD + lanes)
            k, v, q = keys[:, at], values[:, at], queries[:, at]
            outgoing[g, h, :line] = jnp.where(low, k, swap(v)).astype(BF16)
            outgoing[g, h + 1, :line] = jnp.where(low, swap(k), v).astype(BF16)
            q_swap = swap(q)
            outgoing[g, h, line:] = jnp.where(low[:half], q[:half], q_swap[half:]).astype(BF16)
            outgoing[g, h + 1, line:] = jnp.where(low[:half], q_swap[:half], q[half:]).astype(BF16)
        spread(g)

    def self_part(g):
        rows = pl.ds(g * G, G)
        tok_load[g].wait()
        if g == 0:
            gain_load[0].wait()
        group = tok[rows, :]
        normed = rms_norm(group, g_self[...])
        if g == 0:
            qkv_load[0].wait()
        packed[:, :width] = (dot(normed, w_qkv[:, :width]) * (SCALE * LOG2E)).astype(BF16)
        if g == 0:
            qkv_load[1].wait()
            qkv_load[2].wait()
            for src, dst in (
                (w_glob_h, w_glob), (w_qw_h, w_qw), (w_kvw_h, w_kvw), (w_og_h, w_og.at[lat]),
            ):
                later.append(load(src, dst))
        packed[:, width:] = dot(normed, w_qkv[:, width:]).astype(BF16)
        for pair in range(width // lanes):
            at = pair * lanes
            query = packed[:, at : at + lanes]
            keys = packed[:, width + at : width + at + lanes]
            values = packed[:, 2 * width + at : 2 * width + at + lanes]
            out = softmax_mix(spread_heads(query, 2), keys, values)
            mixed[:, at : at + lanes] = fold_heads(out, 2).astype(BF16)
        if g == 0:
            o_load.wait()
        mid[rows, :] = (group.astype(F32) + dot(mixed[...], w_o[...])).astype(BF16)

    quad = 4 * HEAD

    def read_queries():
        for copy in gain_load[1:]:
            copy.wait()
        qr_load.wait()
        query = dot(rms_norm(lat_in[...], g_lat[...]), w_qr[...])
        query = (query * (SCALE * LOG2E)).astype(BF16)
        kvr_load.wait()
        for at in range(0, lat_width, quad):
            keyed = dot_nt(spread_heads(query[:, at : at + quad], 4), w_kvr[:, at : at + quad]).astype(BF16)
            for h in range(4):
                for g in range(groups):
                    start = h * lat_rows + g * NLAT
                    at_head = at // HEAD + h
                    read_q[g, at_head * NLAT : (at_head + 1) * NLAT, :] = keyed[start : start + NLAT, :]

    def read_part(g):
        if g == 0:
            read_queries()
        rows = pl.ds(g * G, G)
        lrows = pl.ds(g * NLAT, NLAT)
        normed = rms_norm(mid[rows, :], g_read[...])
        scores = dot_nt(read_q[g], normed)
        peak = jnp.max(scores, axis=-1, keepdims=True)
        weights = jnp.exp2(scores - peak)
        inverse = 1.0 / jnp.sum(weights, axis=-1, keepdims=True)
        seen = (dot(weights.astype(BF16), normed) * inverse).astype(BF16)
        for at in range(0, lat_width, quad):
            start = at // HEAD * NLAT
            out = dot(seen[start : start + 4 * NLAT], w_kvr[:, lat_width + at : lat_width + at + quad])
            lmid[lrows, at : at + quad] = (
                lat_in[lrows, at : at + quad].astype(F32) + fold_heads(out, 4)
            ).astype(BF16)
        normed_lat[g, lat] = rms_norm(lmid[lrows, :], g_glob[...])
        for i in range(3):
            lat_copy(g, i).start()

    for g in range(groups):
        with scope(f"self{g}"):
            self_part(g)
        if g == 0:
            with scope("bar"):
                pl.semaphore_wait(barrier, dp_count - 1 + here * (lat_count - 1))
            wo_share.start()
            wo_cross[0].start()
        with scope(f"read{g}"):
            read_part(g)
        if g < last:
            wo_cross[1 + g].start()
        if g == 1:
            later[0].wait()
        if 1 <= g < last:
            with scope(f"proj{g - 1}"):
                project(g - 1)
    wo_cross[groups].start()
    with scope("projM"):
        project(last - 1)
    with scope("rel"):
        relay(0)
        relay(1)
    later[1].wait()
    with scope("wq"):
        for g in range(groups):
            rows = pl.ds(g * G, G)
            query = dot(rms_norm(mid[rows, :], g_write[...]), w_qw[...]).astype(BF16)
            tok_out[rows, :] = query * jnp.asarray(SCALE, BF16)
    with scope("projL"):
        project(last)
    later[2].wait()
    later[3].wait()
    for g in range(last):
        with scope(f"gath{g}"):
            gathered(g)
    with scope("rel2"):
        relay(2)
    with scope("gathL"):
        gathered(last)

    def queries_of(c):
        parts = []
        for g in range(groups):
            pack = arrived[g, c * slots + slot, line:].astype(F32)
            low = low_lanes(line // 2)
            parts.append(jnp.where(low, pack, 0.0))
            parts.append(jnp.where(low, swap(pack), 0.0))
        return jnp.concatenate(parts, axis=0).astype(BF16)

    def attend(c):
        query = queries_of(c)
        if dp_count * line * groups <= 2048:
            key_vals = jnp.concatenate(
                [arrived[g, d, :line] for g in range(groups) for d in range(dp_count)], axis=0
            )
            return softmax_mix(query, key_vals, key_vals)

        def fold(i, carry):
            peak, total, acc = carry
            for g in range(groups):
                key_vals = arrived[g, i, :line]
                scores = dot_nt(query, key_vals)
                new = jnp.maximum(peak, jnp.max(scores, axis=-1, keepdims=True))
                weights = jnp.exp2(scores - new)
                keep = jnp.exp2(peak - new)
                total = total * keep + jnp.sum(weights, axis=-1, keepdims=True)
                acc = acc * keep + dot(weights.astype(BF16), key_vals)
                peak = new
            return peak, total, acc

        rows = query.shape[0]
        first = (
            jnp.full((rows, 1), -jnp.inf, F32), jnp.zeros((rows, 1), F32), jnp.zeros((rows, lanes), F32)
        )
        _, total, acc = lax.fori_loop(0, dp_count, fold, first)
        return acc * (1.0 / total)

    mine = lat * here + head

    def result_copy(c, i):
        to = (lat + i) % lat_count
        return remote(
            results.at[c, to], returned.at[mine], t_send.at[c, to], t_recv.at[mine], (c * slots + slot, to)
        )

    with scope("att"):
        for i in range(here):
            c = (head + 1 + i) % here
            out = attend(c)
            low = low_lanes(line)
            for k in range(0, groups, 2):
                even = out[k * line : (k + 1) * line]
                odd = out[(k + 1) * line : (k + 2) * line] if k + 1 < groups else even
                pair = jnp.where(low, swap(even), odd).astype(BF16)
                for l in range(lat_count):
                    results[c, l, k // 2 * NLAT : (k // 2 + 1) * NLAT] = pair[l * NLAT : (l + 1) * NLAT]
            for l in range(1, lat_count):
                result_copy(c, l).start()
            if i < here - 1:
                result_copy(c, 0).start()
            else:
                returned[mine] = results[c, lat]
    with scope("wo1"):
        relay(3)
    with scope("retw"):
        def back_from(h):
            @pl.when(h != mine)
            def _():
                landed(returned.at[h], t_recv.at[h])

        each(0, lat_count * here, back_from)
        wo_share.wait_recv()
        for copy in wo_relay:
            copy.wait_recv()
    with scope("final"):
        low = low_lanes(NLAT)
        for p in range(lat_count * here // 2):
            a, b = returned[2 * p].astype(F32), returned[2 * p + 1].astype(F32)
            a_swap, b_swap = swap(a), swap(b)
            for g in range(groups):
                at = slice(g // 2 * NLAT, (g // 2 + 1) * NLAT)
                both = jnp.where(low, a[at], b_swap[at]) if g % 2 == 0 else jnp.where(low, a_swap[at], b[at])
                mix[g * NLAT : (g + 1) * NLAT, p * lanes : (p + 1) * lanes] = both.astype(BF16)
        total = dot(mix[...], w_og[...].reshape(lat_width, lat_width))
        final = (lmid[...].astype(F32) + total).astype(BF16)
        lat_out[...] = final
        lfin[...] = dot(rms_norm(final, g_wlat[...]), w_kvw[...]).astype(BF16)

    with scope("drain"):
        for copy in [wo_share] + wo_cross + wo_relay:
            copy.wait_send()
        for g in range(groups):
            for i in range(3):
                lat_copy(g, i).wait_send()

            def sent(h):
                @pl.when(h != head)
                def _():
                    to_head(g, h, None).wait_send()

                each(1, slots, lambda j: to_head(g, h, j).wait_send())

            each(0, here, sent)

        def answered(c):
            for l in range(1, lat_count):
                result_copy(c, l).wait_send()

            @pl.when(c != head)
            def _():
                result_copy(c, 0).wait_send()

        each(0, here, answered)


def back(query, final, mid, key_vals, tok_h, lat_h, tok_out, sem):
    width = query.shape[1]
    heads = width // HEAD
    groups = query.shape[0] // G
    copies = [pltpu.make_async_copy(final, lat_h, sem.at[groups])]
    copies[0].start()
    for g in range(groups):
        rows, lrows = pl.ds(g * G, G), pl.ds(g * NLAT, NLAT)
        keys = spread_heads(key_vals[lrows, :width], heads)
        values = spread_heads(key_vals[lrows, width:], heads)
        scores = dot_nt(keys, query[rows, :]).reshape(heads, NLAT, G)
        peak = jnp.max(scores, axis=1, keepdims=True)
        weights = jnp.exp(scores - peak)
        weights = weights * (1.0 / jnp.sum(weights, axis=1, keepdims=True))
        written = dot_tn(weights.reshape(heads * NLAT, G).astype(BF16), values)
        tok_out[rows, :] = (mid[rows, :].astype(F32) + written).astype(BF16)
        copies.append(pltpu.make_async_copy(tok_out.at[rows], tok_h.at[rows], sem.at[g]))
        copies[-1].start()
    for copy in copies:
        copy.wait()


def local(
    tokens, latents, gain_self, w_qkv_tok, w_o_tok, gain_read, w_kv_read, gain_lat, w_q_read,
    gain_glob, w_qkv_glob, w_o_glob, gain_write, w_q_write, gain_wlat, w_kv_write,
):
    dp_count = lax.axis_size("dp")
    lat_count = lax.axis_size("lat")
    rows, width = tokens.shape
    lat_rows, lat_width = latents.shape
    groups = rows // G
    here = w_qkv_glob.shape[2] // HEAD
    line = lat_count * NLAT
    packs = (groups + 1) // 2
    vmem = pl.BlockSpec(memory_space=pltpu.VMEM)
    hbm = pl.BlockSpec(memory_space=pltpu.HBM)
    dma = pltpu.SemaphoreType.DMA
    query, final, mid, key_vals = pl.pallas_call(
        functools.partial(kernel, dp_count, lat_count),
        out_shape=(
            jax.ShapeDtypeStruct(tokens.shape, BF16),
            jax.ShapeDtypeStruct(latents.shape, BF16),
            jax.ShapeDtypeStruct(tokens.shape, BF16),
            jax.ShapeDtypeStruct((lat_rows, w_kv_write.shape[1]), BF16),
        ),
        in_specs=[hbm] * 16,
        out_specs=(vmem,) * 4,
        scratch_shapes=[
            pltpu.VMEM(tokens.shape, BF16),
            pltpu.VMEM(latents.shape, BF16),
            pltpu.VMEM((1, width), F32),
            pltpu.VMEM((1, width), F32),
            pltpu.VMEM((1, lat_width), F32),
            pltpu.VMEM((1, lat_width), F32),
            pltpu.VMEM((1, width), F32),
            pltpu.VMEM((1, lat_width), F32),
            pltpu.VMEM(w_qkv_tok.shape, BF16),
            pltpu.VMEM(w_o_tok.shape, BF16),
            pltpu.VMEM(w_kv_read.shape, BF16),
            pltpu.VMEM(w_q_read.shape, BF16),
            pltpu.VMEM(w_qkv_glob.shape, BF16),
            pltpu.VMEM((lat_count,) + w_o_glob.shape, BF16),
            pltpu.VMEM(w_q_write.shape, BF16),
            pltpu.VMEM(w_kv_write.shape, BF16),
            pltpu.VMEM(latents.shape, BF16),
            pltpu.VMEM((G, w_qkv_tok.shape[1]), BF16),
            pltpu.VMEM((G, width), BF16),
            pltpu.VMEM((groups, lat_width // HEAD * NLAT, width), BF16),
            pltpu.VMEM((groups, lat_count, NLAT, lat_width), BF16),
            pltpu.VMEM((groups, here, line * 3 // 2, 2 * HEAD), BF16),
            pltpu.VMEM((groups, dp_count, line * 3 // 2, 2 * HEAD), BF16),
            pltpu.VMEM((here, lat_count, packs * NLAT, 2 * HEAD), BF16),
            pltpu.VMEM((lat_count * here, packs * NLAT, 2 * HEAD), BF16),
            pltpu.VMEM(latents.shape, BF16),
            dma((17 + groups,)),
            dma((groups, 3)),
            dma((groups, lat_count)),
            dma((groups, dp_count)),
            dma((groups, dp_count)),
            dma((here, lat_count)),
            dma((lat_count * here,)),
            dma((1 + 2 * len(WO_EIGHTHS),)),
            dma((1 + 2 * len(WO_EIGHTHS),)),
        ],
        compiler_params=pltpu.CompilerParams(
            collective_id=0, has_side_effects=True, vmem_limit_bytes=FRONT_BYTES
        ),
    )(
        *(
            pltpu.with_memory_space_constraint(array, pltpu.HBM)
            for array in (
                tokens, latents, gain_self[None], w_qkv_tok, w_o_tok, gain_read[None], w_kv_read,
                gain_lat[None], w_q_read, gain_glob[None], w_qkv_glob, w_o_glob, gain_write[None],
                w_q_write, gain_wlat[None], w_kv_write,
            )
        )
    )
    return pl.pallas_call(
        back,
        out_shape=(
            jax.ShapeDtypeStruct(tokens.shape, BF16),
            jax.ShapeDtypeStruct(latents.shape, BF16),
        ),
        in_specs=[vmem] * 4,
        out_specs=(hbm, hbm),
        scratch_shapes=[pltpu.VMEM(tokens.shape, BF16), dma((groups + 1,))],
        compiler_params=pltpu.CompilerParams(vmem_limit_bytes=BACK_BYTES),
    )(query, final, mid, key_vals)


def solution(mesh):
    rows = P(("dp", "lat"), None)
    whole = P()
    placed = (
        rows, rows, whole, whole, whole, whole, whole, whole, whole, whole,
        P(None, None, "lat"), P("lat", None), whole, whole, whole, whole,
    )
    return jax.shard_map(
        local, mesh=mesh, in_specs=placed, out_specs=(rows, rows), check_vma=False
    )
```

```python
import functools

import jax
import jax.numpy as jnp
from jax import lax
from jax.experimental import pallas as pl
from jax.experimental.pallas import tpu as pltpu
from jax.sharding import PartitionSpec as P

HEAD = 64
G = 256
NLAT = 16
WO_EIGHTHS = (1, 1, 2, 4)
FRONT_BYTES = 40 * 2**20
BACK_BYTES = 8 * 2**20
SCALE = HEAD ** (-0.5)
LOG2E = 1.4426950408889634
MESH = pl.DeviceIdType.MESH
F32 = jnp.float32
BF16 = jnp.bfloat16


def rms_norm(values, gain):
    floats = values.astype(F32)
    factor = lax.rsqrt(jnp.mean(floats * floats, axis=-1, keepdims=True) + 1e-06)
    return (floats * factor * gain).astype(BF16)


def dot(a, b):
    return jnp.dot(a, b, preferred_element_type=F32)


def dot_nt(a, b):
    return lax.dot_general(a, b, (((1,), (1,)), ((), ())), preferred_element_type=F32)


def dot_tn(a, b):
    return lax.dot_general(a, b, (((0,), (0,)), ((), ())), preferred_element_type=F32)


def spread_heads(query, count):
    lane_head = lax.broadcasted_iota(jnp.int32, query.shape, 1) // HEAD
    zero = jnp.zeros_like(query)
    return jnp.concatenate([jnp.where(lane_head == h, query, zero) for h in range(count)], axis=0)


def fold_heads(stacked, count):
    rows = stacked.shape[0] // count
    lane_head = lax.broadcasted_iota(jnp.int32, (rows, stacked.shape[1]), 1) // HEAD
    out = stacked[:rows]
    for h in range(1, count):
        out = jnp.where(lane_head == h, stacked[h * rows : (h + 1) * rows], out)
    return out


def softmax_mix(stacked, keys, values):
    scores = dot_nt(stacked, keys)
    peak = jnp.max(scores, axis=-1, keepdims=True)
    weights = jnp.exp2(scores - peak)
    total = jnp.sum(weights, axis=-1, keepdims=True)
    return dot(weights.astype(BF16), values) * (1.0 / total)


def kernel(
    dp_count, lat_count,
    tok_h, lat_h, g_self_h, w_qkv_h, w_o_h, g_read_h, w_kvr_h, g_lat_h, w_qr_h, g_glob_h,
    w_glob_h, w_og_h, g_write_h, w_qw_h, g_wlat_h, w_kvw_h,
    tok_out, lat_out, mid, lfin,
    tok, lat_in, g_self, g_narrow, g_wide,
    w_qkv, w_o, w_kvr, w_qr, w_glob, w_og, w_qw, w_kvw,
    lmid, packed, mixed, read_q, normed_lat, outgoing, arrived, results, returned,
    early_q, early_top, early_norm, early_acc,
    load_sem, l_send, l_recv, s_send, s_recv, t_send, t_recv, wo_send, wo_recv,
):
    width = tok_h.shape[1]
    lat_width = lat_h.shape[1]
    groups = tok_h.shape[0] // G
    lat_rows = lat_h.shape[0]
    last = groups - 1
    here = w_glob_h.shape[2] // HEAD
    slots = dp_count // here
    line = lat_count * NLAT
    lanes = 2 * HEAD
    dp = lax.axis_index("dp")
    lat = lax.axis_index("lat")
    head, slot = dp // slots, dp % slots
    core = lat % 2
    lat_y = (lat + 2) % 4
    partner = lat + 1 - 2 * core
    diag = (partner + 2) % 4
    upper = head * 2 // here
    g_read, g_write = g_narrow.at[0], g_narrow.at[1]
    g_lat, g_glob, g_wlat = g_wide.at[0], g_wide.at[1], g_wide.at[2]

    def scope(name):
        return jax.named_scope(name)

    def each(low, high, body):
        def one(i, carry):
            body(i)
            return carry

        lax.fori_loop(low, high, one, 0)

    loads = []

    def load(src, dst):
        loads.append(pltpu.make_async_copy(src, dst, load_sem.at[len(loads)]))
        loads[-1].start()
        return loads[-1]

    def load_all(sources, dst):
        sem = load_sem.at[len(loads)]
        for i, src in enumerate(sources):
            pltpu.make_async_copy(src, dst.at[i], sem).start()
        loads.append(pltpu.make_async_copy(dst, dst, sem))
        return loads[-1]

    def group_load(g):
        rows = pl.ds(g * G, G)
        return load(tok_h.at[rows], tok.at[rows])

    tok_load = [group_load(0)]
    gain_load = [load(g_self_h, g_self)]
    qkv_load = []
    for columns in (pl.ds(0, width), pl.ds(width, 2 * width)):
        qkv_load.append(load(w_qkv_h.at[:, columns], w_qkv.at[:, columns]))

    barrier = pltpu.get_barrier_semaphore()

    def greet(peer):
        pl.semaphore_signal(barrier, inc=1, device_id=peer, device_id_type=MESH)

    each(1, dp_count, lambda o: greet(((dp + o) % dp_count, lat)))
    for o in range(1, lat_count):
        each(0, here, lambda h: greet((h * slots + slot, (lat + o) % lat_count)))

    o_load = load(w_o_h, w_o)
    gain_load.append(load(lat_h, lat_in))
    gain_load.append(load_all((g_lat_h, g_glob_h, g_wlat_h), g_wide))
    gain_load.append(load_all((g_read_h, g_write_h), g_narrow))
    qr_load = load(w_qr_h, w_qr)
    kvr_load = load(w_kvr_h, w_kvr)
    for g in range(1, groups):
        tok_load.append(group_load(g))
    later = []

    def remote(src, dst, send_sem, recv_sem, peer):
        return pltpu.make_async_remote_copy(
            src_ref=src, dst_ref=dst, send_sem=send_sem, recv_sem=recv_sem, device_id=peer,
            device_id_type=MESH,
        )

    def landed(ref, sem):
        pltpu.make_async_copy(ref, ref, sem).wait()

    wo_share = remote(w_og_h, w_og.at[lat], wo_send, wo_recv.at[0], (dp, partner))
    wo_cross, wo_relay = [], []
    wo_rows = w_og_h.shape[0] // 8
    for i, count in enumerate(WO_EIGHTHS):
        part_rows = pl.ds(sum(WO_EIGHTHS[:i]) * wo_rows, count * wo_rows)
        there = w_og.at[lat_y, part_rows]
        wo_cross.append(
            remote(w_og_h.at[part_rows], w_og.at[lat, part_rows], wo_send, wo_recv.at[2 + i], (dp, lat_y))
        )
        wo_relay.append(remote(there, there, wo_send, wo_recv.at[1], (dp, partner)))

    def relay(i):
        wo_cross[i].wait_recv()
        wo_relay[i].start()


    def lat_copy(g, i):
        own = normed_lat.at[g, lat]
        peer = (diag, lat_y, partner)[i]
        return remote(own, own, l_send, l_recv.at[g], (dp, peer))

    def far(i):
        return upper * i + (1 - upper) * (here - 1 - i)

    def to_head(g, h, j):
        src, dst = outgoing.at[g, h], arrived.at[g, dp]
        if j is None:
            peer = (h * slots + slot, lat)
            return remote(src, dst, s_send.at[0], s_recv.at[g, 0], peer)
        rows = pl.ds(0, line)
        peer = (h * slots + (slot + j) % slots, lat)
        return remote(src.at[rows], dst.at[rows], s_send.at[1], s_recv.at[g, 1], peer)

    full, most = pl.ds(0, here - 1), pl.ds(0, here * (slots - 1))

    def spread(g):
        def one(i):
            h = far(i)

            @pl.when(h != head)
            def _():
                to_head(g, h, None).start()

            each(1, slots, lambda j: to_head(g, h, j).start())

        each(0, here, one)
        arrived[g, dp] = outgoing[g, head]

    def gathered(g):
        landed(arrived.at[g, full], s_recv.at[g, 0])
        if slots > 1:
            landed(arrived.at[g, most, pl.ds(0, line)], s_recv.at[g, 1])

    def low_lanes(rows):
        return lax.broadcasted_iota(jnp.int32, (rows, lanes), 1) < HEAD

    def swap(values):
        return pltpu.roll(values, HEAD, 1)

    def project(g):
        landed(normed_lat.at[g, pl.ds(0, lat_count - 1)], l_recv.at[g])
        rows = normed_lat[g].reshape(line, lat_width)
        queries = dot(rows, w_glob[0]) * (SCALE * LOG2E)
        keys = dot(rows, w_glob[1])
        values = dot(rows, w_glob[2])
        low, half = low_lanes(line), line // 2
        for h in range(0, here, 2):
            at = slice(h * HEAD, h * HEAD + lanes)
            k, v, q = keys[:, at], values[:, at], queries[:, at]
            outgoing[g, h, :line] = jnp.where(low, k, swap(v)).astype(BF16)
            outgoing[g, h + 1, :line] = jnp.where(low, swap(k), v).astype(BF16)
            q_swap = swap(q)
            outgoing[g, h, line:] = jnp.where(low[:half], q[:half], q_swap[half:]).astype(BF16)
            outgoing[g, h + 1, line:] = jnp.where(low[:half], q_swap[:half], q[half:]).astype(BF16)
        spread(g)

    def self_part(g):
        rows = pl.ds(g * G, G)
        tok_load[g].wait()
        if g == 0:
            gain_load[0].wait()
        group = tok[rows, :]
        normed = rms_norm(group, g_self[...])
        if g == 0:
            qkv_load[0].wait()
        packed[:, :width] = (dot(normed, w_qkv[:, :width]) * (SCALE * LOG2E)).astype(BF16)
        if g == 0:
            qkv_load[1].wait()
            for src, dst in (
                (w_glob_h, w_glob), (w_qw_h, w_qw), (w_kvw_h, w_kvw), (w_og_h, w_og.at[lat]),
            ):
                later.append(load(src, dst))
        packed[:, width:] = dot(normed, w_qkv[:, width:]).astype(BF16)
        for pair in range(width // lanes):
            at = pair * lanes
            query = packed[:, at : at + lanes]
            keys = packed[:, width + at : width + at + lanes]
            values = packed[:, 2 * width + at : 2 * width + at + lanes]
            out = softmax_mix(spread_heads(query, 2), keys, values)
            mixed[:, at : at + lanes] = fold_heads(out, 2).astype(BF16)
        if g == 0:
            o_load.wait()
        mid[rows, :] = (group.astype(F32) + dot(mixed[...], w_o[...])).astype(BF16)

    quad = 4 * HEAD

    def read_queries():
        for copy in gain_load[1:]:
            copy.wait()
        qr_load.wait()
        query = dot(rms_norm(lat_in[...], g_lat[...]), w_qr[...])
        query = (query * (SCALE * LOG2E)).astype(BF16)
        kvr_load.wait()
        for at in range(0, lat_width, quad):
            keyed = dot_nt(spread_heads(query[:, at : at + quad], 4), w_kvr[:, at : at + quad]).astype(BF16)
            for h in range(4):
                for g in range(groups):
                    start = h * lat_rows + g * NLAT
                    at_head = at // HEAD + h
                    read_q[g, at_head * NLAT : (at_head + 1) * NLAT, :] = keyed[start : start + NLAT, :]

    def read_part(g):
        if g == 0:
            read_queries()
        rows = pl.ds(g * G, G)
        lrows = pl.ds(g * NLAT, NLAT)
        normed = rms_norm(mid[rows, :], g_read[...])
        scores = dot_nt(read_q[g], normed)
        peak = jnp.max(scores, axis=-1, keepdims=True)
        weights = jnp.exp2(scores - peak)
        inverse = 1.0 / jnp.sum(weights, axis=-1, keepdims=True)
        seen = (dot(weights.astype(BF16), normed) * inverse).astype(BF16)
        for at in range(0, lat_width, quad):
            start = at // HEAD * NLAT
            out = dot(seen[start : start + 4 * NLAT], w_kvr[:, lat_width + at : lat_width + at + quad])
            lmid[lrows, at : at + quad] = (
                lat_in[lrows, at : at + quad].astype(F32) + fold_heads(out, 4)
            ).astype(BF16)
        normed_lat[g, lat] = rms_norm(lmid[lrows, :], g_glob[...])
        for i in range(3):
            lat_copy(g, i).start()

    for g in range(groups):
        with scope(f"self{g}"):
            self_part(g)
        if g == 0:
            with scope("bar"):
                pl.semaphore_wait(barrier, dp_count - 1 + here * (lat_count - 1))
            wo_share.start()
            wo_cross[0].start()
        with scope(f"read{g}"):
            read_part(g)
        if g < last:
            wo_cross[1 + g].start()
        if g == 1:
            later[0].wait()
        if 1 <= g < last:
            with scope(f"proj{g - 1}"):
                project(g - 1)
    wo_cross[groups].start()
    with scope("projM"):
        project(last - 1)
    with scope("rel"):
        relay(0)
        relay(1)
    later[1].wait()
    with scope("wq"):
        for g in range(groups):
            rows = pl.ds(g * G, G)
            query = dot(rms_norm(mid[rows, :], g_write[...]), w_qw[...]).astype(BF16)
            tok_out[rows, :] = query * jnp.asarray(SCALE, BF16)
    with scope("projL"):
        project(last)
    later[2].wait()
    later[3].wait()
    def query_of(c, g):
        pack = arrived[g, c * slots + slot, line:].astype(F32)
        low = low_lanes(line // 2)
        both = (jnp.where(low, pack, 0.0), jnp.where(low, swap(pack), 0.0))
        return jnp.concatenate(both, axis=0).astype(BF16)

    def key_vals(low, high):
        return jnp.concatenate(
            [arrived[g, d, :line] for g in range(low, high) for d in range(dp_count)], axis=0
        )

    own_at = upper * head + (1 - upper) * (here - 1 - head)
    order = [far(i + (i + here - own_at) // here) for i in range(here - 1)] + [head]
    wide = dp_count * line * groups <= 2048
    batches = [order[i : i + here // 2] for i in range(0, here, here // 2)]
    early_rows = last * line

    def attend_early(b):
        query = jnp.concatenate([query_of(c, g) for c in batches[b] for g in range(last)], axis=0)
        keys = key_vals(0, last)
        scores = dot_nt(query, keys)
        peak = jnp.max(scores, axis=-1, keepdims=True)
        weights = jnp.exp2(scores - peak)
        early_q[b] = query
        early_top[b] = peak
        early_norm[b] = jnp.sum(weights, axis=-1, keepdims=True)
        early_acc[b] = dot(weights.astype(BF16), keys)

    def attend_late(b):
        keys = key_vals(last, groups)
        scores = dot_nt(early_q[b], keys)
        peak = jnp.maximum(early_top[b], jnp.max(scores, axis=-1, keepdims=True))
        weights = jnp.exp2(scores - peak)
        keep = jnp.exp2(early_top[b] - peak)
        total = early_norm[b] * keep + jnp.sum(weights, axis=-1, keepdims=True)
        first = (early_acc[b] * keep + dot(weights.astype(BF16), keys)) * (1.0 / total)
        query = jnp.concatenate([query_of(c, last) for c in batches[b]], axis=0)
        keys = key_vals(0, groups)
        second = softmax_mix(query, keys, keys)
        parts = []
        for i in range(len(batches[b])):
            parts.append([first[i * early_rows + g * line : i * early_rows + (g + 1) * line] for g in range(last)])
            parts[-1].append(second[i * line : (i + 1) * line])
        return parts

    def attend_long(c):
        query = jnp.concatenate([query_of(c, g) for g in range(groups)], axis=0)

        def fold(i, carry):
            peak, total, acc = carry
            for g in range(groups):
                keys = arrived[g, i, :line]
                scores = dot_nt(query, keys)
                new = jnp.maximum(peak, jnp.max(scores, axis=-1, keepdims=True))
                weights = jnp.exp2(scores - new)
                keep = jnp.exp2(peak - new)
                total = total * keep + jnp.sum(weights, axis=-1, keepdims=True)
                acc = acc * keep + dot(weights.astype(BF16), keys)
                peak = new
            return peak, total, acc

        rows = query.shape[0]
        start = (
            jnp.full((rows, 1), -jnp.inf, F32), jnp.zeros((rows, 1), F32), jnp.zeros((rows, lanes), F32)
        )
        _, total, acc = lax.fori_loop(0, dp_count, fold, start)
        out = acc * (1.0 / total)
        return [out[g * line : (g + 1) * line] for g in range(groups)]

    def result_copy(c, i):
        to = (lat + i) % lat_count
        return remote(
            results.at[c, to], returned.at[head, lat], t_send, t_recv.at[head], (c * slots + slot, to)
        )

    def answer(c, parts, own):
        low = low_lanes(line)
        for k in range(0, groups, 2):
            even = parts[k]
            odd = parts[k + 1] if k + 1 < groups else even
            pair = jnp.where(low, swap(even), odd).astype(BF16)
            for l in range(lat_count):
                results[c, l, k // 2 * NLAT : (k // 2 + 1) * NLAT] = pair[l * NLAT : (l + 1) * NLAT]
        for l in range(1, lat_count):
            result_copy(c, l).start()
        if own:
            returned[head, lat] = results[c, lat]
        else:
            result_copy(c, 0).start()

    for g in range(last):
        with scope(f"gath{g}"):
            gathered(g)
    if wide:
        with scope("attE"):
            for b in range(len(batches)):
                attend_early(b)
    with scope("rel2"):
        relay(2)
    with scope("gathL"):
        gathered(last)
    with scope("att"):
        if wide:
            for b, batch in enumerate(batches):
                for c, parts in zip(batch, attend_late(b)):
                    answer(c, parts, c is head)
        else:
            for c in order:
                answer(c, attend_long(c), c is head)
    with scope("wo1"):
        relay(3)
        wo_share.wait_recv()
        landed(w_og.at[0], wo_recv.at[1])
    total = lmid[...].astype(F32)
    low = low_lanes(NLAT)
    for k, h in enumerate([head] + order[-2::-1]):
        with scope("retw"):
            landed(returned.at[h, pl.ds(0, lat_count - 1 if k == 0 else lat_count)], t_recv.at[h])
        tiles = []
        for p in range(0, lat_count, 2):
            a, b = returned[h, p].astype(F32), returned[h, p + 1].astype(F32)
            a_swap, b_swap = swap(a), swap(b)
            column = []
            for g in range(groups):
                at = slice(g // 2 * NLAT, (g // 2 + 1) * NLAT)
                column.append(
                    jnp.where(low, a[at], b_swap[at]) if g % 2 == 0 else jnp.where(low, a_swap[at], b[at])
                )
            tiles.append(jnp.concatenate(column, axis=0))
        rows = pl.ds(pl.multiple_of(h * HEAD, HEAD), HEAD)
        weights = jnp.concatenate([w_og[l, rows, :] for l in range(lat_count)], axis=0)
        total = total + dot(jnp.concatenate(tiles, axis=1).astype(BF16), weights)
    with scope("final"):
        final = total.astype(BF16)
        lat_out[...] = final
        lfin[...] = dot(rms_norm(final, g_wlat[...]), w_kvw[...]).astype(BF16)

    with scope("drain"):
        landed(w_og.at[pl.ds(0, 3)], wo_send)
        landed(normed_lat.at[:, pl.ds(0, 3)], l_send)
        landed(outgoing.at[:, full], s_send.at[0])
        if slots > 1:
            landed(arrived.at[:, most, pl.ds(0, line)], s_send.at[1])
        landed(returned.at[pl.ds(0, here - 1)], t_send)
        landed(returned.at[0, pl.ds(0, lat_count - 1)], t_send)


def back(query, final, mid, key_vals, tok_h, lat_h, tok_out, sem):
    width = query.shape[1]
    heads = width // HEAD
    groups = query.shape[0] // G
    copies = [pltpu.make_async_copy(final, lat_h, sem.at[groups])]
    copies[0].start()
    for g in range(groups):
        rows, lrows = pl.ds(g * G, G), pl.ds(g * NLAT, NLAT)
        keys = spread_heads(key_vals[lrows, :width], heads)
        values = spread_heads(key_vals[lrows, width:], heads)
        scores = dot_nt(keys, query[rows, :]).reshape(heads, NLAT, G)
        peak = jnp.max(scores, axis=1, keepdims=True)
        weights = jnp.exp(scores - peak)
        weights = weights * (1.0 / jnp.sum(weights, axis=1, keepdims=True))
        written = dot_tn(weights.reshape(heads * NLAT, G).astype(BF16), values)
        tok_out[rows, :] = (mid[rows, :].astype(F32) + written).astype(BF16)
        copies.append(pltpu.make_async_copy(tok_out.at[rows], tok_h.at[rows], sem.at[g]))
        copies[-1].start()
    for copy in copies:
        copy.wait()


def local(
    tokens, latents, gain_self, w_qkv_tok, w_o_tok, gain_read, w_kv_read, gain_lat, w_q_read,
    gain_glob, w_qkv_glob, w_o_glob, gain_write, w_q_write, gain_wlat, w_kv_write,
):
    dp_count = lax.axis_size("dp")
    lat_count = lax.axis_size("lat")
    rows, width = tokens.shape
    lat_rows, lat_width = latents.shape
    groups = rows // G
    here = w_qkv_glob.shape[2] // HEAD
    line = lat_count * NLAT
    packs = (groups + 1) // 2
    vmem = pl.BlockSpec(memory_space=pltpu.VMEM)
    hbm = pl.BlockSpec(memory_space=pltpu.HBM)
    dma = pltpu.SemaphoreType.DMA
    query, final, mid, key_vals = pl.pallas_call(
        functools.partial(kernel, dp_count, lat_count),
        out_shape=(
            jax.ShapeDtypeStruct(tokens.shape, BF16),
            jax.ShapeDtypeStruct(latents.shape, BF16),
            jax.ShapeDtypeStruct(tokens.shape, BF16),
            jax.ShapeDtypeStruct((lat_rows, w_kv_write.shape[1]), BF16),
        ),
        in_specs=[hbm] * 16,
        out_specs=(vmem,) * 4,
        scratch_shapes=[
            pltpu.VMEM(tokens.shape, BF16),
            pltpu.VMEM(latents.shape, BF16),
            pltpu.VMEM((1, width), F32),
            pltpu.VMEM((2, 1, width), F32),
            pltpu.VMEM((3, 1, lat_width), F32),
            pltpu.VMEM(w_qkv_tok.shape, BF16),
            pltpu.VMEM(w_o_tok.shape, BF16),
            pltpu.VMEM(w_kv_read.shape, BF16),
            pltpu.VMEM(w_q_read.shape, BF16),
            pltpu.VMEM(w_qkv_glob.shape, BF16),
            pltpu.VMEM((lat_count,) + w_o_glob.shape, BF16),
            pltpu.VMEM(w_q_write.shape, BF16),
            pltpu.VMEM(w_kv_write.shape, BF16),
            pltpu.VMEM(latents.shape, BF16),
            pltpu.VMEM((G, w_qkv_tok.shape[1]), BF16),
            pltpu.VMEM((G, width), BF16),
            pltpu.VMEM((groups, lat_width // HEAD * NLAT, width), BF16),
            pltpu.VMEM((groups, lat_count, NLAT, lat_width), BF16),
            pltpu.VMEM((groups, here, line * 3 // 2, 2 * HEAD), BF16),
            pltpu.VMEM((groups, dp_count, line * 3 // 2, 2 * HEAD), BF16),
            pltpu.VMEM((here, lat_count, packs * NLAT, 2 * HEAD), BF16),
            pltpu.VMEM((here, lat_count, packs * NLAT, 2 * HEAD), BF16),
            pltpu.VMEM((2, here // 2 * (groups - 1) * line, 2 * HEAD), BF16),
            pltpu.VMEM((2, here // 2 * (groups - 1) * line, 1), F32),
            pltpu.VMEM((2, here // 2 * (groups - 1) * line, 1), F32),
            pltpu.VMEM((2, here // 2 * (groups - 1) * line, 2 * HEAD), F32),
            dma((13 + groups,)),
            dma,
            dma((groups,)),
            dma((2,)),
            dma((groups, 2)),
            dma,
            dma((here,)),
            dma,
            dma((2 + len(WO_EIGHTHS),)),
        ],
        compiler_params=pltpu.CompilerParams(
            collective_id=0, has_side_effects=True, vmem_limit_bytes=FRONT_BYTES
        ),
    )(
        *(
            pltpu.with_memory_space_constraint(array, pltpu.HBM)
            for array in (
                tokens, latents, gain_self[None], w_qkv_tok, w_o_tok, gain_read[None], w_kv_read,
                gain_lat[None], w_q_read, gain_glob[None], w_qkv_glob, w_o_glob, gain_write[None],
                w_q_write, gain_wlat[None], w_kv_write,
            )
        )
    )
    return pl.pallas_call(
        back,
        out_shape=(
            jax.ShapeDtypeStruct(tokens.shape, BF16),
            jax.ShapeDtypeStruct(latents.shape, BF16),
        ),
        in_specs=[vmem] * 4,
        out_specs=(hbm, hbm),
        scratch_shapes=[pltpu.VMEM(tokens.shape, BF16), dma((groups + 1,))],
        compiler_params=pltpu.CompilerParams(vmem_limit_bytes=BACK_BYTES),
    )(query, final, mid, key_vals)


def solution(mesh):
    rows = P(("dp", "lat"), None)
    whole = P()
    placed = (
        rows, rows, whole, whole, whole, whole, whole, whole, whole, whole,
        P(None, None, "lat"), P("lat", None), whole, whole, whole, whole,
    )
    return jax.shard_map(
        local, mesh=mesh, in_specs=placed, out_specs=(rows, rows), check_vma=False
    )
```

```python
import functools

import jax
import jax.numpy as jnp
from jax import lax
from jax.experimental import pallas as pl
from jax.experimental.pallas import tpu as pltpu
from jax.sharding import PartitionSpec as P

HEAD = 64
G = 256
NLAT = 16
WO_EIGHTHS = (1, 1, 1, 5)
FRONT_BYTES = 40 * 2**20
BACK_BYTES = 8 * 2**20
SCALE = HEAD ** (-0.5)
LOG2E = 1.4426950408889634
MESH = pl.DeviceIdType.MESH
F32 = jnp.float32
BF16 = jnp.bfloat16


def rms_norm(values, gain):
    floats = values.astype(F32)
    factor = lax.rsqrt(jnp.mean(floats * floats, axis=-1, keepdims=True) + 1e-06)
    return (floats * factor * gain).astype(BF16)


def dot(a, b):
    return jnp.dot(a, b, preferred_element_type=F32)


def dot_nt(a, b):
    return lax.dot_general(a, b, (((1,), (1,)), ((), ())), preferred_element_type=F32)


def dot_tn(a, b):
    return lax.dot_general(a, b, (((0,), (0,)), ((), ())), preferred_element_type=F32)


def spread_heads(query, count):
    lane_head = lax.broadcasted_iota(jnp.int32, query.shape, 1) // HEAD
    zero = jnp.zeros_like(query)
    return jnp.concatenate([jnp.where(lane_head == h, query, zero) for h in range(count)], axis=0)


def fold_heads(stacked, count):
    rows = stacked.shape[0] // count
    lane_head = lax.broadcasted_iota(jnp.int32, (rows, stacked.shape[1]), 1) // HEAD
    out = stacked[:rows]
    for h in range(1, count):
        out = jnp.where(lane_head == h, stacked[h * rows : (h + 1) * rows], out)
    return out


def softmax_mix(stacked, keys, values):
    return mix_values(dot_nt(stacked, keys), values)


def mix_values(scores, values):
    peak = jnp.max(scores, axis=-1, keepdims=True)
    weights = jnp.exp2(scores - peak)
    total = jnp.sum(weights, axis=-1, keepdims=True)
    return dot(weights.astype(BF16), values) * (1.0 / total)


def kernel(
    dp_count, lat_count,
    tok_h, lat_h, g_self_h, w_qkv_h, w_o_h, g_read_h, w_kvr_h, g_lat_h, w_qr_h, g_glob_h,
    w_glob_h, w_og_h, g_write_h, w_qw_h, g_wlat_h, w_kvw_h,
    tok_out, lat_out, mid, lfin,
    tok, lat_in, g_self, g_narrow, g_wide,
    w_qkv, w_o, w_kvr, w_qr, w_glob, w_og, w_qw, w_kvw,
    lmid, packed, mixed, read_q, normed_lat, outgoing, arrived, results, returned,
    early_q, early_top, early_norm, early_acc,
    load_sem, l_send, l_recv, s_send, s_recv, t_send, t_recv, wo_send, wo_recv,
):
    width = tok_h.shape[1]
    lat_width = lat_h.shape[1]
    groups = tok_h.shape[0] // G
    lat_rows = lat_h.shape[0]
    last = groups - 1
    here = w_glob_h.shape[2] // HEAD
    slots = dp_count // here
    line = lat_count * NLAT
    lanes = 2 * HEAD
    dp = lax.axis_index("dp")
    lat = lax.axis_index("lat")
    head, slot = dp // slots, dp % slots
    core = lat % 2
    lat_y = (lat + 2) % 4
    partner = lat + 1 - 2 * core
    diag = (partner + 2) % 4
    offsets = sorted(range(1, here), key=lambda o: -min(o, here - o)) + [0]
    order = [(head + o) % here for o in offsets[:-1]] + [head]
    g_read, g_write = g_narrow.at[0], g_narrow.at[1]
    g_lat, g_glob, g_wlat = g_wide.at[0], g_wide.at[1], g_wide.at[2]

    def scope(name):
        return jax.named_scope(name)

    def each(low, high, body):
        def one(i, carry):
            body(i)
            return carry

        lax.fori_loop(low, high, one, 0)

    loads = []

    def load(src, dst):
        loads.append(pltpu.make_async_copy(src, dst, load_sem.at[len(loads)]))
        loads[-1].start()
        return loads[-1]

    def load_all(sources, dst):
        sem = load_sem.at[len(loads)]
        for i, src in enumerate(sources):
            pltpu.make_async_copy(src, dst.at[i], sem).start()
        loads.append(pltpu.make_async_copy(dst, dst, sem))
        return loads[-1]

    def group_load(g):
        rows = pl.ds(g * G, G)
        return load(tok_h.at[rows], tok.at[rows])

    tok_load = [group_load(0)]
    gain_load = [load(g_self_h, g_self)]
    qkv_load = []
    for columns in (pl.ds(0, width), pl.ds(width, 2 * width)):
        qkv_load.append(load(w_qkv_h.at[:, columns], w_qkv.at[:, columns]))

    barrier = pltpu.get_barrier_semaphore()

    def greet(peer):
        pl.semaphore_signal(barrier, inc=1, device_id=peer, device_id_type=MESH)

    each(1, dp_count, lambda o: greet(((dp + o) % dp_count, lat)))
    for o in range(1, lat_count):
        each(0, here, lambda h: greet((h * slots + slot, (lat + o) % lat_count)))

    o_load = load(w_o_h, w_o)
    gain_load.append(load(lat_h, lat_in))
    gain_load.append(load_all((g_lat_h, g_glob_h, g_wlat_h), g_wide))
    gain_load.append(load_all((g_read_h, g_write_h), g_narrow))
    qr_load = load(w_qr_h, w_qr)
    kvr_load = load(w_kvr_h, w_kvr)
    for g in range(1, groups):
        tok_load.append(group_load(g))
    later = []

    def remote(src, dst, send_sem, recv_sem, peer):
        return pltpu.make_async_remote_copy(
            src_ref=src, dst_ref=dst, send_sem=send_sem, recv_sem=recv_sem, device_id=peer,
            device_id_type=MESH,
        )

    def landed(ref, sem):
        pltpu.make_async_copy(ref, ref, sem).wait()

    wo_share = remote(w_og_h, w_og.at[lat], wo_send, wo_recv.at[0], (dp, partner))
    wo_cross, wo_relay = [], []
    wo_rows = w_og_h.shape[0] // 8
    for i, count in enumerate(WO_EIGHTHS):
        part_rows = pl.ds(sum(WO_EIGHTHS[:i]) * wo_rows, count * wo_rows)
        there = w_og.at[lat_y, part_rows]
        wo_cross.append(
            remote(w_og_h.at[part_rows], w_og.at[lat, part_rows], wo_send, wo_recv.at[2 + i], (dp, lat_y))
        )
        wo_relay.append(remote(there, there, wo_send, wo_recv.at[1], (dp, partner)))

    def relay(i):
        wo_cross[i].wait_recv()
        wo_relay[i].start()


    def lat_copy(g, i):
        own = normed_lat.at[g, lat]
        peer = (diag, lat_y, partner)[i]
        return remote(own, own, l_send, l_recv.at[g], (dp, peer))

    def to_head(g, h, j):
        src, dst = outgoing.at[g, h], arrived.at[g, dp]
        if j is None:
            peer = (h * slots + slot, lat)
            return remote(src, dst, s_send.at[0], s_recv.at[g, 0], peer)
        rows = pl.ds(0, line)
        peer = (h * slots + (slot + j) % slots, lat)
        return remote(src.at[rows], dst.at[rows], s_send.at[1], s_recv.at[g, 1], peer)

    full, most = pl.ds(0, here - 1), pl.ds(0, here * (slots - 1))

    def spread(g):
        for h in order[:-1]:
            each(1, slots, lambda j: to_head(g, h, j).start())
        each(1, slots, lambda j: to_head(g, head, j).start())
        for h in order[:-1]:
            to_head(g, h, None).start()
        arrived[g, dp] = outgoing[g, head]

    def gathered(g):
        landed(arrived.at[g, full], s_recv.at[g, 0])
        if slots > 1:
            landed(arrived.at[g, most, pl.ds(0, line)], s_recv.at[g, 1])

    def low_lanes(rows):
        return lax.broadcasted_iota(jnp.int32, (rows, lanes), 1) < HEAD

    def swap(values):
        return pltpu.roll(values, HEAD, 1)

    def project(g):
        landed(normed_lat.at[g, pl.ds(0, lat_count - 1)], l_recv.at[g])
        rows = normed_lat[g].reshape(line, lat_width)
        queries = dot(rows, w_glob[0]) * (SCALE * LOG2E)
        keys = dot(rows, w_glob[1])
        values = dot(rows, w_glob[2])
        low, half = low_lanes(line), line // 2
        for h in range(0, here, 2):
            at = slice(h * HEAD, h * HEAD + lanes)
            k, v, q = keys[:, at], values[:, at], queries[:, at]
            outgoing[g, h, :line] = jnp.where(low, k, swap(v)).astype(BF16)
            outgoing[g, h + 1, :line] = jnp.where(low, swap(k), v).astype(BF16)
            q_swap = swap(q)
            outgoing[g, h, line:] = jnp.where(low[:half], q[:half], q_swap[half:]).astype(BF16)
            outgoing[g, h + 1, line:] = jnp.where(low[:half], q_swap[:half], q[half:]).astype(BF16)
        spread(g)

    def self_part(g, between):
        rows = pl.ds(g * G, G)
        tok_load[g].wait()
        if g == 0:
            gain_load[0].wait()
        group = tok[rows, :]
        normed = rms_norm(group, g_self[...])
        if g == 0:
            qkv_load[0].wait()
        packed[:, :width] = (dot(normed, w_qkv[:, :width]) * (SCALE * LOG2E)).astype(BF16)
        if g == 0:
            qkv_load[1].wait()
            for src, dst in (
                (w_glob_h, w_glob), (w_qw_h, w_qw), (w_kvw_h, w_kvw), (w_og_h, w_og.at[lat]),
            ):
                later.append(load(src, dst))
        packed[:, width:] = dot(normed, w_qkv[:, width:]).astype(BF16)
        between(g)
        for pair in range(width // lanes):
            at = pair * lanes
            query = packed[:, at : at + lanes]
            keys = packed[:, width + at : width + at + lanes]
            values = packed[:, 2 * width + at : 2 * width + at + lanes]
            out = softmax_mix(spread_heads(query, 2), keys, values)
            mixed[:, at : at + lanes] = fold_heads(out, 2).astype(BF16)
        if g == 0:
            o_load.wait()
        mid[rows, :] = (group.astype(F32) + dot(mixed[...], w_o[...])).astype(BF16)

    quad = 4 * HEAD

    def read_queries():
        for copy in gain_load[1:]:
            copy.wait()
        qr_load.wait()
        query = dot(rms_norm(lat_in[...], g_lat[...]), w_qr[...])
        query = (query * (SCALE * LOG2E)).astype(BF16)
        kvr_load.wait()
        for at in range(0, lat_width, quad):
            keyed = dot_nt(spread_heads(query[:, at : at + quad], 4), w_kvr[:, at : at + quad]).astype(BF16)
            for h in range(4):
                for g in range(groups):
                    start = h * lat_rows + g * NLAT
                    at_head = at // HEAD + h
                    read_q[g, at_head * NLAT : (at_head + 1) * NLAT, :] = keyed[start : start + NLAT, :]

    def read_part(g):
        if g == 0:
            read_queries()
        rows = pl.ds(g * G, G)
        lrows = pl.ds(g * NLAT, NLAT)
        normed = rms_norm(mid[rows, :], g_read[...])
        scores = dot_nt(read_q[g], normed)
        peak = jnp.max(scores, axis=-1, keepdims=True)
        weights = jnp.exp2(scores - peak)
        inverse = 1.0 / jnp.sum(weights, axis=-1, keepdims=True)
        seen = (dot(weights.astype(BF16), normed) * inverse).astype(BF16)
        for at in range(0, lat_width, quad):
            start = at // HEAD * NLAT
            out = dot(seen[start : start + 4 * NLAT], w_kvr[:, lat_width + at : lat_width + at + quad])
            lmid[lrows, at : at + quad] = (
                lat_in[lrows, at : at + quad].astype(F32) + fold_heads(out, 4)
            ).astype(BF16)
        normed_lat[g, lat] = rms_norm(lmid[lrows, :], g_glob[...])
        for i in range(3):
            lat_copy(g, i).start()

    def between(g):
        if g == 2:
            later[0].wait()
        if g >= 2:
            with scope(f"proj{g - 2}"):
                project(g - 2)

    for g in range(groups):
        with scope(f"self{g}"):
            self_part(g, between)
        if g == 0:
            with scope("bar"):
                pl.semaphore_wait(barrier, dp_count - 1 + here * (lat_count - 1))
            wo_share.start()
            wo_cross[0].start()
        with scope(f"read{g}"):
            read_part(g)
        if g < last:
            wo_cross[1 + g].start()
    with scope("projM"):
        project(last - 1)
    later[1].wait()
    with scope("wq"):
        for g in range(groups):
            rows = pl.ds(g * G, G)
            query = dot(rms_norm(mid[rows, :], g_write[...]), w_qw[...]).astype(BF16)
            tok_out[rows, :] = query * jnp.asarray(SCALE, BF16)
    with scope("rel"):
        relay(0)
        relay(1)
        wo_cross[groups].start()
    with scope("projL"):
        project(last)
    later[2].wait()
    later[3].wait()
    def query_of(c, g):
        pack = arrived[g, c * slots + slot, line:].astype(F32)
        low = low_lanes(line // 2)
        both = (jnp.where(low, pack, 0.0), jnp.where(low, swap(pack), 0.0))
        return jnp.concatenate(both, axis=0).astype(BF16)

    def key_vals(low, high):
        return jnp.concatenate(
            [arrived[g, d, :line] for g in range(low, high) for d in range(dp_count)], axis=0
        )

    wide = dp_count * line * groups <= 2048
    batches = [order[i : i + here // 2] for i in range(0, here, here // 2)]
    early_rows = last * line

    def attend_early(b):
        query = jnp.concatenate([query_of(c, g) for c in batches[b] for g in range(last)], axis=0)
        keys = key_vals(0, last)
        scores = dot_nt(query, keys)
        peak = jnp.max(scores, axis=-1, keepdims=True)
        weights = jnp.exp2(scores - peak)
        early_q[b] = query
        early_top[b] = peak
        early_norm[b] = jnp.sum(weights, axis=-1, keepdims=True)
        early_acc[b] = dot(weights.astype(BF16), keys)

    def late_scores(b):
        first = dot_nt(early_q[b], key_vals(last, groups))
        query = jnp.concatenate([query_of(c, last) for c in batches[b]], axis=0)
        return first, dot_nt(query, key_vals(0, groups))

    def attend_late(b, scores):
        peak = jnp.maximum(early_top[b], jnp.max(scores[0], axis=-1, keepdims=True))
        weights = jnp.exp2(scores[0] - peak)
        keep = jnp.exp2(early_top[b] - peak)
        total = early_norm[b] * keep + jnp.sum(weights, axis=-1, keepdims=True)
        first = dot(weights.astype(BF16), key_vals(last, groups))
        first = (early_acc[b] * keep + first) * (1.0 / total)
        second = mix_values(scores[1], key_vals(0, groups))
        parts = []
        for i in range(len(batches[b])):
            parts.append([first[i * early_rows + g * line : i * early_rows + (g + 1) * line] for g in range(last)])
            parts[-1].append(second[i * line : (i + 1) * line])
        return parts

    def attend_long(c):
        query = jnp.concatenate([query_of(c, g) for g in range(groups)], axis=0)

        def fold(i, carry):
            peak, total, acc = carry
            for g in range(groups):
                keys = arrived[g, i, :line]
                scores = dot_nt(query, keys)
                new = jnp.maximum(peak, jnp.max(scores, axis=-1, keepdims=True))
                weights = jnp.exp2(scores - new)
                keep = jnp.exp2(peak - new)
                total = total * keep + jnp.sum(weights, axis=-1, keepdims=True)
                acc = acc * keep + dot(weights.astype(BF16), keys)
                peak = new
            return peak, total, acc

        rows = query.shape[0]
        start = (
            jnp.full((rows, 1), -jnp.inf, F32), jnp.zeros((rows, 1), F32), jnp.zeros((rows, lanes), F32)
        )
        _, total, acc = lax.fori_loop(0, dp_count, fold, start)
        out = acc * (1.0 / total)
        return [out[g * line : (g + 1) * line] for g in range(groups)]

    def result_copy(c, i):
        to = (lat + i) % lat_count
        return remote(
            results.at[c, to], returned.at[head, lat], t_send, t_recv.at[head], (c * slots + slot, to)
        )

    def answer(c, parts, own):
        low = low_lanes(line)
        for k in range(0, groups, 2):
            even = parts[k]
            odd = parts[k + 1] if k + 1 < groups else even
            pair = jnp.where(low, swap(even), odd).astype(BF16)
            for l in range(lat_count):
                results[c, l, k // 2 * NLAT : (k // 2 + 1) * NLAT] = pair[l * NLAT : (l + 1) * NLAT]
        for l in range(1, lat_count):
            result_copy(c, l).start()
        if own:
            returned[head, lat] = results[c, lat]
        else:
            result_copy(c, 0).start()

    for g in range(last):
        with scope(f"gath{g}"):
            gathered(g)
    if wide:
        with scope("attE"):
            for b in range(len(batches)):
                attend_early(b)
    with scope("rel1"):
        relay(2)
    with scope("gathL"):
        gathered(last)
    with scope("rel2"):
        relay(3)
    with scope("att"):
        if wide:
            late = [late_scores(b) for b in range(len(batches))]
            for b, batch in enumerate(batches):
                for c, parts in zip(batch, attend_late(b, late[b])):
                    answer(c, parts, c is head)
        else:
            for c in order:
                answer(c, attend_long(c), c is head)
    with scope("wo1"):
        wo_share.wait_recv()
        landed(w_og.at[0], wo_recv.at[1])
    total = lmid[...].astype(F32)
    low = low_lanes(NLAT)
    for h in order:
        with scope("retw"):
            landed(returned.at[h, pl.ds(0, lat_count - 1 if h is head else lat_count)], t_recv.at[h])
        tiles = []
        for p in range(0, lat_count, 2):
            a, b = returned[h, p].astype(F32), returned[h, p + 1].astype(F32)
            a_swap, b_swap = swap(a), swap(b)
            column = []
            for g in range(groups):
                at = slice(g // 2 * NLAT, (g // 2 + 1) * NLAT)
                column.append(
                    jnp.where(low, a[at], b_swap[at]) if g % 2 == 0 else jnp.where(low, a_swap[at], b[at])
                )
            tiles.append(jnp.concatenate(column, axis=0))
        rows = pl.ds(pl.multiple_of(h * HEAD, HEAD), HEAD)
        weights = jnp.concatenate([w_og[l, rows, :] for l in range(lat_count)], axis=0)
        total = total + dot(jnp.concatenate(tiles, axis=1).astype(BF16), weights)
    with scope("final"):
        final = total.astype(BF16)
        lat_out[...] = final
        lfin[...] = dot(rms_norm(final, g_wlat[...]), w_kvw[...]).astype(BF16)

    with scope("drain"):
        landed(w_og.at[pl.ds(0, 3)], wo_send)
        landed(normed_lat.at[:, pl.ds(0, 3)], l_send)
        landed(outgoing.at[:, full], s_send.at[0])
        if slots > 1:
            landed(arrived.at[:, most, pl.ds(0, line)], s_send.at[1])
        landed(returned.at[pl.ds(0, here - 1)], t_send)
        landed(returned.at[0, pl.ds(0, lat_count - 1)], t_send)


def back(query, final, mid, key_vals, tok_h, lat_h, tok_out, sem):
    width = query.shape[1]
    heads = width // HEAD
    groups = query.shape[0] // G
    copies = [pltpu.make_async_copy(final, lat_h, sem.at[groups])]
    copies[0].start()
    for g in range(groups):
        rows, lrows = pl.ds(g * G, G), pl.ds(g * NLAT, NLAT)
        keys = spread_heads(key_vals[lrows, :width], heads)
        values = spread_heads(key_vals[lrows, width:], heads)
        scores = dot_nt(keys, query[rows, :]).reshape(heads, NLAT, G)
        peak = jnp.max(scores, axis=1, keepdims=True)
        weights = jnp.exp(scores - peak)
        weights = weights * (1.0 / jnp.sum(weights, axis=1, keepdims=True))
        written = dot_tn(weights.reshape(heads * NLAT, G).astype(BF16), values)
        tok_out[rows, :] = (mid[rows, :].astype(F32) + written).astype(BF16)
        copies.append(pltpu.make_async_copy(tok_out.at[rows], tok_h.at[rows], sem.at[g]))
        copies[-1].start()
    for copy in copies:
        copy.wait()


def local(
    tokens, latents, gain_self, w_qkv_tok, w_o_tok, gain_read, w_kv_read, gain_lat, w_q_read,
    gain_glob, w_qkv_glob, w_o_glob, gain_write, w_q_write, gain_wlat, w_kv_write,
):
    dp_count = lax.axis_size("dp")
    lat_count = lax.axis_size("lat")
    rows, width = tokens.shape
    lat_rows, lat_width = latents.shape
    groups = rows // G
    here = w_qkv_glob.shape[2] // HEAD
    line = lat_count * NLAT
    packs = (groups + 1) // 2
    vmem = pl.BlockSpec(memory_space=pltpu.VMEM)
    hbm = pl.BlockSpec(memory_space=pltpu.HBM)
    dma = pltpu.SemaphoreType.DMA
    query, final, mid, key_vals = pl.pallas_call(
        functools.partial(kernel, dp_count, lat_count),
        out_shape=(
            jax.ShapeDtypeStruct(tokens.shape, BF16),
            jax.ShapeDtypeStruct(latents.shape, BF16),
            jax.ShapeDtypeStruct(tokens.shape, BF16),
            jax.ShapeDtypeStruct((lat_rows, w_kv_write.shape[1]), BF16),
        ),
        in_specs=[hbm] * 16,
        out_specs=(vmem,) * 4,
        scratch_shapes=[
            pltpu.VMEM(tokens.shape, BF16),
            pltpu.VMEM(latents.shape, BF16),
            pltpu.VMEM((1, width), F32),
            pltpu.VMEM((2, 1, width), F32),
            pltpu.VMEM((3, 1, lat_width), F32),
            pltpu.VMEM(w_qkv_tok.shape, BF16),
            pltpu.VMEM(w_o_tok.shape, BF16),
            pltpu.VMEM(w_kv_read.shape, BF16),
            pltpu.VMEM(w_q_read.shape, BF16),
            pltpu.VMEM(w_qkv_glob.shape, BF16),
            pltpu.VMEM((lat_count,) + w_o_glob.shape, BF16),
            pltpu.VMEM(w_q_write.shape, BF16),
            pltpu.VMEM(w_kv_write.shape, BF16),
            pltpu.VMEM(latents.shape, BF16),
            pltpu.VMEM((G, w_qkv_tok.shape[1]), BF16),
            pltpu.VMEM((G, width), BF16),
            pltpu.VMEM((groups, lat_width // HEAD * NLAT, width), BF16),
            pltpu.VMEM((groups, lat_count, NLAT, lat_width), BF16),
            pltpu.VMEM((groups, here, line * 3 // 2, 2 * HEAD), BF16),
            pltpu.VMEM((groups, dp_count, line * 3 // 2, 2 * HEAD), BF16),
            pltpu.VMEM((here, lat_count, packs * NLAT, 2 * HEAD), BF16),
            pltpu.VMEM((here, lat_count, packs * NLAT, 2 * HEAD), BF16),
            pltpu.VMEM((2, here // 2 * (groups - 1) * line, 2 * HEAD), BF16),
            pltpu.VMEM((2, here // 2 * (groups - 1) * line, 1), F32),
            pltpu.VMEM((2, here // 2 * (groups - 1) * line, 1), F32),
            pltpu.VMEM((2, here // 2 * (groups - 1) * line, 2 * HEAD), F32),
            dma((13 + groups,)),
            dma,
            dma((groups,)),
            dma((2,)),
            dma((groups, 2)),
            dma,
            dma((here,)),
            dma,
            dma((2 + len(WO_EIGHTHS),)),
        ],
        compiler_params=pltpu.CompilerParams(
            collective_id=0, has_side_effects=True, vmem_limit_bytes=FRONT_BYTES
        ),
    )(
        *(
            pltpu.with_memory_space_constraint(array, pltpu.HBM)
            for array in (
                tokens, latents, gain_self[None], w_qkv_tok, w_o_tok, gain_read[None], w_kv_read,
                gain_lat[None], w_q_read, gain_glob[None], w_qkv_glob, w_o_glob, gain_write[None],
                w_q_write, gain_wlat[None], w_kv_write,
            )
        )
    )
    return pl.pallas_call(
        back,
        out_shape=(
            jax.ShapeDtypeStruct(tokens.shape, BF16),
            jax.ShapeDtypeStruct(latents.shape, BF16),
        ),
        in_specs=[vmem] * 4,
        out_specs=(hbm, hbm),
        scratch_shapes=[pltpu.VMEM(tokens.shape, BF16), dma((groups + 1,))],
        compiler_params=pltpu.CompilerParams(vmem_limit_bytes=BACK_BYTES),
    )(query, final, mid, key_vals)


def solution(mesh):
    rows = P(("dp", "lat"), None)
    whole = P()
    placed = (
        rows, rows, whole, whole, whole, whole, whole, whole, whole, whole,
        P(None, None, "lat"), P("lat", None), whole, whole, whole, whole,
    )
    return jax.shard_map(
        local, mesh=mesh, in_specs=placed, out_specs=(rows, rows), check_vma=False
    )
```

```python
import functools

import jax
import jax.numpy as jnp
from jax import lax
from jax.experimental import pallas as pl
from jax.experimental.pallas import tpu as pltpu
from jax.sharding import PartitionSpec as P

HEAD = 64
G = 256
NLAT = 16
WO_EIGHTHS = (1, 1, 1, 5)
FRONT_BYTES = 40 * 2**20
BACK_BYTES = 8 * 2**20
SCALE = HEAD ** (-0.5)
LOG2E = 1.4426950408889634
MESH = pl.DeviceIdType.MESH
F32 = jnp.float32
BF16 = jnp.bfloat16


def rms_norm(values, gain):
    floats = values.astype(F32)
    factor = lax.rsqrt(jnp.mean(floats * floats, axis=-1, keepdims=True) + 1e-06)
    return (floats * factor * gain).astype(BF16)


def dot(a, b):
    return jnp.dot(a, b, preferred_element_type=F32)


def dot_nt(a, b):
    return lax.dot_general(a, b, (((1,), (1,)), ((), ())), preferred_element_type=F32)


def dot_tn(a, b):
    return lax.dot_general(a, b, (((0,), (0,)), ((), ())), preferred_element_type=F32)


def spread_heads(query, count):
    lane_head = lax.broadcasted_iota(jnp.int32, query.shape, 1) // HEAD
    zero = jnp.zeros_like(query)
    return jnp.concatenate([jnp.where(lane_head == h, query, zero) for h in range(count)], axis=0)


def fold_heads(stacked, count):
    rows = stacked.shape[0] // count
    lane_head = lax.broadcasted_iota(jnp.int32, (rows, stacked.shape[1]), 1) // HEAD
    out = stacked[:rows]
    for h in range(1, count):
        out = jnp.where(lane_head == h, stacked[h * rows : (h + 1) * rows], out)
    return out


def softmax_mix(stacked, keys, values):
    return mix_values(dot_nt(stacked, keys), values)


def mix_values(scores, values):
    peak = jnp.max(scores, axis=-1, keepdims=True)
    weights = jnp.exp2(scores - peak)
    total = jnp.sum(weights, axis=-1, keepdims=True)
    return dot(weights.astype(BF16), values) * (1.0 / total)


def kernel(
    dp_count, lat_count,
    tok_h, lat_h, g_self_h, w_qkv_h, w_o_h, g_read_h, w_kvr_h, g_lat_h, w_qr_h, g_glob_h,
    w_glob_h, w_og_h, g_write_h, w_qw_h, g_wlat_h, w_kvw_h,
    tok_out, lat_out, mid, lfin,
    tok, lat_in, g_self, g_narrow, g_wide,
    w_qkv, w_o, w_kvr, w_qr, w_glob, w_og, w_qw, w_kvw,
    lmid, packed, mixed, read_q, normed_lat, outgoing, arrived, results, returned,
    early_q, early_top, early_norm, early_acc,
    load_sem, l_send, l_recv, s_send, s_recv, t_send, t_recv, wo_send, wo_recv,
):
    width = tok_h.shape[1]
    lat_width = lat_h.shape[1]
    groups = tok_h.shape[0] // G
    lat_rows = lat_h.shape[0]
    last = groups - 1
    here = w_glob_h.shape[2] // HEAD
    slots = dp_count // here
    line = lat_count * NLAT
    lanes = 2 * HEAD
    dp = lax.axis_index("dp")
    lat = lax.axis_index("lat")
    head, slot = dp // slots, dp % slots
    core = lat % 2
    lat_y = (lat + 2) % 4
    partner = lat + 1 - 2 * core
    diag = (partner + 2) % 4
    offsets = sorted(range(1, here), key=lambda o: -min(o, here - o)) + [0]
    order = [(head + o) % here for o in offsets[:-1]] + [head]
    g_read, g_write = g_narrow.at[0], g_narrow.at[1]
    g_lat, g_glob, g_wlat = g_wide.at[0], g_wide.at[1], g_wide.at[2]

    def scope(name):
        return jax.named_scope(name)

    def each(low, high, body):
        def one(i, carry):
            body(i)
            return carry

        lax.fori_loop(low, high, one, 0)

    loads = []

    def load(src, dst):
        loads.append(pltpu.make_async_copy(src, dst, load_sem.at[len(loads)]))
        loads[-1].start()
        return loads[-1]

    def load_all(sources, dst):
        sem = load_sem.at[len(loads)]
        for i, src in enumerate(sources):
            pltpu.make_async_copy(src, dst.at[i], sem).start()
        loads.append(pltpu.make_async_copy(dst, dst, sem))
        return loads[-1]

    def group_load(g):
        rows = pl.ds(g * G, G)
        return load(tok_h.at[rows], tok.at[rows])

    tok_load = [group_load(0)]
    gain_load = [load(g_self_h, g_self)]
    qkv_load = []
    for columns in (pl.ds(0, width), pl.ds(width, 2 * width)):
        qkv_load.append(load(w_qkv_h.at[:, columns], w_qkv.at[:, columns]))

    barrier = pltpu.get_barrier_semaphore()

    def greet(peer):
        pl.semaphore_signal(barrier, inc=1, device_id=peer, device_id_type=MESH)

    each(1, dp_count, lambda o: greet(((dp + o) % dp_count, lat)))
    for o in range(1, lat_count):
        each(0, here, lambda h: greet((h * slots + slot, (lat + o) % lat_count)))

    o_load = load(w_o_h, w_o)
    gain_load.append(load(lat_h, lat_in))
    gain_load.append(load_all((g_lat_h, g_glob_h, g_wlat_h), g_wide))
    gain_load.append(load_all((g_read_h, g_write_h), g_narrow))
    qr_load = load(w_qr_h, w_qr)
    kvr_load = load(w_kvr_h, w_kvr)
    for g in range(1, groups):
        tok_load.append(group_load(g))
    later = []

    def remote(src, dst, send_sem, recv_sem, peer):
        return pltpu.make_async_remote_copy(
            src_ref=src, dst_ref=dst, send_sem=send_sem, recv_sem=recv_sem, device_id=peer,
            device_id_type=MESH,
        )

    def landed(ref, sem):
        pltpu.make_async_copy(ref, ref, sem).wait()

    wo_share = remote(w_og_h, w_og.at[lat], wo_send, wo_recv.at[0], (dp, partner))
    wo_cross, wo_relay = [], []
    wo_rows = w_og_h.shape[0] // 8
    for i, count in enumerate(WO_EIGHTHS):
        part_rows = pl.ds(sum(WO_EIGHTHS[:i]) * wo_rows, count * wo_rows)
        there = w_og.at[lat_y, part_rows]
        wo_cross.append(
            remote(w_og_h.at[part_rows], w_og.at[lat, part_rows], wo_send, wo_recv.at[2 + i], (dp, lat_y))
        )
        wo_relay.append(remote(there, there, wo_send, wo_recv.at[1], (dp, partner)))

    def relay(i):
        wo_cross[i].wait_recv()
        wo_relay[i].start()


    def lat_copy(g, i):
        own = normed_lat.at[g, lat]
        peer = (diag, lat_y, partner)[i]
        return remote(own, own, l_send, l_recv.at[g], (dp, peer))

    def to_head(g, h, j):
        src, dst = outgoing.at[g, h], arrived.at[g, dp]
        if j is None:
            peer = (h * slots + slot, lat)
            return remote(src, dst, s_send.at[0], s_recv.at[g, 0], peer)
        rows = pl.ds(0, line)
        peer = (h * slots + (slot + j) % slots, lat)
        return remote(src.at[rows], dst.at[rows], s_send.at[1], s_recv.at[g, 1], peer)

    full, most = pl.ds(0, here - 1), pl.ds(0, here * (slots - 1))

    def spread(g):
        for h in order[:-1]:
            each(1, slots, lambda j: to_head(g, h, j).start())
        each(1, slots, lambda j: to_head(g, head, j).start())
        for h in order[:-1]:
            to_head(g, h, None).start()
        arrived[g, dp] = outgoing[g, head]

    def gathered(g):
        landed(arrived.at[g, full], s_recv.at[g, 0])
        if slots > 1:
            landed(arrived.at[g, most, pl.ds(0, line)], s_recv.at[g, 1])

    def low_lanes(rows):
        return lax.broadcasted_iota(jnp.int32, (rows, lanes), 1) < HEAD

    def swap(values):
        return pltpu.roll(values, HEAD, 1)

    def project(g):
        landed(normed_lat.at[g, pl.ds(0, lat_count - 1)], l_recv.at[g])
        rows = normed_lat[g].reshape(line, lat_width)
        queries = dot(rows, w_glob[0]) * (SCALE * LOG2E)
        keys = dot(rows, w_glob[1])
        values = dot(rows, w_glob[2])
        low, half = low_lanes(line), line // 2
        for h in range(0, here, 2):
            at = slice(h * HEAD, h * HEAD + lanes)
            k, v, q = keys[:, at], values[:, at], queries[:, at]
            outgoing[g, h, :line] = jnp.where(low, k, swap(v)).astype(BF16)
            outgoing[g, h + 1, :line] = jnp.where(low, swap(k), v).astype(BF16)
            q_swap = swap(q)
            outgoing[g, h, line:] = jnp.where(low[:half], q[:half], q_swap[half:]).astype(BF16)
            outgoing[g, h + 1, line:] = jnp.where(low[:half], q_swap[:half], q[half:]).astype(BF16)
        spread(g)

    def self_part(g, between):
        rows = pl.ds(g * G, G)
        tok_load[g].wait()
        if g == 0:
            gain_load[0].wait()
        group = tok[rows, :]
        normed = rms_norm(group, g_self[...])
        if g == 0:
            qkv_load[0].wait()
        packed[:, :width] = (dot(normed, w_qkv[:, :width]) * (SCALE * LOG2E)).astype(BF16)
        if g == 0:
            qkv_load[1].wait()
            for src, dst in (
                (w_glob_h, w_glob), (w_qw_h, w_qw), (w_kvw_h, w_kvw), (w_og_h, w_og.at[lat]),
            ):
                later.append(load(src, dst))
        packed[:, width:] = dot(normed, w_qkv[:, width:]).astype(BF16)
        between(g)
        for pair in range(width // lanes):
            at = pair * lanes
            query = packed[:, at : at + lanes]
            keys = packed[:, width + at : width + at + lanes]
            values = packed[:, 2 * width + at : 2 * width + at + lanes]
            out = softmax_mix(spread_heads(query, 2), keys, values)
            mixed[:, at : at + lanes] = fold_heads(out, 2).astype(BF16)
        if g == 0:
            o_load.wait()
        mid[rows, :] = (group.astype(F32) + dot(mixed[...], w_o[...])).astype(BF16)

    quad = 4 * HEAD

    def read_queries():
        for copy in gain_load[1:]:
            copy.wait()
        qr_load.wait()
        query = dot(rms_norm(lat_in[...], g_lat[...]), w_qr[...])
        query = (query * (SCALE * LOG2E)).astype(BF16)
        kvr_load.wait()
        for at in range(0, lat_width, quad):
            keyed = dot_nt(spread_heads(query[:, at : at + quad], 4), w_kvr[:, at : at + quad]).astype(BF16)
            for h in range(4):
                for g in range(groups):
                    start = h * lat_rows + g * NLAT
                    at_head = at // HEAD + h
                    read_q[g, at_head * NLAT : (at_head + 1) * NLAT, :] = keyed[start : start + NLAT, :]

    def read_part(g):
        if g == 0:
            read_queries()
        rows = pl.ds(g * G, G)
        lrows = pl.ds(g * NLAT, NLAT)
        normed = rms_norm(mid[rows, :], g_read[...])
        scores = dot_nt(read_q[g], normed)
        peak = jnp.max(scores, axis=-1, keepdims=True)
        weights = jnp.exp2(scores - peak)
        inverse = 1.0 / jnp.sum(weights, axis=-1, keepdims=True)
        seen = (dot(weights.astype(BF16), normed) * inverse).astype(BF16)
        for at in range(0, lat_width, quad):
            start = at // HEAD * NLAT
            out = dot(seen[start : start + 4 * NLAT], w_kvr[:, lat_width + at : lat_width + at + quad])
            lmid[lrows, at : at + quad] = (
                lat_in[lrows, at : at + quad].astype(F32) + fold_heads(out, 4)
            ).astype(BF16)
        normed_lat[g, lat] = rms_norm(lmid[lrows, :], g_glob[...])
        for i in range(3):
            lat_copy(g, i).start()

    def between(g):
        if g == 2:
            later[0].wait()
        if g >= 2:
            with scope(f"proj{g - 2}"):
                project(g - 2)

    for g in range(groups):
        with scope(f"self{g}"):
            self_part(g, between)
        if g == 0:
            with scope("bar"):
                pl.semaphore_wait(barrier, dp_count - 1 + here * (lat_count - 1))
            wo_share.start()
            wo_cross[0].start()
        with scope(f"read{g}"):
            read_part(g)
        if g < last:
            wo_cross[1 + g].start()
    with scope("projM"):
        project(last - 1)
    later[1].wait()
    with scope("wq"):
        for g in range(groups):
            rows = pl.ds(g * G, G)
            query = dot(rms_norm(mid[rows, :], g_write[...]), w_qw[...]).astype(BF16)
            tok_out[rows, :] = query * jnp.asarray(SCALE, BF16)
    with scope("rel"):
        relay(0)
        relay(1)
    with scope("projL"):
        project(last)
    wo_cross[groups].start()
    later[2].wait()
    later[3].wait()
    def query_of(c, g):
        pack = arrived[g, c * slots + slot, line:].astype(F32)
        low = low_lanes(line // 2)
        both = (jnp.where(low, pack, 0.0), jnp.where(low, swap(pack), 0.0))
        return jnp.concatenate(both, axis=0).astype(BF16)

    def key_vals(low, high):
        return jnp.concatenate(
            [arrived[g, d, :line] for g in range(low, high) for d in range(dp_count)], axis=0
        )

    wide = dp_count * line * groups <= 2048
    batches = [order[i : i + here // 2] for i in range(0, here, here // 2)]
    early_rows = last * line

    def attend_early(b):
        query = jnp.concatenate([query_of(c, g) for c in batches[b] for g in range(last)], axis=0)
        keys = key_vals(0, last)
        scores = dot_nt(query, keys)
        peak = jnp.max(scores, axis=-1, keepdims=True)
        weights = jnp.exp2(scores - peak)
        early_q[b] = query
        early_top[b] = peak
        early_norm[b] = jnp.sum(weights, axis=-1, keepdims=True)
        early_acc[b] = dot(weights.astype(BF16), keys)

    def late_scores(b):
        first = dot_nt(early_q[b], key_vals(last, groups))
        query = jnp.concatenate([query_of(c, last) for c in batches[b]], axis=0)
        return first, dot_nt(query, key_vals(0, groups))

    def attend_late(b, scores):
        peak = jnp.maximum(early_top[b], jnp.max(scores[0], axis=-1, keepdims=True))
        weights = jnp.exp2(scores[0] - peak)
        keep = jnp.exp2(early_top[b] - peak)
        total = early_norm[b] * keep + jnp.sum(weights, axis=-1, keepdims=True)
        first = dot(weights.astype(BF16), key_vals(last, groups))
        first = (early_acc[b] * keep + first) * (1.0 / total)
        second = mix_values(scores[1], key_vals(0, groups))
        parts = []
        for i in range(len(batches[b])):
            parts.append([first[i * early_rows + g * line : i * early_rows + (g + 1) * line] for g in range(last)])
            parts[-1].append(second[i * line : (i + 1) * line])
        return parts

    def attend_long(c):
        query = jnp.concatenate([query_of(c, g) for g in range(groups)], axis=0)

        def fold(i, carry):
            peak, total, acc = carry
            for g in range(groups):
                keys = arrived[g, i, :line]
                scores = dot_nt(query, keys)
                new = jnp.maximum(peak, jnp.max(scores, axis=-1, keepdims=True))
                weights = jnp.exp2(scores - new)
                keep = jnp.exp2(peak - new)
                total = total * keep + jnp.sum(weights, axis=-1, keepdims=True)
                acc = acc * keep + dot(weights.astype(BF16), keys)
                peak = new
            return peak, total, acc

        rows = query.shape[0]
        start = (
            jnp.full((rows, 1), -jnp.inf, F32), jnp.zeros((rows, 1), F32), jnp.zeros((rows, lanes), F32)
        )
        _, total, acc = lax.fori_loop(0, dp_count, fold, start)
        out = acc * (1.0 / total)
        return [out[g * line : (g + 1) * line] for g in range(groups)]

    def result_copy(c, i):
        to = (lat + i) % lat_count
        return remote(
            results.at[c, to], returned.at[head, lat], t_send, t_recv.at[head], (c * slots + slot, to)
        )

    def answer(c, parts, own):
        low = low_lanes(line)
        for k in range(0, groups, 2):
            even = swap(parts[k])
            if k + 1 < groups:
                pair = jnp.where(low, even, parts[k + 1]).astype(BF16)
                for l in range(lat_count):
                    results[c, l, k // 2 * NLAT : (k // 2 + 1) * NLAT] = pair[l * NLAT : (l + 1) * NLAT]
            else:
                for l in range(lat_count):
                    top = slice(l * NLAT, l * NLAT + NLAT // 2)
                    bottom = slice(l * NLAT + NLAT // 2, (l + 1) * NLAT)
                    halves = jnp.where(low[: NLAT // 2], even[top], parts[k][bottom])
                    results[c, l, k // 2 * NLAT :] = halves.astype(BF16)
        for l in range(1, lat_count):
            result_copy(c, l).start()
        if own:
            returned[head, lat] = results[c, lat]
        else:
            result_copy(c, 0).start()

    for g in range(last):
        with scope(f"gath{g}"):
            gathered(g)
    if wide:
        with scope("attE"):
            for b in range(len(batches)):
                attend_early(b)
    with scope("rel1"):
        relay(2)
    with scope("gathL"):
        gathered(last)
    with scope("att"):
        if wide:
            late = [late_scores(b) for b in range(len(batches))]
            for b, batch in enumerate(batches):
                for c, parts in zip(batch, attend_late(b, late[b])):
                    answer(c, parts, c is head)
        else:
            for c in order:
                answer(c, attend_long(c), c is head)
    with scope("wo1"):
        relay(3)
        wo_share.wait_recv()
        landed(w_og.at[0], wo_recv.at[1])
    total = lmid[...].astype(F32)
    low = low_lanes(NLAT)
    for k, h in enumerate(order):
        with scope(f"ret{k}"):
            landed(returned.at[h, pl.ds(0, lat_count - 1 if h is head else lat_count)], t_recv.at[h])
        tiles = []
        for p in range(0, lat_count, 2):
            a, b = returned[h, p].astype(F32), returned[h, p + 1].astype(F32)
            a_swap, b_swap = swap(a), swap(b)
            column = []
            for g in range(0, groups, 2):
                at = slice(g // 2 * NLAT, (g // 2 + 1) * NLAT)
                mask = low if g + 1 < groups else low[: NLAT // 2]
                column.append(jnp.where(mask, a[at], b_swap[at]))
                column.append(jnp.where(mask, a_swap[at], b[at]))
            tiles.append(jnp.concatenate(column, axis=0))
        rows = pl.ds(pl.multiple_of(h * HEAD, HEAD), HEAD)
        weights = jnp.concatenate([w_og[l, rows, :] for l in range(lat_count)], axis=0)
        total = total + dot(jnp.concatenate(tiles, axis=1).astype(BF16), weights)
    with scope("final"):
        final = total.astype(BF16)
        lat_out[...] = final
        lfin[...] = dot(rms_norm(final, g_wlat[...]), w_kvw[...]).astype(BF16)

    with scope("drain"):
        landed(w_og.at[pl.ds(0, 3)], wo_send)
        landed(normed_lat.at[:, pl.ds(0, 3)], l_send)
        landed(outgoing.at[:, full], s_send.at[0])
        if slots > 1:
            landed(arrived.at[:, most, pl.ds(0, line)], s_send.at[1])
        landed(returned.at[pl.ds(0, here - 1)], t_send)
        landed(returned.at[0, pl.ds(0, lat_count - 1)], t_send)


def back(query, final, mid, key_vals, tok_h, lat_h, tok_out, sem):
    width = query.shape[1]
    heads = width // HEAD
    groups = query.shape[0] // G
    copies = [pltpu.make_async_copy(final, lat_h, sem.at[groups])]
    copies[0].start()
    scores = []
    for g in range(groups):
        keys = spread_heads(key_vals[g * NLAT : (g + 1) * NLAT, :width], heads)
        scores.append(dot_nt(keys, query[g * G : (g + 1) * G, :]).reshape(heads, NLAT, G))
    for g in range(groups):
        rows = pl.ds(g * G, G)
        values = spread_heads(key_vals[g * NLAT : (g + 1) * NLAT, width:], heads)
        peak = jnp.max(scores[g], axis=1, keepdims=True)
        weights = jnp.exp(scores[g] - peak)
        weights = weights * (1.0 / jnp.sum(weights, axis=1, keepdims=True))
        written = dot_tn(weights.reshape(heads * NLAT, G).astype(BF16), values)
        tok_out[rows, :] = (mid[rows, :].astype(F32) + written).astype(BF16)
        copies.append(pltpu.make_async_copy(tok_out.at[rows], tok_h.at[rows], sem.at[g]))
        copies[-1].start()
    for copy in copies:
        copy.wait()


def local(
    tokens, latents, gain_self, w_qkv_tok, w_o_tok, gain_read, w_kv_read, gain_lat, w_q_read,
    gain_glob, w_qkv_glob, w_o_glob, gain_write, w_q_write, gain_wlat, w_kv_write,
):
    dp_count = lax.axis_size("dp")
    lat_count = lax.axis_size("lat")
    rows, width = tokens.shape
    lat_rows, lat_width = latents.shape
    groups = rows // G
    here = w_qkv_glob.shape[2] // HEAD
    line = lat_count * NLAT
    vmem = pl.BlockSpec(memory_space=pltpu.VMEM)
    hbm = pl.BlockSpec(memory_space=pltpu.HBM)
    dma = pltpu.SemaphoreType.DMA
    query, final, mid, key_vals = pl.pallas_call(
        functools.partial(kernel, dp_count, lat_count),
        out_shape=(
            jax.ShapeDtypeStruct(tokens.shape, BF16),
            jax.ShapeDtypeStruct(latents.shape, BF16),
            jax.ShapeDtypeStruct(tokens.shape, BF16),
            jax.ShapeDtypeStruct((lat_rows, w_kv_write.shape[1]), BF16),
        ),
        in_specs=[hbm] * 16,
        out_specs=(vmem,) * 4,
        scratch_shapes=[
            pltpu.VMEM(tokens.shape, BF16),
            pltpu.VMEM(latents.shape, BF16),
            pltpu.VMEM((1, width), F32),
            pltpu.VMEM((2, 1, width), F32),
            pltpu.VMEM((3, 1, lat_width), F32),
            pltpu.VMEM(w_qkv_tok.shape, BF16),
            pltpu.VMEM(w_o_tok.shape, BF16),
            pltpu.VMEM(w_kv_read.shape, BF16),
            pltpu.VMEM(w_q_read.shape, BF16),
            pltpu.VMEM(w_qkv_glob.shape, BF16),
            pltpu.VMEM((lat_count,) + w_o_glob.shape, BF16),
            pltpu.VMEM(w_q_write.shape, BF16),
            pltpu.VMEM(w_kv_write.shape, BF16),
            pltpu.VMEM(latents.shape, BF16),
            pltpu.VMEM((G, w_qkv_tok.shape[1]), BF16),
            pltpu.VMEM((G, width), BF16),
            pltpu.VMEM((groups, lat_width // HEAD * NLAT, width), BF16),
            pltpu.VMEM((groups, lat_count, NLAT, lat_width), BF16),
            pltpu.VMEM((groups, here, line * 3 // 2, 2 * HEAD), BF16),
            pltpu.VMEM((groups, dp_count, line * 3 // 2, 2 * HEAD), BF16),
            pltpu.VMEM((here, lat_count, groups * NLAT // 2, 2 * HEAD), BF16),
            pltpu.VMEM((here, lat_count, groups * NLAT // 2, 2 * HEAD), BF16),
            pltpu.VMEM((2, here // 2 * (groups - 1) * line, 2 * HEAD), BF16),
            pltpu.VMEM((2, here // 2 * (groups - 1) * line, 1), F32),
            pltpu.VMEM((2, here // 2 * (groups - 1) * line, 1), F32),
            pltpu.VMEM((2, here // 2 * (groups - 1) * line, 2 * HEAD), F32),
            dma((13 + groups,)),
            dma,
            dma((groups,)),
            dma((2,)),
            dma((groups, 2)),
            dma,
            dma((here,)),
            dma,
            dma((2 + len(WO_EIGHTHS),)),
        ],
        compiler_params=pltpu.CompilerParams(
            collective_id=0, has_side_effects=True, vmem_limit_bytes=FRONT_BYTES
        ),
    )(
        *(
            pltpu.with_memory_space_constraint(array, pltpu.HBM)
            for array in (
                tokens, latents, gain_self[None], w_qkv_tok, w_o_tok, gain_read[None], w_kv_read,
                gain_lat[None], w_q_read, gain_glob[None], w_qkv_glob, w_o_glob, gain_write[None],
                w_q_write, gain_wlat[None], w_kv_write,
            )
        )
    )
    return pl.pallas_call(
        back,
        out_shape=(
            jax.ShapeDtypeStruct(tokens.shape, BF16),
            jax.ShapeDtypeStruct(latents.shape, BF16),
        ),
        in_specs=[vmem] * 4,
        out_specs=(hbm, hbm),
        scratch_shapes=[pltpu.VMEM(tokens.shape, BF16), dma((groups + 1,))],
        compiler_params=pltpu.CompilerParams(vmem_limit_bytes=BACK_BYTES),
    )(query, final, mid, key_vals)


def solution(mesh):
    rows = P(("dp", "lat"), None)
    whole = P()
    placed = (
        rows, rows, whole, whole, whole, whole, whole, whole, whole, whole,
        P(None, None, "lat"), P("lat", None), whole, whole, whole, whole,
    )
    return jax.shard_map(
        local, mesh=mesh, in_specs=placed, out_specs=(rows, rows), check_vma=False
    )
```

```python
import functools

import jax
import jax.numpy as jnp
from jax import lax
from jax.experimental import pallas as pl
from jax.experimental.pallas import tpu as pltpu
from jax.sharding import PartitionSpec as P

HEAD = 64
G = 256
NLAT = 16
WO_EIGHTHS = (1, 1, 1, 2, 3)
FRONT_BYTES = 40 * 2**20
BACK_BYTES = 8 * 2**20
SCALE = HEAD ** (-0.5)
LOG2E = 1.4426950408889634
MESH = pl.DeviceIdType.MESH
F32 = jnp.float32
BF16 = jnp.bfloat16


def rms_norm(values, gain):
    floats = values.astype(F32)
    factor = lax.rsqrt(jnp.mean(floats * floats, axis=-1, keepdims=True) + 1e-06)
    return (floats * factor * gain).astype(BF16)


def dot(a, b):
    return jnp.dot(a, b, preferred_element_type=F32)


def dot_nt(a, b):
    return lax.dot_general(a, b, (((1,), (1,)), ((), ())), preferred_element_type=F32)


def dot_tn(a, b):
    return lax.dot_general(a, b, (((0,), (0,)), ((), ())), preferred_element_type=F32)


def spread_heads(query, count):
    lane_head = lax.broadcasted_iota(jnp.int32, query.shape, 1) // HEAD
    zero = jnp.zeros_like(query)
    return jnp.concatenate([jnp.where(lane_head == h, query, zero) for h in range(count)], axis=0)


def fold_heads(stacked, count):
    rows = stacked.shape[0] // count
    lane_head = lax.broadcasted_iota(jnp.int32, (rows, stacked.shape[1]), 1) // HEAD
    out = stacked[:rows]
    for h in range(1, count):
        out = jnp.where(lane_head == h, stacked[h * rows : (h + 1) * rows], out)
    return out


def softmax_mix(stacked, keys, values):
    return mix_values(dot_nt(stacked, keys), values)


def mix_values(scores, values):
    peak = jnp.max(scores, axis=-1, keepdims=True)
    weights = jnp.exp2(scores - peak)
    total = jnp.sum(weights, axis=-1, keepdims=True)
    return dot(weights.astype(BF16), values) * (1.0 / total)


def kernel(
    dp_count, lat_count,
    tok_h, lat_h, g_self_h, w_qkv_h, w_o_h, g_read_h, w_kvr_h, g_lat_h, w_qr_h, g_glob_h,
    w_glob_h, w_og_h, g_write_h, w_qw_h, g_wlat_h, w_kvw_h,
    tok_out, lat_out, mid, lfin,
    tok, lat_in, g_self, g_narrow, g_wide,
    w_qkv, w_o, w_kvr, w_qr, w_glob, w_og, w_qw, w_kvw,
    lmid, packed, mixed, read_q, normed_lat, outgoing, arrived, results, returned,
    early_q, early_top, early_norm, early_acc,
    load_sem, l_send, l_recv, s_send, s_recv, t_send, t_recv, wo_send, wo_recv,
):
    width = tok_h.shape[1]
    lat_width = lat_h.shape[1]
    groups = tok_h.shape[0] // G
    lat_rows = lat_h.shape[0]
    last = groups - 1
    here = w_glob_h.shape[2] // HEAD
    slots = dp_count // here
    line = lat_count * NLAT
    lanes = 2 * HEAD
    dp = lax.axis_index("dp")
    lat = lax.axis_index("lat")
    head, slot = dp // slots, dp % slots
    core = lat % 2
    lat_y = (lat + 2) % 4
    partner = lat + 1 - 2 * core
    diag = (partner + 2) % 4
    upper = head * 2 // here
    own_at = upper * head + (1 - upper) * (here - 1 - head)
    places = [i + (i + here - own_at) // here for i in range(here - 1)]
    order = [upper * i + (1 - upper) * (here - 1 - i) for i in places] + [head]
    g_read, g_write = g_narrow.at[0], g_narrow.at[1]
    g_lat, g_glob, g_wlat = g_wide.at[0], g_wide.at[1], g_wide.at[2]

    def scope(name):
        return jax.named_scope(name)

    def each(low, high, body):
        def one(i, carry):
            body(i)
            return carry

        lax.fori_loop(low, high, one, 0)

    loads = []

    def load(src, dst):
        loads.append(pltpu.make_async_copy(src, dst, load_sem.at[len(loads)]))
        loads[-1].start()
        return loads[-1]

    def load_all(sources, dst):
        sem = load_sem.at[len(loads)]
        for i, src in enumerate(sources):
            pltpu.make_async_copy(src, dst.at[i], sem).start()
        loads.append(pltpu.make_async_copy(dst, dst, sem))
        return loads[-1]

    def group_load(g):
        rows = pl.ds(g * G, G)
        return load(tok_h.at[rows], tok.at[rows])

    tok_load = [group_load(0)]
    gain_load = [load(g_self_h, g_self)]
    qkv_load = []
    for i in range(3):
        sem = load_sem.at[len(loads)]
        columns = pl.ds(i * width, width)
        for k in range(2):
            rows = pl.ds(k * width // 2, width // 2)
            pltpu.make_async_copy(w_qkv_h.at[rows, columns], w_qkv.at[rows, columns], sem).start()
        loads.append(pltpu.make_async_copy(w_qkv.at[:, columns], w_qkv.at[:, columns], sem))
        qkv_load.append(loads[-1])

    barrier = pltpu.get_barrier_semaphore()

    def greet(peer):
        pl.semaphore_signal(barrier, inc=1, device_id=peer, device_id_type=MESH)

    each(1, dp_count, lambda o: greet(((dp + o) % dp_count, lat)))
    for o in range(1, lat_count):
        each(0, here, lambda h: greet((h * slots + slot, (lat + o) % lat_count)))

    o_load = load(w_o_h, w_o)
    gain_load.append(load(lat_h, lat_in))
    gain_load.append(load_all((g_lat_h, g_glob_h, g_wlat_h), g_wide))
    gain_load.append(load_all((g_read_h, g_write_h), g_narrow))
    qr_load = load(w_qr_h, w_qr)
    kvr_load = load(w_kvr_h, w_kvr)
    for g in range(1, groups):
        tok_load.append(group_load(g))
    later = []

    def remote(src, dst, send_sem, recv_sem, peer):
        return pltpu.make_async_remote_copy(
            src_ref=src, dst_ref=dst, send_sem=send_sem, recv_sem=recv_sem, device_id=peer,
            device_id_type=MESH,
        )

    def landed(ref, sem):
        pltpu.make_async_copy(ref, ref, sem).wait()

    wo_share = remote(w_og_h, w_og.at[lat], wo_send, wo_recv.at[0], (dp, partner))
    wo_cross, wo_relay = [], []
    wo_rows = w_og_h.shape[0] // 8
    for i, count in enumerate(WO_EIGHTHS):
        part_rows = pl.ds(sum(WO_EIGHTHS[:i]) * wo_rows, count * wo_rows)
        there = w_og.at[lat_y, part_rows]
        wo_cross.append(
            remote(w_og_h.at[part_rows], w_og.at[lat, part_rows], wo_send, wo_recv.at[2 + i], (dp, lat_y))
        )
        wo_relay.append(remote(there, there, wo_send, wo_recv.at[1], (dp, partner)))

    def relay(i):
        wo_cross[i].wait_recv()
        wo_relay[i].start()


    def lat_copy(g, i):
        own = normed_lat.at[g, lat]
        peer = (diag, lat_y, partner)[i]
        return remote(own, own, l_send, l_recv.at[g], (dp, peer))

    def to_head(g, h, j):
        src, dst = outgoing.at[g, h], arrived.at[g, dp]
        if j is None:
            peer = (h * slots + slot, lat)
            return remote(src, dst, s_send.at[0], s_recv.at[g, 0], peer)
        rows = pl.ds(0, line)
        peer = (h * slots + (slot + j) % slots, lat)
        return remote(src.at[rows], dst.at[rows], s_send.at[1], s_recv.at[g, 1], peer)

    full, most = pl.ds(0, here - 1), pl.ds(0, here * (slots - 1))

    def spread(g):
        if not staged(g):
            for h in order[:-1]:
                each(1, slots, lambda j: to_head(g, h, j).start())
        each(1, slots, lambda j: to_head(g, head, j).start())
        for h in order[:-1]:
            to_head(g, h, None).start()
        arrived[g, dp] = outgoing[g, head]

    def staged(g):
        return slots > 1 and g < last - 1

    def pass_on(g):
        landed(arrived.at[g, full], s_recv.at[g, 0])
        for h in order[:-1]:
            block = arrived.at[g, h * slots + slot, pl.ds(0, line)]

            def one(j):
                peer = (head * slots + (slot + j) % slots, lat)
                remote(block, block, s_send.at[1], s_recv.at[g, 1], peer).start()

            each(1, slots, one)

    def gathered(g):
        if not staged(g):
            landed(arrived.at[g, full], s_recv.at[g, 0])
        if slots > 1:
            landed(arrived.at[g, most, pl.ds(0, line)], s_recv.at[g, 1])

    def low_lanes(rows):
        return lax.broadcasted_iota(jnp.int32, (rows, lanes), 1) < HEAD

    def swap(values):
        return pltpu.roll(values, HEAD, 1)

    def project(g):
        landed(normed_lat.at[g, pl.ds(0, lat_count - 1)], l_recv.at[g])
        rows = normed_lat[g].reshape(line, lat_width)
        queries = dot(rows, w_glob[0]) * (SCALE * LOG2E)
        keys = dot(rows, w_glob[1])
        values = dot(rows, w_glob[2])
        low, half = low_lanes(line), line // 2
        for h in range(0, here, 2):
            at = slice(h * HEAD, h * HEAD + lanes)
            k, v, q = keys[:, at], values[:, at], queries[:, at]
            outgoing[g, h, :line] = jnp.where(low, k, swap(v)).astype(BF16)
            outgoing[g, h + 1, :line] = jnp.where(low, swap(k), v).astype(BF16)
            q_swap = swap(q)
            outgoing[g, h, line:] = jnp.where(low[:half], q[:half], q_swap[half:]).astype(BF16)
            outgoing[g, h + 1, line:] = jnp.where(low[:half], q_swap[:half], q[half:]).astype(BF16)
        spread(g)

    def self_part(g, between):
        rows = pl.ds(g * G, G)
        tok_load[g].wait()
        if g == 0:
            gain_load[0].wait()
        group = tok[rows, :]
        normed = rms_norm(group, g_self[...])
        if g == 0:
            qkv_load[0].wait()
        packed[:, :width] = (dot(normed, w_qkv[:, :width]) * (SCALE * LOG2E)).astype(BF16)
        if g == 0:
            qkv_load[1].wait()
            qkv_load[2].wait()
            for src, dst in (
                (w_glob_h, w_glob), (w_qw_h, w_qw), (w_kvw_h, w_kvw), (w_og_h, w_og.at[lat]),
            ):
                later.append(load(src, dst))
        packed[:, width:] = dot(normed, w_qkv[:, width:]).astype(BF16)
        for pair in range(width // lanes):
            at = pair * lanes
            query = packed[:, at : at + lanes]
            keys = packed[:, width + at : width + at + lanes]
            values = packed[:, 2 * width + at : 2 * width + at + lanes]
            out = softmax_mix(spread_heads(query, 2), keys, values)
            mixed[:, at : at + lanes] = fold_heads(out, 2).astype(BF16)
            if pair == 1:
                between(g)
        if g == 0:
            o_load.wait()
        mid[rows, :] = (group.astype(F32) + dot(mixed[...], w_o[...])).astype(BF16)

    quad = 4 * HEAD

    def read_queries():
        for copy in gain_load[1:]:
            copy.wait()
        qr_load.wait()
        query = dot(rms_norm(lat_in[...], g_lat[...]), w_qr[...])
        query = (query * (SCALE * LOG2E)).astype(BF16)
        kvr_load.wait()
        for at in range(0, lat_width, quad):
            keyed = dot_nt(spread_heads(query[:, at : at + quad], 4), w_kvr[:, at : at + quad]).astype(BF16)
            for h in range(4):
                for g in range(groups):
                    start = h * lat_rows + g * NLAT
                    at_head = at // HEAD + h
                    read_q[g, at_head * NLAT : (at_head + 1) * NLAT, :] = keyed[start : start + NLAT, :]

    def read_part(g):
        if g == 0:
            read_queries()
        rows = pl.ds(g * G, G)
        lrows = pl.ds(g * NLAT, NLAT)
        normed = rms_norm(mid[rows, :], g_read[...])
        scores = dot_nt(read_q[g], normed)
        peak = jnp.max(scores, axis=-1, keepdims=True)
        weights = jnp.exp2(scores - peak)
        inverse = 1.0 / jnp.sum(weights, axis=-1, keepdims=True)
        seen = (dot(weights.astype(BF16), normed) * inverse).astype(BF16)
        for at in range(0, lat_width, quad):
            start = at // HEAD * NLAT
            out = dot(seen[start : start + 4 * NLAT], w_kvr[:, lat_width + at : lat_width + at + quad])
            lmid[lrows, at : at + quad] = (
                lat_in[lrows, at : at + quad].astype(F32) + fold_heads(out, 4)
            ).astype(BF16)
        normed_lat[g, lat] = rms_norm(lmid[lrows, :], g_glob[...])
        for i in range(3):
            lat_copy(g, i).start()

    def between(g):
        if g == 2:
            later[0].wait()
        if g >= 2:
            with scope(f"proj{g - 2}"):
                project(g - 2)

    for g in range(groups):
        with scope(f"self{g}"):
            self_part(g, between)
        if g == 0:
            with scope("bar"):
                pl.semaphore_wait(barrier, dp_count - 1 + here * (lat_count - 1))
            wo_share.start()
            wo_cross[0].start()
        with scope(f"read{g}"):
            read_part(g)
        if g < last:
            wo_cross[1 + g].start()
    with scope("projM"):
        project(last - 1)
    later[1].wait()
    with scope("wq"):
        for g in range(groups):
            rows = pl.ds(g * G, G)
            query = dot(rms_norm(mid[rows, :], g_write[...]), w_qw[...]).astype(BF16)
            tok_out[rows, :] = query * jnp.asarray(SCALE, BF16)
    with scope("rel"):
        for g in range(groups):
            if staged(g):
                pass_on(g)
        relay(0)
        relay(1)
        wo_cross[groups].start()
    with scope("projL"):
        project(last)
    wo_cross[groups + 1].start()
    later[2].wait()
    later[3].wait()
    def query_of(c, g):
        pack = arrived[g, c * slots + slot, line:].astype(F32)
        low = low_lanes(line // 2)
        both = (jnp.where(low, pack, 0.0), jnp.where(low, swap(pack), 0.0))
        return jnp.concatenate(both, axis=0).astype(BF16)

    def key_vals(low, high):
        return jnp.concatenate(
            [arrived[g, d, :line] for g in range(low, high) for d in range(dp_count)], axis=0
        )

    wide = dp_count * line * groups <= 2048
    batches = [order[i : i + here // 2] for i in range(0, here, here // 2)]
    early_rows = last * line

    def attend_early(b):
        query = jnp.concatenate([query_of(c, g) for c in batches[b] for g in range(last)], axis=0)
        keys = key_vals(0, last)
        scores = dot_nt(query, keys)
        peak = jnp.max(scores, axis=-1, keepdims=True)
        weights = jnp.exp2(scores - peak)
        early_q[b] = query
        early_top[b] = peak
        early_norm[b] = jnp.sum(weights, axis=-1, keepdims=True)
        early_acc[b] = dot(weights.astype(BF16), keys)

    def late_scores(b):
        first = dot_nt(early_q[b], key_vals(last, groups))
        query = jnp.concatenate([query_of(c, last) for c in batches[b]], axis=0)
        return first, dot_nt(query, key_vals(0, groups))

    def attend_late(b, scores):
        peak = jnp.maximum(early_top[b], jnp.max(scores[0], axis=-1, keepdims=True))
        weights = jnp.exp2(scores[0] - peak)
        keep = jnp.exp2(early_top[b] - peak)
        total = early_norm[b] * keep + jnp.sum(weights, axis=-1, keepdims=True)
        first = dot(weights.astype(BF16), key_vals(last, groups))
        first = (early_acc[b] * keep + first) * (1.0 / total)
        second = mix_values(scores[1], key_vals(0, groups))
        parts = []
        for i in range(len(batches[b])):
            parts.append([first[i * early_rows + g * line : i * early_rows + (g + 1) * line] for g in range(last)])
            parts[-1].append(second[i * line : (i + 1) * line])
        return parts

    def attend_long(c):
        query = jnp.concatenate([query_of(c, g) for g in range(groups)], axis=0)

        def fold(i, carry):
            peak, total, acc = carry
            for g in range(groups):
                keys = arrived[g, i, :line]
                scores = dot_nt(query, keys)
                new = jnp.maximum(peak, jnp.max(scores, axis=-1, keepdims=True))
                weights = jnp.exp2(scores - new)
                keep = jnp.exp2(peak - new)
                total = total * keep + jnp.sum(weights, axis=-1, keepdims=True)
                acc = acc * keep + dot(weights.astype(BF16), keys)
                peak = new
            return peak, total, acc

        rows = query.shape[0]
        start = (
            jnp.full((rows, 1), -jnp.inf, F32), jnp.zeros((rows, 1), F32), jnp.zeros((rows, lanes), F32)
        )
        _, total, acc = lax.fori_loop(0, dp_count, fold, start)
        out = acc * (1.0 / total)
        return [out[g * line : (g + 1) * line] for g in range(groups)]

    def result_copy(c, i):
        to = (lat + i) % lat_count
        return remote(
            results.at[c, to], returned.at[head, lat], t_send, t_recv.at[head], (c * slots + slot, to)
        )

    def answer(c, parts, own):
        low = low_lanes(line)
        for k in range(0, groups, 2):
            even = swap(parts[k])
            if k + 1 < groups:
                pair = jnp.where(low, even, parts[k + 1]).astype(BF16)
                for l in range(lat_count):
                    results[c, l, k // 2 * NLAT : (k // 2 + 1) * NLAT] = pair[l * NLAT : (l + 1) * NLAT]
            else:
                for l in range(lat_count):
                    top = slice(l * NLAT, l * NLAT + NLAT // 2)
                    bottom = slice(l * NLAT + NLAT // 2, (l + 1) * NLAT)
                    halves = jnp.where(low[: NLAT // 2], even[top], parts[k][bottom])
                    results[c, l, k // 2 * NLAT :] = halves.astype(BF16)
        for l in range(1, lat_count):
            result_copy(c, l).start()
        if own:
            returned[head, lat] = results[c, lat]
        else:
            result_copy(c, 0).start()

    for g in range(last):
        with scope(f"gath{g}"):
            gathered(g)
    if wide:
        with scope("attE"):
            for b in range(len(batches)):
                attend_early(b)
    with scope("rel1"):
        relay(2)
        relay(3)
    with scope("gathL"):
        gathered(last)
    with scope("att"):
        if wide:
            late = [late_scores(b) for b in range(len(batches))]
            for b, batch in enumerate(batches):
                for c, parts in zip(batch, attend_late(b, late[b])):
                    answer(c, parts, c is head)
        else:
            for c in order:
                answer(c, attend_long(c), c is head)
    with scope("wo1"):
        relay(4)
        wo_share.wait_recv()
        landed(w_og.at[0], wo_recv.at[1])
    total = lmid[...].astype(F32)
    low = low_lanes(NLAT)
    for k, h in enumerate(order[::-1]):
        with scope(f"ret{k}"):
            landed(returned.at[h, pl.ds(0, lat_count - 1 if h is head else lat_count)], t_recv.at[h])
        tiles = []
        for p in range(0, lat_count, 2):
            a, b = returned[h, p].astype(F32), returned[h, p + 1].astype(F32)
            a_swap, b_swap = swap(a), swap(b)
            column = []
            for g in range(0, groups, 2):
                at = slice(g // 2 * NLAT, (g // 2 + 1) * NLAT)
                mask = low if g + 1 < groups else low[: NLAT // 2]
                column.append(jnp.where(mask, a[at], b_swap[at]))
                column.append(jnp.where(mask, a_swap[at], b[at]))
            tiles.append(jnp.concatenate(column, axis=0))
        rows = pl.ds(pl.multiple_of(h * HEAD, HEAD), HEAD)
        weights = jnp.concatenate([w_og[l, rows, :] for l in range(lat_count)], axis=0)
        total = total + dot(jnp.concatenate(tiles, axis=1).astype(BF16), weights)
    with scope("final"):
        final = total.astype(BF16)
        lat_out[...] = final
        lfin[...] = dot(rms_norm(final, g_wlat[...]), w_kvw[...]).astype(BF16)

    with scope("drain"):
        landed(w_og.at[pl.ds(0, 3)], wo_send)
        landed(normed_lat.at[:, pl.ds(0, 3)], l_send)
        landed(outgoing.at[:, full], s_send.at[0])
        if slots > 1:
            landed(arrived.at[:, most, pl.ds(0, line)], s_send.at[1])
        landed(returned.at[pl.ds(0, here - 1)], t_send)
        landed(returned.at[0, pl.ds(0, lat_count - 1)], t_send)


def back(query, final, mid, key_vals, tok_h, lat_h, tok_out, sem):
    width = query.shape[1]
    heads = width // HEAD
    groups = query.shape[0] // G
    copies = [pltpu.make_async_copy(final, lat_h, sem.at[groups])]
    copies[0].start()
    scores = []
    for g in range(groups):
        keys = spread_heads(key_vals[g * NLAT : (g + 1) * NLAT, :width], heads)
        scores.append(dot_nt(keys, query[g * G : (g + 1) * G, :]).reshape(heads, NLAT, G))
    for g in range(groups):
        rows = pl.ds(g * G, G)
        values = spread_heads(key_vals[g * NLAT : (g + 1) * NLAT, width:], heads)
        peak = jnp.max(scores[g], axis=1, keepdims=True)
        weights = jnp.exp(scores[g] - peak)
        weights = weights * (1.0 / jnp.sum(weights, axis=1, keepdims=True))
        written = dot_tn(weights.reshape(heads * NLAT, G).astype(BF16), values)
        tok_out[rows, :] = (mid[rows, :].astype(F32) + written).astype(BF16)
        copies.append(pltpu.make_async_copy(tok_out.at[rows], tok_h.at[rows], sem.at[g]))
        copies[-1].start()
    for copy in copies:
        copy.wait()


def local(
    tokens, latents, gain_self, w_qkv_tok, w_o_tok, gain_read, w_kv_read, gain_lat, w_q_read,
    gain_glob, w_qkv_glob, w_o_glob, gain_write, w_q_write, gain_wlat, w_kv_write,
):
    dp_count = lax.axis_size("dp")
    lat_count = lax.axis_size("lat")
    rows, width = tokens.shape
    lat_rows, lat_width = latents.shape
    groups = rows // G
    here = w_qkv_glob.shape[2] // HEAD
    line = lat_count * NLAT
    vmem = pl.BlockSpec(memory_space=pltpu.VMEM)
    hbm = pl.BlockSpec(memory_space=pltpu.HBM)
    dma = pltpu.SemaphoreType.DMA
    query, final, mid, key_vals = pl.pallas_call(
        functools.partial(kernel, dp_count, lat_count),
        out_shape=(
            jax.ShapeDtypeStruct(tokens.shape, BF16),
            jax.ShapeDtypeStruct(latents.shape, BF16),
            jax.ShapeDtypeStruct(tokens.shape, BF16),
            jax.ShapeDtypeStruct((lat_rows, w_kv_write.shape[1]), BF16),
        ),
        in_specs=[hbm] * 16,
        out_specs=(vmem,) * 4,
        scratch_shapes=[
            pltpu.VMEM(tokens.shape, BF16),
            pltpu.VMEM(latents.shape, BF16),
            pltpu.VMEM((1, width), F32),
            pltpu.VMEM((2, 1, width), F32),
            pltpu.VMEM((3, 1, lat_width), F32),
            pltpu.VMEM(w_qkv_tok.shape, BF16),
            pltpu.VMEM(w_o_tok.shape, BF16),
            pltpu.VMEM(w_kv_read.shape, BF16),
            pltpu.VMEM(w_q_read.shape, BF16),
            pltpu.VMEM(w_qkv_glob.shape, BF16),
            pltpu.VMEM((lat_count,) + w_o_glob.shape, BF16),
            pltpu.VMEM(w_q_write.shape, BF16),
            pltpu.VMEM(w_kv_write.shape, BF16),
            pltpu.VMEM(latents.shape, BF16),
            pltpu.VMEM((G, w_qkv_tok.shape[1]), BF16),
            pltpu.VMEM((G, width), BF16),
            pltpu.VMEM((groups, lat_width // HEAD * NLAT, width), BF16),
            pltpu.VMEM((groups, lat_count, NLAT, lat_width), BF16),
            pltpu.VMEM((groups, here, line * 3 // 2, 2 * HEAD), BF16),
            pltpu.VMEM((groups, dp_count, line * 3 // 2, 2 * HEAD), BF16),
            pltpu.VMEM((here, lat_count, groups * NLAT // 2, 2 * HEAD), BF16),
            pltpu.VMEM((here, lat_count, groups * NLAT // 2, 2 * HEAD), BF16),
            pltpu.VMEM((2, here // 2 * (groups - 1) * line, 2 * HEAD), BF16),
            pltpu.VMEM((2, here // 2 * (groups - 1) * line, 1), F32),
            pltpu.VMEM((2, here // 2 * (groups - 1) * line, 1), F32),
            pltpu.VMEM((2, here // 2 * (groups - 1) * line, 2 * HEAD), F32),
            dma((14 + groups,)),
            dma,
            dma((groups,)),
            dma((2,)),
            dma((groups, 2)),
            dma,
            dma((here,)),
            dma,
            dma((2 + len(WO_EIGHTHS),)),
        ],
        compiler_params=pltpu.CompilerParams(
            collective_id=0, has_side_effects=True, vmem_limit_bytes=FRONT_BYTES
        ),
    )(
        *(
            pltpu.with_memory_space_constraint(array, pltpu.HBM)
            for array in (
                tokens, latents, gain_self[None], w_qkv_tok, w_o_tok, gain_read[None], w_kv_read,
                gain_lat[None], w_q_read, gain_glob[None], w_qkv_glob, w_o_glob, gain_write[None],
                w_q_write, gain_wlat[None], w_kv_write,
            )
        )
    )
    return pl.pallas_call(
        back,
        out_shape=(
            jax.ShapeDtypeStruct(tokens.shape, BF16),
            jax.ShapeDtypeStruct(latents.shape, BF16),
        ),
        in_specs=[vmem] * 4,
        out_specs=(hbm, hbm),
        scratch_shapes=[pltpu.VMEM(tokens.shape, BF16), dma((groups + 1,))],
        compiler_params=pltpu.CompilerParams(vmem_limit_bytes=BACK_BYTES),
    )(query, final, mid, key_vals)


def solution(mesh):
    rows = P(("dp", "lat"), None)
    whole = P()
    placed = (
        rows, rows, whole, whole, whole, whole, whole, whole, whole, whole,
        P(None, None, "lat"), P("lat", None), whole, whole, whole, whole,
    )
    return jax.shard_map(
        local, mesh=mesh, in_specs=placed, out_specs=(rows, rows), check_vma=False
    )
```
